32 devices in a mesh: dp: 16 (over z, y, x), seq: 2 (over core).
Axes of the slice: x: 2, y: 2, z: 4, core: 2. Of those that a mesh axis runs over, the one named last changes fastest.
Arguments:
- tokens: bfloat16 [32768, 512], P(('dp', 'seq')), may hold values from -6 to 6
- route: int32 [512], P(('dp', 'seq')), may hold values from 0 to 511, as said below
- lengths: int32 [16, 6], P('dp'), may hold values from 1 to 1024, 2048 in all within a row
- query_weight: bfloat16 [512, 512], replicated, may hold values from -0.25 to 0.25
- query_bias: bfloat16 [512], replicated, may hold values from -3 to 3
- key_weight: bfloat16 [512, 512], replicated, may hold values from -0.25 to 0.25
- value_weight: bfloat16 [512, 512], replicated, may hold values from -0.25 to 0.25
- value_bias: bfloat16 [512], replicated, may hold values from -3 to 3
- output_weight: bfloat16 [512, 512], replicated, may hold values from -2 to 2
- output_bias: bfloat16 [512], replicated, may hold values from -3 to 3
- first_gain: bfloat16 [512], replicated, may hold values from 0.5 to 1.5
- first_shift: bfloat16 [512], replicated, may hold values from -3 to 3
- up_weight: bfloat16 [512, 2048], replicated, may hold values from -0.25 to 0.25
- up_bias: bfloat16 [2048], replicated, may hold values from -3 to 3
- down_weight: bfloat16 [2048, 512], replicated, may hold values from -0.1875 to 0.1875
- down_bias: bfloat16 [512], replicated, may hold values from -3 to 3
- second_gain: bfloat16 [512], replicated, may hold values from 0.5 to 1.5
- second_shift: bfloat16 [512], replicated, may hold values from -3 to 3
- cotangent: bfloat16 [32768, 512], P(('dp', 'seq')), may hold values from -6 to 6
Outputs:
- layer_out: bfloat16 [32768, 512], P(('dp', 'seq'))
- token_grad: bfloat16 [32768, 512], P(('dp', 'seq'))
- query_weight_gradient: float32 [512, 512], replicated
- query_bias_gradient: float32 [512], replicated
- key_weight_gradient: float32 [512, 512], replicated
- value_weight_gradient: float32 [512, 512], replicated
- value_bias_gradient: float32 [512], replicated
- output_weight_gradient: float32 [512, 512], replicated
- output_bias_gradient: float32 [512], replicated
- first_gain_gradient: float32 [512], replicated
- first_shift_gradient: float32 [512], replicated
- up_weight_gradient: float32 [512, 2048], replicated
- up_bias_gradient: float32 [2048], replicated
- down_weight_gradient: float32 [2048, 512], replicated
- down_bias_gradient: float32 [512], replicated
- second_gain_gradient: float32 [512], replicated
- second_shift_gradient: float32 [512], replicated
The draws below stay inside these ranges and needn't reach their ends.
Inputs may be any that keep to these rules, and one draw needn't show every extreme that they name: route is a permutation of the piece numbers. The device with index b of dp+seq (b = dp index * 2 + seq index) holds entries b * 16 to (b + 1) * 16 - 1, and packed piece t lies on the device with that index t // 16. Each device's 16 entries name 16 different groups, one piece for each, always on the device of the same seq index, so each device receives exactly one piece from every group. Each group's 6 lengths add up to 2048; in every group the longest is exactly 1024.
All inputs are finite; a program needn't handle non-finite values.
Results may differ from the reference program's by a relative error of at most 0.014.
The reference program's roundings to bfloat16 on the way count: a program that leaves them out, or rounds other values in their place, can miss the bound.
Values may be sent and summed in bfloat16 or wider, within the bound.
A program may use at most 256 MiB of HBM per device.

```python
import math
import jax
import jax.numpy as jnp
import numpy as np
from jax import lax

D = 512
HEADS = 8
HEAD = 64
FF = 2048
MAXTAB = 6
GROUPS = 16
GROUP_TOK = 2048
LONGEST = 1024
TOKENS = 32768
N_DP = 16
N_SEQ = 2


def draw_route(key, part):
    groups = N_DP
    pairs = N_SEQ
    first_key, second_key = jax.random.split(key)
    dest_keys = jax.random.split(first_key, groups * pairs)
    slot_keys = jax.random.split(second_key, groups * pairs)
    destination = jax.vmap(lambda single: jax.random.permutation(single, groups))(dest_keys).astype(jnp.int32)
    slot_table = jax.vmap(lambda single: jax.random.permutation(single, groups))(slot_keys).astype(jnp.int32)
    sources = jnp.arange(groups * pairs, dtype=jnp.int32)
    source_group = (sources // pairs)[:, None]
    source_seq = (sources % pairs)[:, None]
    target = destination * pairs + source_seq
    slot = slot_table[target, jnp.broadcast_to(source_group, target.shape)]
    return (target * groups + slot).reshape(-1).astype(jnp.int32)


def levels(own_key, dims, pieces, least, top_value):
    level, own = 1.0, jax.random.fold_in(own_key, 6)
    for axis_at, blocks in pieces:
        steps = jnp.exp(jax.random.uniform(jax.random.fold_in(own, axis_at), (blocks,), jnp.float32, least / len(pieces), top_value / len(pieces)))
        level = level * jnp.repeat(steps, dims[axis_at] // blocks).reshape([-1 if axis == axis_at else 1 for axis in range(len(dims))])
    return level


def length_profile(amount, total, bound, lean):
    portions = [(1 << 20) // math.isqrt(grade ** lean) + 1 for grade in range(2, amount + 1)]
    rest, holding = total - bound - (amount - 1), [1] * (amount - 1)
    while rest > 0:
        candidates = [i for i in range(amount - 1) if holding[i] < bound]
        whole, budget = sum([portions[i] for i in candidates]), rest
        for i in candidates:
            more = min(bound - holding[i], max(1, budget * portions[i] // whole), rest)
            holding[i] = holding[i] + more
            rest = rest - more
    return np.array([bound] + holding)


def ragged(own_key, amount, total, bound, skew):
    if amount == 2:
        one = jax.random.randint(own_key, (), max(1, total - bound), min(bound, total - 1) + 1)
        return jnp.stack([one, total - one])
    sizes = jnp.asarray(length_profile(amount, total, bound, skew), jnp.int32)
    twos = (amount - 1) // 2
    giver, receiver = sizes[1:1 + 2 * twos:2], sizes[2:2 + 2 * twos:2]
    room = jnp.minimum(giver - 1, bound - receiver)
    passed = jax.random.randint(jax.random.fold_in(own_key, 1), (twos,), 0, 1 << 20) % (room + 1)
    sizes = sizes.at[1:1 + 2 * twos:2].set(giver - passed).at[2:2 + 2 * twos:2].set(receiver + passed)
    return sizes[jax.random.permutation(jax.random.fold_in(own_key, 2), amount)]


def gaussian(rng, extent, scale, reach, shards=(), kind=jnp.bfloat16):
    values = jax.random.normal(rng, extent, jnp.float32) * scale
    if len(shards) > 0:
        values = levels(rng, extent, shards, -0.22, 0.18) * values
    return jnp.clip(values, min=-reach, max=reach).astype(kind)


def setup_inputs(seed: int = 0) -> dict:
    key_list = jax.random.split(jax.random.key(seed), 20)
    tokens = gaussian(key_list[0], (TOKENS, D), 1.0, 6.0, ((0, 32),))
    route = draw_route(jax.random.fold_in(key_list[19], 71), 0)
    lengths = jax.vmap(lambda own: ragged(own, MAXTAB, GROUP_TOK, LONGEST, 2))(jax.random.split(key_list[2], GROUPS)).reshape((GROUPS, MAXTAB)).astype(jnp.int32)
    query_weight = gaussian(key_list[3], (D, D), D ** -0.5, 0.25)
    query_bias = gaussian(key_list[4], (D,), 0.5, 3.0)
    key_weight = gaussian(key_list[5], (D, D), D ** -0.5, 0.25)
    value_weight = gaussian(key_list[6], (D, D), D ** -0.5, 0.25)
    value_bias = gaussian(key_list[7], (D,), 0.5, 3.0)
    output_weight = gaussian(key_list[8], (D, D), (D // 64) ** -0.5, 2.0)
    output_bias = gaussian(key_list[9], (D,), 0.5, 3.0)
    first_gain = jnp.clip(1.0 + 0.1 * jax.random.normal(key_list[10], (D,), jnp.float32), 0.5, 1.5).astype(jnp.bfloat16)
    first_shift = gaussian(key_list[11], (D,), 0.5, 3.0)
    up_weight = gaussian(key_list[12], (D, FF), D ** -0.5, 0.25)
    up_bias = gaussian(key_list[13], (FF,), 0.5, 3.0)
    down_weight = gaussian(key_list[14], (FF, D), (FF // 2) ** -0.5, 0.1875)
    down_bias = gaussian(key_list[15], (D,), 0.5, 3.0)
    second_gain = jnp.clip(1.0 + 0.1 * jax.random.normal(key_list[16], (D,), jnp.float32), 0.5, 1.5).astype(jnp.bfloat16)
    second_shift = gaussian(key_list[17], (D,), 0.5, 3.0)
    cotangent = gaussian(key_list[18], (TOKENS, D), 1.0, 6.0, ((0, 32),))
    return {"tokens": tokens, "route": route, "lengths": lengths, "query_weight": query_weight, "query_bias": query_bias, "key_weight": key_weight, "value_weight": value_weight, "value_bias": value_bias, "output_weight": output_weight, "output_bias": output_bias, "first_gain": first_gain, "first_shift": first_shift, "up_weight": up_weight, "up_bias": up_bias, "down_weight": down_weight, "down_bias": down_bias, "second_gain": second_gain, "second_shift": second_shift, "cotangent": cotangent}


@jax.custom_vjp
def low(v):
    return lax.optimization_barrier(v.astype(jnp.bfloat16)).astype(jnp.float32)

@jax.custom_vjp
def low_back(v):
    return v

def low_keep(v):
    return (low(v), None)

def low_pass(kept, grad):
    return (grad,)

def back_keep(v):
    return (v, None)

def back_low(kept, grad):
    return (low(grad),)
low.defvjp(low_keep, low_pass)
low_back.defvjp(back_keep, back_low)
highest = lax.Precision.HIGHEST

def both_ways(value):
    return low_back(low(value))

def norm_rows(value, gain, shift):
    center = value - lax.optimization_barrier(jnp.mean(value, axis=-1, keepdims=True))
    spread = lax.optimization_barrier(jnp.mean(center * center, axis=-1, keepdims=True))
    return center * lax.rsqrt(spread + 1e-05) * gain + shift

def group_layer(inputs, segment, params):
    query_weight, query_bias, key_weight, value_weight, value_bias, output_weight, output_bias, first_gain, first_shift, up_weight, up_bias, down_weight, down_bias, second_gain, second_shift = params
    count = inputs.shape[0]
    queries = both_ways(jnp.dot(inputs, query_weight, precision=highest) + query_bias)
    keyset = both_ways(jnp.dot(inputs, key_weight, precision=highest))
    valueset = both_ways(jnp.dot(inputs, value_weight, precision=highest) + value_bias)
    query_heads = queries.reshape(count, HEADS, HEAD)
    key_heads = keyset.reshape(count, HEADS, HEAD)
    value_heads = valueset.reshape(count, HEADS, HEAD)
    scores = low_back(jnp.einsum('qhd,khd->hqk', query_heads, key_heads, precision=highest) * HEAD ** (-0.5))
    same = segment[:, None] == segment[None, :]
    scores = jnp.where(same[None], scores, -jnp.inf)
    top = lax.optimization_barrier(jnp.max(scores, axis=-1, keepdims=True))
    expo = jnp.exp(scores - top)
    attend = expo / lax.optimization_barrier(jnp.sum(expo, axis=-1, keepdims=True))
    mixed = jnp.einsum('hqk,khd->qhd', low(attend), value_heads, precision=highest).reshape(count, D)
    mixed = both_ways(mixed)
    branch = low_back(jnp.dot(mixed, output_weight, precision=highest) + output_bias)
    first = norm_rows(inputs + branch, first_gain, first_shift)
    hidden = low_back(jnp.dot(low(first), up_weight, precision=highest) + up_bias)
    active = low(jax.nn.gelu(hidden, approximate=False))
    update = low_back(jnp.dot(active, down_weight, precision=highest) + down_bias)
    return norm_rows(first + update, second_gain, second_shift)

def reference(tokens, route, lengths, query_weight, query_bias, key_weight, value_weight, value_bias, output_weight, output_bias, first_gain, first_shift, up_weight, up_bias, down_weight, down_bias, second_gain, second_shift, cotangent):
    params = tuple((member.astype(jnp.float32) for member in (query_weight, query_bias, key_weight, value_weight, value_bias, output_weight, output_bias, first_gain, first_shift, up_weight, up_bias, down_weight, down_bias, second_gain, second_shift)))
    inputs_all = tokens.astype(jnp.float32)
    pieces_all = route.shape[0]
    piece = tokens.shape[0] // pieces_all
    bounds = jnp.cumsum(lengths, axis=1).astype(jnp.int32)
    positions = jnp.arange(GROUP_TOK, dtype=jnp.int32)
    segments = lax.optimization_barrier(jnp.sum((bounds[:, None, :] <= positions[None, :, None]).astype(jnp.int32), axis=2)).astype(jnp.int32)

    def forward(inputs, weights):
        blocks = inputs.reshape(pieces_all, piece, D)
        packed = jnp.zeros_like(blocks).at[route].set(blocks).reshape(GROUPS, GROUP_TOK, D)

        def one_group(pair):
            return group_layer(pair[0], pair[1], weights)
        return lax.map(jax.checkpoint(one_group), (packed, segments)).reshape(-1, D)
    output, pullback = jax.vjp(forward, inputs_all, params)
    token_grad, grads = pullback(cotangent.astype(jnp.float32))
    return (output.astype(jnp.bfloat16), token_grad.astype(jnp.bfloat16), grads[0], grads[1], grads[2], grads[3], grads[4], grads[5], grads[6], grads[7], grads[8], grads[9], grads[10], grads[11], grads[12], grads[13], grads[14])
```

```python
import functools

import jax
import jax.numpy as jnp
from jax import lax
from jax.experimental import pallas as pl
from jax.experimental.pallas import tpu as pltpu
from jax.sharding import PartitionSpec as P

D = 512
HEADS = 8
HEAD = 64
HL = HEADS // 2
C = HL * HEAD
PAIR = 128
NEG = -1e30
BQ = 256
BK = 256
F32 = jnp.float32
BF16 = jnp.bfloat16
MESH = pl.DeviceIdType.MESH
VMEM = pltpu.VMEM
SMEM = pltpu.SMEM


def norm_rows(value, gain, shift):
    center = value - jnp.mean(value, axis=-1, keepdims=True)
    spread = jnp.mean(center * center, axis=-1, keepdims=True)
    return center * lax.rsqrt(spread + 1e-05) * gain + shift


def gelu_exact(value):
    return jax.nn.gelu(value, approximate=False)


def product(left, right):
    return jnp.dot(left, right, preferred_element_type=F32)


def product_left(left, right):
    return lax.dot_general(left, right, (((0,), (0,)), ((), ())), preferred_element_type=F32)


def product_right(left, right):
    return lax.dot_general(left, right, (((1,), (1,)), ((), ())), preferred_element_type=F32)


def column_sums(value):
    return jnp.sum(value.astype(F32), axis=0)


def swap_kernel(x_ref, o_ref, send, recv, local):
    dp, me = lax.axis_index("dp"), lax.axis_index("seq")
    other = 1 - me
    barrier = pltpu.get_barrier_semaphore()
    pl.semaphore_signal(barrier, inc=1, device_id=(dp, other), device_id_type=MESH)
    pl.semaphore_wait(barrier, 1)
    whole = len(x_ref.shape) == 2
    copy = pltpu.make_async_remote_copy(
        src_ref=x_ref if whole else x_ref.at[other],
        dst_ref=o_ref.at[me],
        send_sem=send,
        recv_sem=recv,
        device_id=(dp, other),
        device_id_type=MESH,
    )
    copy.start()
    own = pltpu.make_async_copy(x_ref if whole else x_ref.at[me], o_ref.at[me], local)
    own.start()
    own.wait()
    copy.wait()


def swap(x, collective_id):
    shape = x.shape if x.ndim == 3 else (2,) + x.shape
    return pl.pallas_call(
        swap_kernel,
        out_shape=jax.ShapeDtypeStruct(shape, x.dtype),
        in_specs=[pl.BlockSpec(memory_space=VMEM)],
        out_specs=pl.BlockSpec(memory_space=VMEM),
        scratch_shapes=[pltpu.SemaphoreType.DMA] * 3,
        compiler_params=pltpu.CompilerParams(collective_id=collective_id, has_side_effects=True),
    )(x)


def table_starts(bounds_ref, position):
    start = jnp.zeros_like(position)
    end = None
    for j in range(bounds_ref.shape[0]):
        b = bounds_ref[j]
        start = jnp.where(b <= position, b, start)
    for j in range(bounds_ref.shape[0] - 1, -1, -1):
        b = bounds_ref[j]
        end = jnp.where(b > position, b, end if end is not None else b)
    return start, end


def head_masks():
    lane = lax.broadcasted_iota(jnp.int32, (1, PAIR), 1)
    low = (lane < HEAD).astype(F32).astype(BF16)
    return low, (lane >= HEAD).astype(F32).astype(BF16)


def block_range(bounds_ref, i):
    start, _ = table_starts(bounds_ref, i * BQ)
    _, end = table_starts(bounds_ref, i * BQ + BQ - 1)
    return start // BK, (end + BK - 1) // BK


def tile_mask(bounds_ref, i):
    pos = i * BQ + lax.broadcasted_iota(jnp.int32, (1, BQ), 1)
    return table_starts(bounds_ref, pos)


def forward_kernel(
    bounds_ref, me_ref, x_ref, wq_ref, wk_ref, wv_ref, bq_ref, bv_ref,
    q_ref, k_ref, v_ref, mixed_ref, out_ref, lse_ref,
    vt_ref, acc_ref,
):
    span = x_ref.shape[0]
    blocks = span // BQ

    def project(i, _):
        rows = pl.ds(pl.multiple_of(i * BQ, BQ), BQ)
        x = x_ref[rows, :]
        q = (product(x, wq_ref[...]) + bq_ref[...].astype(F32)).astype(BF16)
        q_ref[rows, :] = (q.astype(F32) * (HEAD**-0.5)).astype(BF16)
        k_ref[rows, :] = product(x, wk_ref[...]).astype(BF16)
        v = (product(x, wv_ref[...]) + bv_ref[...].astype(F32)).astype(BF16)
        v_ref[rows, :] = v
        vt_ref[:, rows] = v.T
        return 0

    lax.fori_loop(0, blocks, project, 0)
    masks = head_masks()

    def query_block(i, _):
        rows = pl.ds(pl.multiple_of(i * BQ, BQ), BQ)
        lo, hi = block_range(bounds_ref, i)
        start, end = tile_mask(bounds_ref, i)
        q = q_ref[rows, :]
        heads = [q[:, (h // 2) * PAIR : (h // 2 + 1) * PAIR] * masks[h % 2] for h in range(HL)]
        acc_ref[...] = jnp.zeros_like(acc_ref)

        def key_block(j, carry):
            keys = pl.ds(pl.multiple_of(j * BK, BK), BK)
            kpos = j * BK + lax.broadcasted_iota(jnp.int32, (BK, BQ), 0)
            mask = (kpos >= start) & (kpos < end)
            tops, totals = carry
            new_tops, new_totals = [], []
            for h in range(HL):
                kp = k_ref[keys, (h // 2) * PAIR : (h // 2 + 1) * PAIR]
                s = jnp.where(mask, product_right(kp, heads[h]), NEG)
                top = jnp.maximum(tops[h], jnp.max(s, axis=0, keepdims=True))
                p = jnp.exp(s - top)
                alpha = jnp.exp(tops[h] - top)
                new_totals.append(totals[h] * alpha + jnp.sum(p, axis=0, keepdims=True))
                new_tops.append(top)
                lanes = slice(h * HEAD, (h + 1) * HEAD)
                acc_ref[lanes, :] = acc_ref[lanes, :] * alpha + product(
                    vt_ref[lanes, keys], p.astype(BF16)
                )
            return tuple(new_tops), tuple(new_totals)

        tops = tuple(jnp.full((1, BQ), NEG, F32) for _ in range(HL))
        totals = tuple(jnp.zeros((1, BQ), F32) for _ in range(HL))
        tops, totals = lax.fori_loop(lo, hi, key_block, (tops, totals))
        for h in range(HL):
            lanes = slice(h * HEAD, (h + 1) * HEAD)
            acc_ref[lanes, :] = acc_ref[lanes, :] / totals[h]
            lse_ref[h : h + 1, rows] = tops[h] + jnp.log(totals[h])
        out = acc_ref[...]
        out_ref[:, rows] = out
        mixed_ref[rows, :] = out.T.astype(BF16)
        return 0

    lax.fori_loop(0, blocks, query_block, 0)


def column_block(shape):
    return pl.BlockSpec(shape, lambda i, bounds, me: (0, me[0]))


def whole_block(shape):
    return pl.BlockSpec(shape, lambda i, bounds, me: (0,) * len(shape))


def attend_forward(x_all, bounds, me, wq, wk, wv, bq, bv):
    span = x_all.shape[0]
    rows_shape = jax.ShapeDtypeStruct((span, C), BF16)
    return pl.pallas_call(
        forward_kernel,
        grid_spec=pltpu.PrefetchScalarGridSpec(
            num_scalar_prefetch=2,
            grid=(1,),
            in_specs=[
                whole_block((span, D)),
                column_block((D, C)),
                column_block((D, C)),
                column_block((D, C)),
                column_block((1, C)),
                column_block((1, C)),
            ],
            out_specs=[whole_block((span, C))] * 4 + [whole_block((C, span)), whole_block((8, span))],
            scratch_shapes=[VMEM((C, span), BF16), VMEM((C, BQ), F32)],
        ),
        out_shape=[rows_shape] * 4
        + [jax.ShapeDtypeStruct((C, span), F32), jax.ShapeDtypeStruct((8, span), F32)],
        name="attend_forward",
    )(bounds, me, x_all, wq, wk, wv, bq.reshape(1, D), bv.reshape(1, D))


def backward_kernel(
    bounds_ref, me_ref, x_ref, q_ref, k_ref, v_ref, g_ref, out_ref, lse_ref, wq_ref, wk_ref, wv_ref,
    gw_ref, sums_ref, gx_ref,
    kt_ref, gq_ref, gk_ref, gv_ref, gqt_ref,
):
    span = x_ref.shape[0]
    blocks = span // BQ
    scale = HEAD**-0.5

    def prepare(i, _):
        rows = pl.ds(pl.multiple_of(i * BQ, BQ), BQ)
        kt_ref[:, rows] = k_ref[rows, :].T
        gk_ref[rows, :] = jnp.zeros((BQ, C), F32)
        gv_ref[rows, :] = jnp.zeros((BQ, C), F32)
        return 0

    lax.fori_loop(0, blocks, prepare, 0)
    masks = head_masks()

    def query_block(i, _):
        rows = pl.ds(pl.multiple_of(i * BQ, BQ), BQ)
        lo, hi = block_range(bounds_ref, i)
        start, end = tile_mask(bounds_ref, i)
        q = q_ref[rows, :]
        g = g_ref[rows, :]
        pairs = [slice((h // 2) * PAIR, (h // 2 + 1) * PAIR) for h in range(HL)]
        queries = [q[:, pairs[h]] * masks[h % 2] for h in range(HL)]
        grads = [g[:, pairs[h]] * masks[h % 2] for h in range(HL)]
        weighted = g.astype(F32).T * out_ref[:, rows]
        inner = [
            jnp.sum(weighted[h * HEAD : (h + 1) * HEAD], axis=0, keepdims=True) for h in range(HL)
        ]
        logsum = [lse_ref[h : h + 1, rows] for h in range(HL)]
        gqt_ref[...] = jnp.zeros_like(gqt_ref)

        def key_block(j, _):
            keys = pl.ds(pl.multiple_of(j * BK, BK), BK)
            kpos = j * BK + lax.broadcasted_iota(jnp.int32, (BK, BQ), 0)
            mask = (kpos >= start) & (kpos < end)
            for p in range(HL // 2):
                lanes = slice(p * PAIR, (p + 1) * PAIR)
                kp, vp = k_ref[keys, lanes], v_ref[keys, lanes]
                gk = gk_ref[keys, lanes]
                gv = gv_ref[keys, lanes]
                for h in (2 * p, 2 * p + 1):
                    s = product_right(kp, queries[h])
                    w = jnp.where(mask, jnp.exp(s - logsum[h]), 0.0)
                    gw = product_right(vp, grads[h])
                    gs = (w * (gw - inner[h])).astype(BF16)
                    gv = gv + product(w.astype(BF16), grads[h])
                    gk = gk + product(gs, queries[h])
                    part = slice(h * HEAD, (h + 1) * HEAD)
                    gqt_ref[part, :] += product(kt_ref[part, keys], gs)
                gk_ref[keys, lanes] = gk
                gv_ref[keys, lanes] = gv
            return 0

        lax.fori_loop(lo, hi, key_block, 0)
        gq_ref[rows, :] = (gqt_ref[...].T * scale).astype(BF16)
        return 0

    lax.fori_loop(0, blocks, query_block, 0)

    wide = span // 4

    def tail(i, _):
        rows = pl.ds(pl.multiple_of(i * wide, wide), wide)
        gq, gk, gv = gq_ref[rows, :], gk_ref[rows, :].astype(BF16), gv_ref[rows, :].astype(BF16)
        gx = product_right(gq, wq_ref[...]) + product_right(gk, wk_ref[...])
        gx_ref[rows, :] = (gx + product_right(gv, wv_ref[...])).astype(BF16)
        x = x_ref[rows, :]
        for n, part in enumerate((gq, gk, gv)):
            term = product_left(x, part)
            gw_ref[n] = jnp.where(i == 0, term, gw_ref[n] + term)
        sums = jnp.concatenate(
            [jnp.sum(a.astype(F32), axis=0, keepdims=True) for a in (gq, gv)], axis=1
        )
        sums_ref[...] = jnp.where(i == 0, sums, sums_ref[...] + sums)
        return 0

    lax.fori_loop(0, 4, tail, 0)


def attend_backward(bounds, me, x_all, q, k, v, g, out, lse, wq, wk, wv):
    span = x_all.shape[0]
    rows = whole_block((span, C))
    return pl.pallas_call(
        backward_kernel,
        grid_spec=pltpu.PrefetchScalarGridSpec(
            num_scalar_prefetch=2,
            grid=(1,),
            in_specs=[whole_block((span, D)), rows, rows, rows, rows]
            + [whole_block((C, span)), whole_block((8, span))]
            + [column_block((D, C))] * 3,
            out_specs=[whole_block((3, D, C)), whole_block((1, 2 * C)), whole_block((span, D))],
            scratch_shapes=[
                VMEM((C, span), BF16),
                VMEM((span, C), BF16),
                VMEM((span, C), F32),
                VMEM((span, C), F32),
                VMEM((C, BQ), F32),
            ],
        ),
        out_shape=[
            jax.ShapeDtypeStruct((3, D, C), F32),
            jax.ShapeDtypeStruct((1, 2 * C), F32),
            jax.ShapeDtypeStruct((span, D), BF16),
        ],
        name="attend_backward",
    )(bounds, me, x_all, q, k, v, g, out, lse, wq, wk, wv)


def sum_plan(n):
    weights = []
    w = 1
    while w < n:
        weights.append(w)
        w *= 2
    first = list(weights)
    second = list(weights)
    second[0], second[1] = second[1], second[0]
    return list(zip(first, second))


def rows_add(acc, base, other, size, into):
    step = min(size, 64 if acc.shape[-1] > 1024 else 128)

    def add(i, _):
        here = pl.ds(pl.multiple_of(base + i * step, 16), step)
        there = pl.ds(pl.multiple_of(i * step, step), step)
        into[here, :] = (acc[here, :].astype(F32) + other[there, :].astype(F32)).astype(acc.dtype)
        return 0

    lax.fori_loop(0, size // step, add, 0)


def sum_kernel(n, count, *refs):
    ins = refs[: count + 2]
    outs = refs[count + 2 : 2 * count + 4]
    accs = refs[2 * count + 4 : 3 * count + 5]
    recvs = refs[3 * count + 5 : 4 * count + 6]
    fulls = refs[4 * count + 6 : 5 * count + 7]
    handed, vec_recv, send, recv = refs[5 * count + 7 :]
    shared, own_in, vec_in = ins[:count], ins[count], ins[count + 1]
    dp, me = lax.axis_index("dp"), lax.axis_index("seq")
    plan = sum_plan(n)

    def peer(weights):
        w = weights[0] + me * (weights[1] - weights[0])
        bit = (dp // w) % 2
        return dp + (1 - 2 * bit) * w, bit

    barrier = pltpu.get_barrier_semaphore()
    for a, b in plan:
        w = a
        bit = (dp // w) % 2
        pl.semaphore_signal(
            barrier, inc=1, device_id=(dp + (1 - 2 * bit) * w, me), device_id_type=MESH
        )
    pl.semaphore_signal(barrier, inc=1, device_id=(dp, 1 - me), device_id_type=MESH)
    pl.semaphore_wait(barrier, len(plan) + 1)

    def push(src, dst, chunk, stage, device):
        return pltpu.make_async_remote_copy(
            src_ref=src,
            dst_ref=dst,
            send_sem=send.at[chunk, stage],
            recv_sem=recv.at[chunk, stage],
            device_id=device,
            device_id_type=MESH,
        )

    def chunk_steps(c):
        acc, landing, full = accs[c], recvs[c], fulls[c]
        rows = acc.shape[0]
        paired = c < count
        steps = []
        state = {"base": 0, "size": rows, "copy": None, "offset": 0, "stage": 0, "kept": []}

        def send_half(device, bit):
            half = state["size"] // 2
            keep = state["base"] + bit * half
            give = state["base"] + (1 - bit) * half
            src = acc.at[pl.ds(pl.multiple_of(give, 16), half), :]
            dst = landing.at[pl.ds(state["offset"], half), :]
            copy = push(src, dst, c, state["stage"], device)
            copy.start()
            state["copy"] = (copy, keep, half, state["offset"])
            state["kept"].append((keep, half, device))
            state["stage"] += 1

        def finish_half(into=acc):
            copy, keep, half, offset = state["copy"]
            copy.wait()
            rows_add(acc, keep, landing.at[pl.ds(offset, half), :], half, into)
            state["base"], state["size"], state["offset"] = keep, half, offset + half

        def first():
            if paired:
                send_half((dp, 1 - me), me)
            else:
                device, bit = peer(plan[0])
                send_half((device, me), bit)

        steps.append(first)
        rest = plan if paired else plan[1:]
        for weights in rest:

            def onward(weights=weights):
                finish_half()
                device, bit = peer(weights)
                send_half((device, me), bit)

            steps.append(onward)

        def gather(last):
            def run():
                if not last:
                    finish_half(full)
                    state["back"] = list(reversed(state["kept"]))
                else:
                    state["copy"].wait()
                    state["back"].pop(0)
                keep, half, device = state["back"][0]
                region = full.at[pl.ds(pl.multiple_of(keep, 16), half), :]
                copy = push(region, region, c, state["stage"], device)
                copy.start()
                state["copy"] = copy
                state["stage"] += 1

            return run

        for g in range(len(rest) + 1):
            steps.append(gather(g > 0))
        if not paired:

            def hand_over():
                state["copy"].wait()
                copy = push(full, handed, c, state["stage"], (dp, 1 - me))
                copy.start()
                state["copy"] = copy

            steps.append(hand_over)

        def close():
            state["copy"].wait()
            if paired:
                out = outs[c]
                step = 128 if acc.shape[1] <= 512 else 32

                def widen(i, _):
                    here = pl.ds(pl.multiple_of(i * step, step), step)
                    out[here, :] = full[here, :].astype(F32)
                    return 0

                lax.fori_loop(0, rows // step, widen, 0)
            else:
                out = outs[c]
                third = acc.shape[1] // 3
                for w in range(3):
                    for source, half in ((full, me), (handed, 1 - me)):
                        lanes = pl.ds(pl.multiple_of(half * third, third), third)
                        out[w, :, lanes] = source[0:rows, w * third : (w + 1) * third].astype(F32)

        steps.append(close)
        return steps

    vec_out = outs[count + 1]

    def vec_steps():
        state = {}
        steps = []
        peers = [(dp, 1 - me)]
        for a, _ in plan:
            bit = (dp // a) % 2
            peers.append((dp + (1 - 2 * bit) * a, me))
        for s, device in enumerate(peers):

            def run(s=s, device=device):
                if s == 0:
                    vec_out[...] = vec_in[...]
                else:
                    state["copy"].wait()
                    vec_out[...] += vec_recv[s - 1]
                sent = vec_recv.at[len(peers) + s]
                sent[...] = vec_out[...]
                copy = push(sent, vec_recv.at[s], count + 1, s, device)
                copy.start()
                state["copy"] = copy

            steps.append(run)

        def close():
            state["copy"].wait()
            vec_out[...] += vec_recv[len(peers) - 1]

        steps.append(close)
        return steps

    for c in range(count + 1):
        source = shared[c] if c < count else own_in
        acc = accs[c]
        step = min(64, acc.shape[0])

        def load(i, _, acc=acc, source=source, step=step):
            here = pl.ds(pl.multiple_of(i * step, step), step)
            acc[here, :] = source[here, :].astype(BF16)
            return 0

        lax.fori_loop(0, acc.shape[0] // step, load, 0)

    lines = [chunk_steps(c) for c in range(count + 1)] + [vec_steps()]
    ticks = max(len(line) + at for at, line in enumerate(lines))
    for t in range(ticks):
        for at, line in enumerate(lines):
            if 0 <= t - at < len(line):
                line[t - at]()


def sum_gradients(shared, own, vec, n, collective_id):
    count = len(shared)
    stages = 2 * len(sum_plan(n)) + 3
    accs = [VMEM(a.shape, BF16) for a in shared] + [VMEM(own.shape, BF16)]
    vmem = pl.BlockSpec(memory_space=VMEM)
    return pl.pallas_call(
        functools.partial(sum_kernel, n, count),
        out_shape=[jax.ShapeDtypeStruct(a.shape, F32) for a in shared]
        + [jax.ShapeDtypeStruct((3, own.shape[0], 2 * own.shape[1] // 3), F32)]
        + [jax.ShapeDtypeStruct(vec.shape, F32)],
        in_specs=[vmem] * (count + 2),
        out_specs=[vmem] * (count + 2),
        scratch_shapes=accs
        + accs
        + accs
        + [
            VMEM(own.shape, BF16),
            VMEM((2 * len(sum_plan(n)) + 2,) + vec.shape, F32),
            pltpu.SemaphoreType.DMA((count + 2, stages)),
            pltpu.SemaphoreType.DMA((count + 2, stages)),
        ],
        compiler_params=pltpu.CompilerParams(
            collective_id=collective_id, has_side_effects=True, vmem_limit_bytes=60 << 20
        ),
        name="sum_gradients",
    )(*shared, own, vec)


def body(
    tokens,
    route,
    lengths,
    query_weight,
    query_bias,
    key_weight,
    value_weight,
    value_bias,
    output_weight,
    output_bias,
    first_gain,
    first_shift,
    up_weight,
    up_bias,
    down_weight,
    down_bias,
    second_gain,
    second_shift,
    cotangent,
):
    groups = lax.axis_size("dp")
    rows = tokens.shape[0]
    piece = rows // groups
    span = rows * lax.axis_size("seq")
    seq = lax.axis_index("seq")
    target = route // groups // lax.axis_size("seq")
    place = route % groups
    outgoing = jnp.zeros((groups, piece, D), BF16).at[target].set(tokens.reshape(groups, piece, D))
    slots_out = jnp.zeros((groups,), jnp.int32).at[target].set(place)
    incoming, slots_in = (
        lax.all_to_all(outgoing, "dp", split_axis=0, concat_axis=0, tiled=True),
        lax.all_to_all(slots_out, "dp", split_axis=0, concat_axis=0, tiled=True),
    )
    inputs = jnp.zeros_like(incoming).at[slots_in].set(incoming).reshape(rows, D)
    bounds = jnp.cumsum(lengths[0]).astype(jnp.int32)
    me = seq.reshape(1).astype(jnp.int32)
    x_all = swap(inputs, 0).reshape(span, D)
    q, k, v, mixed_all, attend_out, lse = attend_forward(
        x_all, bounds, me, query_weight, key_weight, value_weight, query_bias, value_bias
    )
    mixed_halves = swap(mixed_all.reshape(2, rows, C), 1)
    mixed = jnp.concatenate([mixed_halves[0], mixed_halves[1]], axis=1)
    branch = product(mixed, output_weight) + output_bias
    residual = inputs.astype(F32) + branch
    first, first_back = jax.vjp(
        norm_rows, residual, first_gain.astype(F32), first_shift.astype(F32)
    )
    first_low = first.astype(BF16)
    hidden = product(first_low, up_weight) + up_bias
    active = gelu_exact(hidden).astype(BF16)
    update = product(active, down_weight) + down_bias
    layer_out, second_back = jax.vjp(
        norm_rows, first + update, second_gain.astype(F32), second_shift.astype(F32)
    )
    grad_second, grad_second_gain, grad_second_shift = second_back(cotangent.astype(F32))
    grad_update = grad_second.astype(BF16)
    again = product(first_low, up_weight) + up_bias
    active_again, gelu_back = jax.vjp(gelu_exact, again)
    active_low = active_again.astype(BF16)
    grad_down = product_left(active_low, grad_update)
    grad_down_bias = column_sums(grad_update)
    (grad_active,) = gelu_back(product_right(grad_update, down_weight))
    grad_hidden = grad_active.astype(BF16)
    grad_up = product_left(first_low, grad_hidden)
    grad_up_bias = column_sums(grad_hidden)
    grad_first = grad_second + product_right(grad_hidden, up_weight)
    grad_residual, grad_first_gain, grad_first_shift = first_back(grad_first)
    grad_branch = grad_residual.astype(BF16)
    grad_output = product_left(mixed, grad_branch)
    grad_output_bias = column_sums(grad_branch)
    grad_mixed = product_right(grad_branch, output_weight).astype(BF16)
    grad_halves = jnp.stack([grad_mixed[:, :C], grad_mixed[:, C:]])
    grad_mixed_all = swap(grad_halves, 2).reshape(span, C)
    grad_columns, column_parts, grad_x = attend_backward(
        bounds, me, x_all, q, k, v, grad_mixed_all, attend_out, lse,
        query_weight, key_weight, value_weight,
    )
    grad_parts = swap(grad_x.reshape(2, rows, D), 3)
    grad_inputs = grad_residual + grad_parts[0].astype(F32) + grad_parts[1].astype(F32)
    back_rows = grad_inputs.astype(BF16).reshape(groups, piece, D)[slots_in]
    returned = lax.all_to_all(back_rows, "dp", split_axis=0, concat_axis=0, tiled=True)
    token_grad = returned[target].reshape(rows, D)

    def own_columns(part):
        return lax.dynamic_update_slice(jnp.zeros((1, D), F32), part, (0, seq * C))

    vec = jnp.concatenate(
        [
            own_columns(column_parts[:, :C]),
            own_columns(column_parts[:, C:]),
            jnp.stack(
                [
                    grad_output_bias,
                    grad_first_gain,
                    grad_first_shift,
                    grad_down_bias,
                    grad_second_gain,
                    grad_second_shift,
                ]
            ),
            grad_up_bias.reshape(-1, D),
            jnp.zeros((4, D), F32),
        ]
    )
    if groups == 16:
        up_sum, down_sum, out_sum, columns, vec = sum_gradients(
            [grad_up, grad_down, grad_output],
            jnp.concatenate([grad_columns[0], grad_columns[1], grad_columns[2]], axis=1),
            vec, groups, 4,
        )
        query_sum, key_sum, value_sum = columns[0], columns[1], columns[2]
    else:
        up_sum, down_sum, out_sum, vec = lax.psum((grad_up, grad_down, grad_output, vec), ("dp", "seq"))
        columns = lax.all_gather(lax.psum(grad_columns, "dp"), "seq", axis=2, tiled=True)
        query_sum, key_sum, value_sum = columns[0], columns[1], columns[2]
    return (
        layer_out.astype(BF16),
        token_grad,
        query_sum,
        vec[0],
        key_sum,
        value_sum,
        vec[1],
        out_sum,
        vec[2],
        vec[3],
        vec[4],
        up_sum,
        vec[8:12].reshape(-1),
        down_sum,
        vec[5],
        vec[6],
        vec[7],
    )


def solution(mesh):
    both, one = P(("dp", "seq"), None), P()
    return jax.shard_map(
        body,
        mesh=mesh,
        in_specs=(both, P(("dp", "seq")), P("dp", None)) + (one,) * 15 + (both,),
        out_specs=(both, both) + (one,) * 15,
        check_vma=False,
    )
```

```python
import functools

import jax
import jax.numpy as jnp
from jax import lax
from jax.experimental import pallas as pl
from jax.experimental.pallas import tpu as pltpu
from jax.sharding import PartitionSpec as P

D = 512
HEADS = 8
HEAD = 64
HL = HEADS // 2
C = HL * HEAD
PAIR = 128
NEG = -1e30
LOG2E = 1.4426950408889634
BQ = 256
BK = 256
F32 = jnp.float32
BF16 = jnp.bfloat16
MESH = pl.DeviceIdType.MESH
VMEM = pltpu.VMEM
SMEM = pltpu.SMEM


def norm_rows(value, gain, shift):
    center = value - jnp.mean(value, axis=-1, keepdims=True)
    spread = jnp.mean(center * center, axis=-1, keepdims=True)
    return center * lax.rsqrt(spread + 1e-05) * gain + shift


def gelu_exact(value):
    return jax.nn.gelu(value, approximate=False)


def product(left, right):
    return jnp.dot(left, right, preferred_element_type=F32)


def product_left(left, right):
    return lax.dot_general(left, right, (((0,), (0,)), ((), ())), preferred_element_type=F32)


def product_right(left, right):
    return lax.dot_general(left, right, (((1,), (1,)), ((), ())), preferred_element_type=F32)


def column_sums(value):
    return jnp.sum(value.astype(F32), axis=0)


def swap_kernel(x_ref, o_ref, send, recv, local):
    dp, me = lax.axis_index("dp"), lax.axis_index("seq")
    other = 1 - me
    barrier = pltpu.get_barrier_semaphore()
    pl.semaphore_signal(barrier, inc=1, device_id=(dp, other), device_id_type=MESH)
    pl.semaphore_wait(barrier, 1)
    whole = len(x_ref.shape) == 2
    copy = pltpu.make_async_remote_copy(
        src_ref=x_ref if whole else x_ref.at[other],
        dst_ref=o_ref.at[me],
        send_sem=send,
        recv_sem=recv,
        device_id=(dp, other),
        device_id_type=MESH,
    )
    copy.start()
    own = pltpu.make_async_copy(x_ref if whole else x_ref.at[me], o_ref.at[me], local)
    own.start()
    own.wait()
    copy.wait()


def swap(x, collective_id):
    shape = x.shape if x.ndim == 3 else (2,) + x.shape
    return pl.pallas_call(
        swap_kernel,
        out_shape=jax.ShapeDtypeStruct(shape, x.dtype),
        in_specs=[pl.BlockSpec(memory_space=VMEM)],
        out_specs=pl.BlockSpec(memory_space=VMEM),
        scratch_shapes=[pltpu.SemaphoreType.DMA] * 3,
        compiler_params=pltpu.CompilerParams(collective_id=collective_id, has_side_effects=True),
    )(x)


def table_starts(bounds_ref, position):
    start = jnp.zeros_like(position)
    end = None
    for j in range(bounds_ref.shape[0]):
        b = bounds_ref[j]
        start = jnp.where(b <= position, b, start)
    for j in range(bounds_ref.shape[0] - 1, -1, -1):
        b = bounds_ref[j]
        end = jnp.where(b > position, b, end if end is not None else b)
    return start, end


def head_masks():
    lane = lax.broadcasted_iota(jnp.int32, (1, PAIR), 1)
    low = (lane < HEAD).astype(F32).astype(BF16)
    return low, (lane >= HEAD).astype(F32).astype(BF16)


def block_range(bounds_ref, i):
    start, first_end = table_starts(bounds_ref, i * BQ)
    last_start, end = table_starts(bounds_ref, i * BQ + BQ - 1)
    lo, hi = start // BK, (end + BK - 1) // BK
    a, b = (last_start + BK - 1) // BK, first_end // BK
    some = a < b
    return lo, jnp.where(some, a, hi), jnp.where(some, b, hi), hi


def tile_mask(bounds_ref, i):
    pos = i * BQ + lax.broadcasted_iota(jnp.int32, (1, BQ), 1)
    return table_starts(bounds_ref, pos)


def three_loops(ranges, run, carry):
    lo, a, b, hi = ranges
    carry = lax.fori_loop(lo, a, functools.partial(run, True), carry)
    carry = lax.fori_loop(a, b, functools.partial(run, False), carry)
    return lax.fori_loop(b, hi, functools.partial(run, True), carry)


def by_eight(value, op):
    return op(value.reshape(value.shape[0] // 8, 8, value.shape[1]), axis=0)


def forward_kernel(
    pieces, bounds_ref, me_ref, slot_ref, loaded_ref, wq_ref, wk_ref, wv_ref, bq_ref, bv_ref,
    q_ref, k_ref, v_ref, mixed_ref, out_ref, lse_ref, own_ref,
    vt_ref, acc_ref, s_ref, packed_ref,
):
    span = loaded_ref.shape[0]
    blocks = span // BQ
    x_ref = packed_ref if pieces else loaded_ref
    if pieces:
        piece = span // pieces
        for k in range(pieces):
            row = (k // (pieces // 2)) * (span // 2) + slot_ref[k] * piece
            rows = pl.ds(pl.multiple_of(row, piece), piece)
            packed_ref[rows, :] = loaded_ref[k * piece : (k + 1) * piece, :]
    half = span // 2
    own_ref[...] = x_ref[pl.ds(pl.multiple_of(me_ref[0] * half, half), half), :]

    def project(i, _):
        rows = pl.ds(pl.multiple_of(i * BQ, BQ), BQ)
        x = x_ref[rows, :]
        q = (product(x, wq_ref[...]) + bq_ref[...].astype(F32)).astype(BF16)
        q_ref[rows, :] = (q.astype(F32) * (HEAD**-0.5)).astype(BF16)
        k_ref[rows, :] = product(x, wk_ref[...]).astype(BF16)
        v = (product(x, wv_ref[...]) + bv_ref[...].astype(F32)).astype(BF16)
        v_ref[rows, :] = v
        vt_ref[:, rows] = v.T
        return 0

    lax.fori_loop(0, blocks, project, 0)
    masks = head_masks()

    def query_block(i, _):
        rows = pl.ds(pl.multiple_of(i * BQ, BQ), BQ)
        ranges = block_range(bounds_ref, i)
        start, end = tile_mask(bounds_ref, i)
        q = q_ref[rows, :]
        heads = [q[:, (h // 2) * PAIR : (h // 2 + 1) * PAIR] * masks[h % 2] for h in range(HL)]
        acc_ref[...] = jnp.zeros_like(acc_ref)

        def score_block(masked, j, tops):
            keys = pl.ds(pl.multiple_of(j * BK, BK), BK)
            if masked:
                kpos = j * BK + lax.broadcasted_iota(jnp.int32, (BK, BQ), 0)
                mask = (kpos >= start) & (kpos < end)
            new = []
            for h in range(HL):
                kp = k_ref[keys, (h // 2) * PAIR : (h // 2 + 1) * PAIR]
                s = product_right(kp, heads[h]) * LOG2E
                if masked:
                    s = jnp.where(mask, s, NEG)
                s_ref[h, keys, :] = s
                new.append(jnp.maximum(tops[h], by_eight(s, jnp.max)))
            return tuple(new)

        tops = three_loops(
            ranges, score_block, tuple(jnp.full((8, BQ), NEG, F32) for _ in range(HL))
        )
        tops = [jnp.max(t, axis=0, keepdims=True) for t in tops]

        def mix_block(j, totals):
            keys = pl.ds(pl.multiple_of(j * BK, BK), BK)
            new = []
            for h in range(HL):
                p = jnp.exp2(s_ref[h, keys, :] - tops[h])
                new.append(totals[h] + by_eight(p, jnp.sum))
                lanes = slice(h * HEAD, (h + 1) * HEAD)
                acc_ref[lanes, :] += product(vt_ref[lanes, keys], p.astype(BF16))
            return tuple(new)

        totals = lax.fori_loop(
            ranges[0], ranges[3], mix_block, tuple(jnp.zeros((8, BQ), F32) for _ in range(HL))
        )
        for h in range(HL):
            total = jnp.sum(totals[h], axis=0, keepdims=True)
            lanes = slice(h * HEAD, (h + 1) * HEAD)
            acc_ref[lanes, :] = acc_ref[lanes, :] / total
            lse_ref[h : h + 1, rows] = tops[h] + jnp.log2(total)
        out = acc_ref[...]
        out_ref[:, rows] = out
        mixed_ref[rows, :] = out.T.astype(BF16)
        return 0

    lax.fori_loop(0, blocks, query_block, 0)


def column_block(shape):
    return pl.BlockSpec(shape, lambda i, bounds, me, slots: (0, me[0]))


def whole_block(shape):
    return pl.BlockSpec(shape, lambda i, bounds, me, slots: (0,) * len(shape))


def attend_forward(x_all, pieces, bounds, me, slots, wq, wk, wv, bq, bv):
    span = x_all.shape[0]
    rows_shape = jax.ShapeDtypeStruct((span, C), BF16)
    return pl.pallas_call(
        functools.partial(forward_kernel, pieces),
        grid_spec=pltpu.PrefetchScalarGridSpec(
            num_scalar_prefetch=3,
            grid=(1,),
            in_specs=[
                whole_block((span, D)),
                column_block((D, C)),
                column_block((D, C)),
                column_block((D, C)),
                column_block((1, C)),
                column_block((1, C)),
            ],
            out_specs=[whole_block((span, C))] * 4
            + [whole_block((C, span)), whole_block((8, span)), whole_block((span // 2, D))],
            scratch_shapes=[VMEM((C, span), BF16), VMEM((C, BQ), F32), VMEM((HL, span, BQ), F32), VMEM((span, D), BF16)],
        ),
        out_shape=[rows_shape] * 4
        + [jax.ShapeDtypeStruct((C, span), F32), jax.ShapeDtypeStruct((8, span), F32)]
        + [jax.ShapeDtypeStruct((span // 2, D), BF16)],
        name="attend_forward",
    )(bounds, me, slots, x_all, wq, wk, wv, bq.reshape(1, D), bv.reshape(1, D))


def backward_kernel(
    pieces, bounds_ref, me_ref, slot_ref,
    x_ref, q_ref, k_ref, v_ref, g_ref, out_ref, lse_ref, wq_ref, wk_ref, wv_ref, res_ref,
    gw_ref, sums_ref, ga_ref, gb_ref,
    kt_ref, gq_ref, gk_ref, gv_ref, gqt_ref, qs_ref, gs_ref, w_ref, ds_ref, term_ref,
):
    span = x_ref.shape[0]
    blocks = span // BQ
    scale = HEAD**-0.5

    def prepare(i, _):
        rows = pl.ds(pl.multiple_of(i * BQ, BQ), BQ)
        kt_ref[:, rows] = k_ref[rows, :].T
        gk_ref[rows, :] = jnp.zeros((BQ, C), F32)
        gv_ref[rows, :] = jnp.zeros((BQ, C), F32)
        return 0

    lax.fori_loop(0, blocks, prepare, 0)
    lane = lax.broadcasted_iota(jnp.int32, (1, C), 1) // HEAD
    masks = [(lane == h).astype(F32).astype(BF16) for h in range(HL)]

    def query_block(i, _):
        rows = pl.ds(pl.multiple_of(i * BQ, BQ), BQ)
        ranges = block_range(bounds_ref, i)
        start, end = tile_mask(bounds_ref, i)
        q = q_ref[rows, :]
        g = g_ref[rows, :]
        for h in range(HL):
            part = slice(h * BQ, (h + 1) * BQ)
            qs_ref[part, :] = q * masks[h]
            gs_ref[part, :] = g * masks[h]
        weighted = g.astype(F32).T * out_ref[:, rows]
        inner = [
            jnp.sum(weighted[h * HEAD : (h + 1) * HEAD], axis=0, keepdims=True) for h in range(HL)
        ]
        logsum = [lse_ref[h : h + 1, rows] for h in range(HL)]
        gqt_ref[...] = jnp.zeros_like(gqt_ref)

        def key_block(masked, j, _):
            keys = pl.ds(pl.multiple_of(j * BK, BK), BK)
            if masked:
                kpos = j * BK + lax.broadcasted_iota(jnp.int32, (BK, BQ), 0)
                mask = (kpos >= start) & (kpos < end)
            for h in range(HL):
                part = slice(h * BQ, (h + 1) * BQ)
                pair = slice((h // 2) * PAIR, (h // 2 + 1) * PAIR)
                s = product_right(k_ref[keys, pair], qs_ref[part, pair])
                w = jnp.exp2(s * LOG2E - logsum[h])
                if masked:
                    w = jnp.where(mask, w, 0.0)
                gw = product_right(v_ref[keys, pair], gs_ref[part, pair])
                gs = (w * (gw - inner[h])).astype(BF16)
                w_ref[keys, part] = w.astype(BF16)
                ds_ref[keys, part] = gs
            return 0

        def product_block(j, _):
            keys = pl.ds(pl.multiple_of(j * BK, BK), BK)
            for h in range(HL):
                part = slice(h * BQ, (h + 1) * BQ)
                lanes = slice(h * HEAD, (h + 1) * HEAD)
                gqt_ref[lanes, :] += product(kt_ref[lanes, keys], ds_ref[keys, part])
            gv_ref[keys, :] += product(w_ref[keys, :], gs_ref[...])
            gk_ref[keys, :] += product(ds_ref[keys, :], qs_ref[...])
            return 0

        three_loops(ranges, key_block, 0)
        lax.fori_loop(ranges[0], ranges[3], product_block, 0)
        gq_ref[rows, :] = (gqt_ref[...].T * scale).astype(BF16)
        return 0

    lax.fori_loop(0, blocks, query_block, 0)

    count = 4
    wide = span // count
    half = span // 2

    def load(ref, i):
        if not pieces:
            return ref[pl.ds(pl.multiple_of(i * wide, wide), wide), :].astype(BF16)
        piece = span // pieces
        each = pieces // count
        parts = []
        for k in range(each):
            row = (i // (count // 2)) * half + slot_ref[i * each + k] * piece
            parts.append(ref[pl.ds(pl.multiple_of(row, piece), piece), :].astype(BF16))
        return jnp.concatenate(parts, axis=0)

    def own_rows(i):
        if not pieces:
            return res_ref[pl.ds(pl.multiple_of(i * wide, wide), wide), :]
        piece = span // pieces
        each = pieces // count
        parts = []
        for k in range(each):
            row = slot_ref[me_ref[0] * (pieces // 2) + i * each + k] * piece
            parts.append(res_ref[pl.ds(pl.multiple_of(row, piece), piece), :])
        return jnp.concatenate(parts, axis=0)

    def gradients(i):
        rows = pl.ds(pl.multiple_of(i * wide, wide), wide)
        gq, gk, gv = load(gq_ref, i), load(gk_ref, i), load(gv_ref, i)
        x = x_ref[rows, :]
        for n, part in enumerate((gq, gk, gv)):
            term_ref[n] += product_left(x, part)
        sums_ref[...] += jnp.concatenate(
            [jnp.sum(a.astype(F32), axis=0, keepdims=True) for a in (gq, gv)], axis=1
        )
        gx = product_right(gq, wq_ref[...]) + product_right(gk, wk_ref[...])
        return gx + product_right(gv, wv_ref[...])

    term_ref[...] = jnp.zeros_like(term_ref)
    sums_ref[...] = jnp.zeros_like(sums_ref)
    blocks_each = count // 2

    def own_tail(i, _):
        gx = gradients(me_ref[0] * blocks_each + i)
        ga_ref[pl.ds(pl.multiple_of(i * wide, wide), wide), :] = gx + own_rows(i)
        return 0

    def other_tail(i, _):
        gx = gradients((1 - me_ref[0]) * blocks_each + i)
        gb_ref[pl.ds(pl.multiple_of(i * wide, wide), wide), :] = gx.astype(BF16)
        return 0

    lax.fori_loop(0, blocks_each, own_tail, 0)
    lax.fori_loop(0, blocks_each, other_tail, 0)
    gw_ref[...] = term_ref[...].astype(BF16)


def attend_backward(bounds, me, slots, pieces, x_all, q, k, v, g, out, lse, wq, wk, wv, res):
    span = x_all.shape[0]
    rows = whole_block((span, C))
    return pl.pallas_call(
        functools.partial(backward_kernel, pieces),
        grid_spec=pltpu.PrefetchScalarGridSpec(
            num_scalar_prefetch=3,
            grid=(1,),
            in_specs=[whole_block((span, D)), rows, rows, rows, rows]
            + [whole_block((C, span)), whole_block((8, span))]
            + [column_block((D, C))] * 3
            + [whole_block((span // 2, D))],
            out_specs=[whole_block((3, D, C)), whole_block((1, 2 * C))]
            + [whole_block((span // 2, D))] * 2,
            scratch_shapes=[
                VMEM((C, span), BF16),
                VMEM((span, C), BF16),
                VMEM((span, C), F32),
                VMEM((span, C), F32),
                VMEM((C, BQ), F32),
                VMEM((HL * BQ, C), BF16),
                VMEM((HL * BQ, C), BF16),
                VMEM((span, HL * BQ), BF16),
                VMEM((span, HL * BQ), BF16),
                VMEM((3, D, C), F32),
            ],
        ),
        out_shape=[
            jax.ShapeDtypeStruct((3, D, C), BF16),
            jax.ShapeDtypeStruct((1, 2 * C), F32),
            jax.ShapeDtypeStruct((span // 2, D), F32),
            jax.ShapeDtypeStruct((span // 2, D), BF16),
        ],
        name="attend_backward",
    )(bounds, me, slots, x_all, q, k, v, g, out, lse, wq, wk, wv, res)


def arrange_kernel(groups, route_ref, x_ref, o_ref, slot_ref):
    for k in range(groups):
        packed = route_ref[k]
        group = packed // (2 * groups)
        o_ref[group] = x_ref[k]
        slot_ref[group] = jnp.full(slot_ref.shape[1:], packed % groups, jnp.int32)


def arrange(pieces, route):
    groups, piece, _ = pieces.shape
    return pl.pallas_call(
        functools.partial(arrange_kernel, groups),
        grid_spec=pltpu.PrefetchScalarGridSpec(
            num_scalar_prefetch=1,
            grid=(1,),
            in_specs=[pl.BlockSpec(pieces.shape, lambda i, r: (0, 0, 0))],
            out_specs=[
                pl.BlockSpec(pieces.shape, lambda i, r: (0, 0, 0)),
                pl.BlockSpec((groups, 8, 128), lambda i, r: (0, 0, 0)),
            ],
        ),
        out_shape=[
            jax.ShapeDtypeStruct(pieces.shape, BF16),
            jax.ShapeDtypeStruct((groups, 8, 128), jnp.int32),
        ],
        name="arrange",
    )(route, pieces)


def restore_kernel(groups, route_ref, x_ref, o_ref):
    for k in range(groups):
        o_ref[k] = x_ref[route_ref[k] // (2 * groups)]


def restore(pieces, route):
    spec = pl.BlockSpec(pieces.shape, lambda i, r: (0, 0, 0))
    return pl.pallas_call(
        functools.partial(restore_kernel, pieces.shape[0]),
        grid_spec=pltpu.PrefetchScalarGridSpec(
            num_scalar_prefetch=1, grid=(1,), in_specs=[spec], out_specs=spec
        ),
        out_shape=jax.ShapeDtypeStruct(pieces.shape, BF16),
        name="restore",
    )(route, pieces)


def far_first(n):
    return sorted(range(1, n), key=lambda k: abs(k - n // 2))


def dispatch_kernel(n, x_ref, slot_ref, o_ref, slots_ref, send, recv, ssend, srecv, fsend, frecv):
    dp, me = lax.axis_index("dp"), lax.axis_index("seq")
    partner = (dp, 1 - me)
    barrier = pltpu.get_barrier_semaphore()
    for k in range(1, n):
        pl.semaphore_signal(barrier, inc=1, device_id=((dp + k) % n, me), device_id_type=MESH)
    pl.semaphore_signal(barrier, inc=1, device_id=partner, device_id_type=MESH)
    pl.semaphore_wait(barrier, n)

    def push(src, dst, s, r, device):
        return pltpu.make_async_remote_copy(
            src_ref=src, dst_ref=dst, send_sem=s, recv_sem=r,
            device_id=device, device_id_type=MESH,
        )

    order = far_first(n)
    copies, small = {}, {}
    for k in order:
        p = (dp + k) % n
        copies[k] = push(x_ref.at[p], o_ref.at[me, dp], send.at[k], recv.at[k], (p, me))
        copies[k].start()
        small[k] = push(slot_ref.at[p], slots_ref.at[me, dp], ssend.at[k], srecv.at[k], (p, me))
        small[k].start()
    forwards = [push(x_ref.at[dp], o_ref.at[me, dp], fsend.at[0], frecv.at[0], partner)]
    forwards[0].start()
    o_ref[me, dp] = x_ref[dp]
    slots_ref[me, dp] = slot_ref[dp]
    for k in order:
        s = (dp + n - k) % n
        copies[k].wait_recv()
        forward = push(o_ref.at[me, s], o_ref.at[me, s], fsend.at[k], frecv.at[k], partner)
        forward.start()
        forwards.append(forward)
    for k in order:
        small[k].wait_recv()
    last = push(slots_ref.at[me], slots_ref.at[me], fsend.at[n], frecv.at[n], partner)
    last.start()
    forwards.append(last)
    for k in order:
        copies[k].wait_send()
        small[k].wait_send()
    for forward in forwards:
        forward.wait()


def dispatch(outgoing, slots, collective_id):
    n = outgoing.shape[0]
    vmem = pl.BlockSpec(memory_space=VMEM)
    return pl.pallas_call(
        functools.partial(dispatch_kernel, n),
        out_shape=[
            jax.ShapeDtypeStruct((2,) + outgoing.shape, BF16),
            jax.ShapeDtypeStruct((2,) + slots.shape, jnp.int32),
        ],
        in_specs=[vmem] * 2,
        out_specs=[vmem] * 2,
        scratch_shapes=[pltpu.SemaphoreType.DMA((n,))] * 4 + [pltpu.SemaphoreType.DMA((n + 1,))] * 2,
        compiler_params=pltpu.CompilerParams(collective_id=collective_id, has_side_effects=True),
        name="dispatch",
    )(outgoing, slots)


class Chunk:
    def __init__(self, env, number, source, full, acc, landing, shared):
        self.env, self.number, self.shared = env, number, shared
        self.source, self.full, self.acc, self.landing = source, full, acc, landing
        self.base, self.size, self.offset, self.stage = 0, source.shape[0], 0, 0
        self.from_source, self.kept, self.copies = True, [], []

    def push(self, src, dst, device):
        e = self.env
        copy = pltpu.make_async_remote_copy(
            src_ref=src, dst_ref=dst,
            send_sem=e["send"].at[self.number, self.stage],
            recv_sem=e["recv"].at[self.number, self.stage],
            device_id=device, device_id_type=MESH,
        )
        copy.start()
        self.stage += 1
        self.copies.append(copy)

    def at(self, ref, start, size):
        return ref.at[pl.ds(start if isinstance(start, int) else pl.multiple_of(start, 16), size), :]

    def halve(self, peer):
        device, bit = peer
        half = self.size // 2
        keep, give = self.base + bit * half, self.base + (1 - bit) * half
        src = self.source if self.from_source else self.acc
        self.push(self.at(src, give, half), self.at(self.landing, self.offset, half), device)
        self.kept.append((keep, half, device))

    def finish_half(self):
        for copy in self.copies:
            copy.wait()
        self.copies = []
        keep, half, _ = self.kept[-1]
        src = self.source if self.from_source else self.acc
        step = min(half, 64)
        base, offset = keep, self.offset

        def add(i, _):
            here = pl.ds(pl.multiple_of(base + i * step, 16), step)
            there = pl.ds(pl.multiple_of(offset + i * step, 16), step)
            total = src[here, :].astype(F32) + self.landing[there, :].astype(F32)
            self.acc[here, :] = total.astype(BF16)
            return 0

        lax.fori_loop(0, half // step, add, 0)
        self.base, self.size, self.offset = keep, half, offset + half
        self.from_source = False

    def quarter(self):
        e = self.env
        q = self.size // 4
        for k in range(1, 4):
            z = (e["z"] + k) % 4
            self.push(
                self.at(self.acc, self.base + z * q, q),
                self.at(self.landing, self.offset + (k - 1) * q, q),
                ((e["dp"] + 4 * k) % 16, e["me"]),
            )

    def finish_quarter(self):
        for copy in self.copies:
            copy.wait()
        self.copies = []
        q = self.size // 4
        here = pl.ds(pl.multiple_of(self.base + self.env["z"] * q, 16), q)
        total = self.acc[here, :].astype(F32)
        for k in range(3):
            total += self.landing[self.offset + k * q : self.offset + (k + 1) * q, :].astype(F32)
        self.full[here, :] = total.astype(BF16)
        region = self.at(self.full, self.base + self.env["z"] * q, q)
        for k in range(1, 4):
            self.push(region, region, ((self.env["dp"] + 4 * k) % 16, self.env["me"]))

    def spread(self):
        for copy in self.copies:
            copy.wait()
        self.copies = []
        keep, half, device = self.kept.pop()
        region = self.at(self.full, keep, half)
        self.push(region, region, device)

    def hand_over(self):
        for copy in self.copies:
            copy.wait()
        self.copies = []
        self.push(self.full, self.full, (self.env["dp"], 1 - self.env["me"]))

    def close(self):
        for copy in self.copies:
            copy.wait()

    def steps(self):
        e = self.env
        first, second = e["axes"]
        line = []
        if self.shared:
            line.append(lambda: self.halve(((e["dp"], 1 - e["me"]), e["me"])))
            line.append(lambda: (self.finish_half(), self.halve(first)))
        else:
            line.append(lambda: self.halve(first))
        line.append(lambda: (self.finish_half(), self.halve(second)))
        line.append(lambda: (self.finish_half(), self.quarter()))
        line.append(self.finish_quarter)
        line += [self.spread] * (3 if self.shared else 2)
        if not self.shared:
            line.append(self.hand_over)
        line.append(self.close)
        return line


def final_kernel(
    ga_ref, gb_ref, up_ref, down_ref, out_ref, qkv_ref, vec_ref,
    back_ref, up_full, down_full, out_full, qkv_full, vec_full,
    ret_ref, gbr_ref, acc_ref, landing_ref, acc_own, landing_own, vec_recv,
    send, recv, asend, arecv, gsend, grecv, vsend, vrecv,
):
    n = 16
    dp, me = lax.axis_index("dp"), lax.axis_index("seq")
    rows = ga_ref.shape[0]
    piece = rows // n
    partner = (dp, 1 - me)
    wa, wb = 1 + me, 2 - me
    bit_a, bit_b = (dp // wa) % 2, (dp // wb) % 2
    env = {
        "dp": dp,
        "me": me,
        "z": dp // 4,
        "axes": (
            ((dp + (1 - 2 * bit_a) * wa, me), bit_a),
            ((dp + (1 - 2 * bit_b) * wb, me), bit_b),
        ),
        "send": send,
        "recv": recv,
    }
    barrier = pltpu.get_barrier_semaphore()
    for k in range(1, n):
        pl.semaphore_signal(barrier, inc=1, device_id=((dp + k) % n, me), device_id_type=MESH)
    pl.semaphore_signal(barrier, inc=1, device_id=partner, device_id_type=MESH)
    pl.semaphore_wait(barrier, n)

    def push(src, dst, s, r, device):
        return pltpu.make_async_remote_copy(
            src_ref=src, dst_ref=dst, send_sem=s, recv_sem=r,
            device_id=device, device_id_type=MESH,
        )

    quarter = rows // 4
    halves = []
    for j in range(4):
        part = pl.ds(j * quarter, quarter)
        copy = push(gb_ref.at[part, :], gbr_ref.at[part, :], gsend.at[j], grecv.at[j], partner)
        copy.start()
        halves.append(copy)

    chunks = []
    for c in range(4):
        lanes = pl.ds(c * D, D)
        chunks.append((up_ref.at[:, lanes], up_full.at[:, lanes], True))
    for c in range(4):
        part = pl.ds(c * D, D)
        chunks.append((down_ref.at[part, :], down_full.at[part, :], True))
    chunks.append((out_ref, out_full, True))
    for c in range(3):
        chunks.append((qkv_ref.at[c], qkv_full.at[me, c], False))
    lines = []
    counts = {True: 0, False: 0}
    for number, (source, full, shared) in enumerate(chunks):
        i = counts[shared]
        counts[shared] += 1
        acc = (acc_ref if shared else acc_own).at[i]
        landing = (landing_ref if shared else landing_own).at[i]
        lines.append(Chunk(env, number, source, full, acc, landing, shared).steps())
    peers = [partner]
    for w, size in ((1, 2), (2, 2), (4, 2), (8, 2)):
        bit = (dp // w) % 2
        peers.append((dp + (1 - 2 * bit) * w, me))
    vec_copies = []

    def vec_step(s):
        if s == 0:
            vec_full[...] = vec_ref[...]
        else:
            vec_copies[-1].wait()
            vec_full[...] += vec_recv[s - 1]
        if s < len(peers):
            sent = vec_recv.at[len(peers) + s]
            sent[...] = vec_full[...]
            copy = push(sent, vec_recv.at[s], vsend.at[s], vrecv.at[s], peers[s])
            copy.start()
            vec_copies.append(copy)

    lines.append([functools.partial(vec_step, s) for s in range(len(peers) + 1)])

    returns = []

    def give_back():
        for j in range(4):
            halves[j].wait()

            def add(i, _, j=j):
                here = pl.ds(pl.multiple_of(j * quarter + i * 64, 64), 64)
                ret_ref[here, :] = (ga_ref[here, :] + gbr_ref[here, :].astype(F32)).astype(BF16)
                return 0

            lax.fori_loop(0, quarter // 64, add, 0)
        mine = pl.ds(pl.multiple_of(dp * piece, piece), piece)
        for k in far_first(n):
            p = (dp + k) % n
            theirs = pl.ds(pl.multiple_of(p * piece, piece), piece)
            copy = push(
                ret_ref.at[theirs, :], back_ref.at[mine, :], asend.at[k], arecv.at[k], (p, me)
            )
            copy.start()
            returns.append(copy)
        back_ref[mine, :] = ret_ref[mine, :]

    ticks = max(len(line) + at for at, line in enumerate(lines))
    for t in range(ticks):
        for at, line in enumerate(lines):
            if 0 <= t - at < len(line):
                line[t - at]()
        if t == 0:
            give_back()
    for copy in returns:
        copy.wait()


def give_back_and_sum(ga, gb, up, down, out, qkv, vec, collective_id):
    vmem = pl.BlockSpec(memory_space=VMEM)
    shape = jax.ShapeDtypeStruct
    dma = pltpu.SemaphoreType.DMA
    return pl.pallas_call(
        final_kernel,
        out_shape=[
            shape(gb.shape, BF16),
            shape(up.shape, BF16),
            shape(down.shape, BF16),
            shape(out.shape, BF16),
            shape((2,) + qkv.shape, BF16),
            shape(vec.shape, F32),
        ],
        in_specs=[vmem] * 7,
        out_specs=[vmem] * 6,
        scratch_shapes=[
            VMEM(gb.shape, BF16),
            VMEM(gb.shape, BF16),
            VMEM((9, D, D), BF16),
            VMEM((9, D, D), BF16),
            VMEM((3, D, C), BF16),
            VMEM((3, D, C), BF16),
            VMEM((10,) + vec.shape, F32),
            dma((12, 12)), dma((12, 12)),
            dma((16,)), dma((16,)),
            dma((4,)), dma((4,)),
            dma((5,)), dma((5,)),
        ],
        compiler_params=pltpu.CompilerParams(
            collective_id=collective_id, has_side_effects=True, vmem_limit_bytes=62 << 20
        ),
        name="give_back_and_sum",
    )(ga, gb, up, down, out, qkv, vec)


def body(
    tokens,
    route,
    lengths,
    query_weight,
    query_bias,
    key_weight,
    value_weight,
    value_bias,
    output_weight,
    output_bias,
    first_gain,
    first_shift,
    up_weight,
    up_bias,
    down_weight,
    down_bias,
    second_gain,
    second_shift,
    cotangent,
):
    groups = lax.axis_size("dp")
    rows = tokens.shape[0]
    piece = rows // groups
    span = rows * lax.axis_size("seq")
    seq = lax.axis_index("seq")
    bounds = jnp.cumsum(lengths[0]).astype(jnp.int32)
    me = seq.reshape(1).astype(jnp.int32)
    kernels = groups == 16 and piece % 16 == 0
    if kernels:
        pieces = 2 * groups
        outgoing, slots_out = arrange(tokens.reshape(groups, piece, D), route)
        x_all, slots_all = dispatch(outgoing, slots_out, 0)
        x_all = x_all.reshape(span, D)
        slots = slots_all[:, :, 0, 0].reshape(pieces)
    else:
        pieces = 0
        target = route // groups // lax.axis_size("seq")
        place = route % groups
        outgoing = jnp.zeros((groups, piece, D), BF16).at[target].set(tokens.reshape(groups, piece, D))
        slots_out = jnp.zeros((groups,), jnp.int32).at[target].set(place)
        incoming, slots = (
            lax.all_to_all(outgoing, "dp", split_axis=0, concat_axis=0, tiled=True),
            lax.all_to_all(slots_out, "dp", split_axis=0, concat_axis=0, tiled=True),
        )
        inputs = jnp.zeros_like(incoming).at[slots].set(incoming).reshape(rows, D)
        x_all = swap(inputs, 0).reshape(span, D)
    q, k, v, mixed_all, attend_out, lse, inputs = attend_forward(
        x_all, pieces, bounds, me, slots,
        query_weight, key_weight, value_weight, query_bias, value_bias,
    )
    mixed_halves = swap(mixed_all.reshape(2, rows, C), 1)
    mixed = jnp.concatenate([mixed_halves[0], mixed_halves[1]], axis=1)
    branch = product(mixed, output_weight) + output_bias
    residual = inputs.astype(F32) + branch
    first, first_back = jax.vjp(
        norm_rows, residual, first_gain.astype(F32), first_shift.astype(F32)
    )
    first_low = first.astype(BF16)
    hidden = product(first_low, up_weight) + up_bias
    active = gelu_exact(hidden).astype(BF16)
    update = product(active, down_weight) + down_bias
    layer_out, second_back = jax.vjp(
        norm_rows, first + update, second_gain.astype(F32), second_shift.astype(F32)
    )
    grad_second, grad_second_gain, grad_second_shift = second_back(cotangent.astype(F32))
    grad_update = grad_second.astype(BF16)
    again = product(first_low, up_weight) + up_bias
    active_again, gelu_back = jax.vjp(gelu_exact, again)
    active_low = active_again.astype(BF16)
    grad_down = product_left(active_low, grad_update)
    grad_down_bias = column_sums(grad_update)
    (grad_active,) = gelu_back(product_right(grad_update, down_weight))
    grad_hidden = grad_active.astype(BF16)
    grad_up = product_left(first_low, grad_hidden)
    grad_up_bias = column_sums(grad_hidden)
    grad_first = grad_second + product_right(grad_hidden, up_weight)
    grad_residual, grad_first_gain, grad_first_shift = first_back(grad_first)
    grad_branch = grad_residual.astype(BF16)
    grad_output = product_left(mixed, grad_branch)
    grad_output_bias = column_sums(grad_branch)
    grad_mixed = product_right(grad_branch, output_weight).astype(BF16)
    grad_halves = jnp.stack([grad_mixed[:, :C], grad_mixed[:, C:]])
    grad_mixed_all = swap(grad_halves, 2).reshape(span, C)
    grad_columns, column_parts, grad_own, grad_other = attend_backward(
        bounds, me, slots, pieces, x_all, q, k, v, grad_mixed_all, attend_out, lse,
        query_weight, key_weight, value_weight, grad_residual,
    )

    def own_columns(part):
        return lax.dynamic_update_slice(jnp.zeros((1, D), F32), part, (0, seq * C))

    vec = jnp.concatenate(
        [
            own_columns(column_parts[:, :C]),
            own_columns(column_parts[:, C:]),
            jnp.stack(
                [
                    grad_output_bias,
                    grad_first_gain,
                    grad_first_shift,
                    grad_down_bias,
                    grad_second_gain,
                    grad_second_shift,
                ]
            ),
            grad_up_bias.reshape(-1, D),
            jnp.zeros((4, D), F32),
        ]
    )
    if kernels:
        back, up_sum, down_sum, out_sum, columns, vec = give_back_and_sum(
            grad_own, grad_other,
            grad_up.astype(BF16), grad_down.astype(BF16), grad_output.astype(BF16),
            grad_columns, vec, 4,
        )
        token_grad = restore(back.reshape(groups, piece, D), route).reshape(rows, D)
        up_sum, down_sum, out_sum = (a.astype(F32) for a in (up_sum, down_sum, out_sum))
        columns = jnp.concatenate([columns[0], columns[1]], axis=2).astype(F32)
    else:
        grad_inputs = grad_own + swap(jnp.stack([grad_other, grad_other]), 3)[1 - seq].astype(F32)
        back_rows = grad_inputs.astype(BF16).reshape(groups, piece, D)[slots]
        returned = lax.all_to_all(back_rows, "dp", split_axis=0, concat_axis=0, tiled=True)
        token_grad = returned[target].reshape(rows, D)
        up_sum, down_sum, out_sum, vec = lax.psum((grad_up, grad_down, grad_output, vec), ("dp", "seq"))
        columns = lax.psum(grad_columns.astype(F32), "dp")
        columns = lax.all_gather(columns, "seq", axis=2, tiled=True)
    query_sum, key_sum, value_sum = columns[0], columns[1], columns[2]
    return (
        layer_out.astype(BF16),
        token_grad,
        query_sum,
        vec[0],
        key_sum,
        value_sum,
        vec[1],
        out_sum,
        vec[2],
        vec[3],
        vec[4],
        up_sum,
        vec[8:12].reshape(-1),
        down_sum,
        vec[5],
        vec[6],
        vec[7],
    )


def solution(mesh):
    both, one = P(("dp", "seq"), None), P()
    return jax.shard_map(
        body,
        mesh=mesh,
        in_specs=(both, P(("dp", "seq")), P("dp", None)) + (one,) * 15 + (both,),
        out_specs=(both, both) + (one,) * 15,
        check_vma=False,
    )
```

```python
import functools

import jax
import jax.numpy as jnp
from jax import lax
from jax.experimental import pallas as pl
from jax.experimental.pallas import tpu as pltpu
from jax.sharding import PartitionSpec as P

D = 512
HEADS = 8
HEAD = 64
HL = HEADS // 2
C = HL * HEAD
PAIR = 128
NEG = -1e30
LOG2E = 1.4426950408889634
BQ = 256
BK = 256
F32 = jnp.float32
BF16 = jnp.bfloat16
MESH = pl.DeviceIdType.MESH
VMEM = pltpu.VMEM
SMEM = pltpu.SMEM


def norm_rows(value, gain, shift):
    center = value - jnp.mean(value, axis=-1, keepdims=True)
    spread = jnp.mean(center * center, axis=-1, keepdims=True)
    return center * lax.rsqrt(spread + 1e-05) * gain + shift


def gelu_exact(value):
    return jax.nn.gelu(value, approximate=False)


def product(left, right):
    return jnp.dot(left, right, preferred_element_type=F32)


def product_left(left, right):
    return lax.dot_general(left, right, (((0,), (0,)), ((), ())), preferred_element_type=F32)


def product_right(left, right):
    return lax.dot_general(left, right, (((1,), (1,)), ((), ())), preferred_element_type=F32)


def column_sums(value):
    return jnp.sum(value.astype(F32), axis=0)


def swap_kernel(x_ref, o_ref, send, recv, local):
    dp, me = lax.axis_index("dp"), lax.axis_index("seq")
    other = 1 - me
    barrier = pltpu.get_barrier_semaphore()
    pl.semaphore_signal(barrier, inc=1, device_id=(dp, other), device_id_type=MESH)
    pl.semaphore_wait(barrier, 1)
    whole = len(x_ref.shape) == 2
    copy = pltpu.make_async_remote_copy(
        src_ref=x_ref if whole else x_ref.at[other],
        dst_ref=o_ref.at[me],
        send_sem=send,
        recv_sem=recv,
        device_id=(dp, other),
        device_id_type=MESH,
    )
    copy.start()
    own = pltpu.make_async_copy(x_ref if whole else x_ref.at[me], o_ref.at[me], local)
    own.start()
    own.wait()
    copy.wait()


def swap(x, collective_id):
    shape = x.shape if x.ndim == 3 else (2,) + x.shape
    return pl.pallas_call(
        swap_kernel,
        out_shape=jax.ShapeDtypeStruct(shape, x.dtype),
        in_specs=[pl.BlockSpec(memory_space=VMEM)],
        out_specs=pl.BlockSpec(memory_space=VMEM),
        scratch_shapes=[pltpu.SemaphoreType.DMA] * 3,
        compiler_params=pltpu.CompilerParams(collective_id=collective_id, has_side_effects=True),
    )(x)


def rotation(len_ref, span):
    lengths = [len_ref[j] for j in range(len_ref.shape[0])]
    longest = functools.reduce(jnp.maximum, lengths)
    shift, total, ends = jnp.int32(0), jnp.int32(0), []
    for length in lengths:
        shift = jnp.where(length == longest, total, shift)
        total = total + length
        ends.append(total)
    turned = [e - shift for e in ends]
    return shift, [jnp.where(e <= 0, e + span, e) for e in turned]


def rows_from(ref, start, count):
    base = lax.div(start, 8) * 8
    r = start - base
    x = ref[pl.ds(base, count + 8), :]
    width = x.shape[1]
    row = lax.broadcasted_iota(jnp.int32, (1, 8, 1), 1)
    for bit in (1, 2, 4):
        by_eights = x.reshape(x.shape[0] // 8, 8, width)
        turned = pltpu.roll(by_eights, 8 - bit, axis=1)
        following = jnp.concatenate([turned[1:], turned[:1]], axis=0)
        moved = jnp.where(row < 8 - bit, turned, following).reshape(x.shape)
        x = jnp.where(jnp.full(x.shape, r & bit) != 0, moved, x)
    return x[:count]


def table_of(ends, position):
    start, end = jnp.zeros_like(position), jnp.full_like(position, 1 << 30)
    for e in ends:
        start = jnp.where(e <= position, jnp.maximum(start, e), start)
        end = jnp.where(e > position, jnp.minimum(end, e), end)
    return start, end


def tile_mask(ends, i):
    return table_of(ends, i * BQ + lax.broadcasted_iota(jnp.int32, (1, BQ), 1))


def head_masks():
    lane = lax.broadcasted_iota(jnp.int32, (1, PAIR), 1)
    low = (lane < HEAD).astype(F32).astype(BF16)
    return low, (lane >= HEAD).astype(F32).astype(BF16)


def by_eight(value, op):
    return op(value.reshape(value.shape[0] // 8, 8, value.shape[1]), axis=0)


def forward_kernel(
    pieces, len_ref, me_ref, slot_ref, loaded_ref, wq_ref, wk_ref, wv_ref, bq_ref, bv_ref,
    x_ref, q_ref, k_ref, v_ref, mixed_ref, out_ref, lse_ref, own_ref,
    vt_ref, acc_ref, s_ref, packed_ref, turned_ref,
):
    span = loaded_ref.shape[0]
    half, blocks = span // 2, span // BQ
    near = blocks // 2
    shift, ends = rotation(len_ref, span)
    count = pieces if pieces else 32
    piece = span // count

    def place(k, _):
        slot = slot_ref[k] if pieces else k % (count // 2)
        row = (k // (count // 2)) * half + slot * piece
        packed_ref[pl.ds(pl.multiple_of(row, piece), piece), :] = loaded_ref[
            pl.ds(pl.multiple_of(k * piece, piece), piece), :
        ].astype(F32)
        return 0

    lax.fori_loop(0, count, place, 0)
    packed_ref[span:, :] = packed_ref[: BQ + 8, :]
    own_ref[...] = packed_ref[pl.ds(pl.multiple_of(me_ref[0] * half, half), half), :].astype(BF16)

    def project(i, _):
        rows = pl.ds(pl.multiple_of(i * BQ, BQ), BQ)
        x = rows_from(packed_ref, lax.rem(i * BQ + shift, span), BQ).astype(BF16)
        x_ref[rows, :] = x
        q = (product(x, wq_ref[...]) + bq_ref[...].astype(F32)).astype(BF16)
        q_ref[rows, :] = (q.astype(F32) * (HEAD**-0.5)).astype(BF16)
        k_ref[rows, :] = product(x, wk_ref[...]).astype(BF16)
        v = (product(x, wv_ref[...]) + bv_ref[...].astype(F32)).astype(BF16)
        v_ref[rows, :] = v
        vt_ref[:, rows] = v.T
        return 0

    lax.fori_loop(0, blocks, project, 0)
    masks = head_masks()

    def query_block(masked, i, _):
        rows = pl.ds(pl.multiple_of(i * BQ, BQ), BQ)
        base = near if masked else 0
        if masked:
            start, end = tile_mask(ends, i)
        q = q_ref[rows, :]
        heads = [q[:, (h // 2) * PAIR : (h // 2 + 1) * PAIR] * masks[h % 2] for h in range(HL)]
        acc_ref[...] = jnp.zeros_like(acc_ref)

        def score_block(j, tops):
            keys = pl.ds(pl.multiple_of((base + j) * BK, BK), BK)
            if masked:
                kpos = (base + j) * BK + lax.broadcasted_iota(jnp.int32, (BK, BQ), 0)
                mask = (kpos >= start) & (kpos < end)
            new = []
            for h in range(HL):
                kp = k_ref[keys, (h // 2) * PAIR : (h // 2 + 1) * PAIR]
                s = product_right(kp, heads[h]) * LOG2E
                if masked:
                    s = jnp.where(mask, s, NEG)
                s_ref[h, pl.ds(pl.multiple_of(j * BK, BK), BK), :] = s
                new.append(jnp.maximum(tops[h], by_eight(s, jnp.max)))
            return tuple(new)

        tops = lax.fori_loop(
            0, near, score_block, tuple(jnp.full((8, BQ), NEG, F32) for _ in range(HL))
        )
        tops = [jnp.max(t, axis=0, keepdims=True) for t in tops]

        def mix_block(j, totals):
            keys = pl.ds(pl.multiple_of((base + j) * BK, BK), BK)
            new = []
            for h in range(HL):
                p = jnp.exp2(s_ref[h, pl.ds(pl.multiple_of(j * BK, BK), BK), :] - tops[h])
                new.append(totals[h] + by_eight(p, jnp.sum))
                lanes = slice(h * HEAD, (h + 1) * HEAD)
                acc_ref[lanes, :] += product(vt_ref[lanes, keys], p.astype(BF16))
            return tuple(new)

        totals = lax.fori_loop(
            0, near, mix_block, tuple(jnp.zeros((8, BQ), F32) for _ in range(HL))
        )
        for h in range(HL):
            total = jnp.sum(totals[h], axis=0, keepdims=True)
            lanes = slice(h * HEAD, (h + 1) * HEAD)
            acc_ref[lanes, :] = acc_ref[lanes, :] / total
            lse_ref[h : h + 1, rows] = tops[h] + jnp.log2(total)
        out = acc_ref[...]
        out_ref[:, rows] = out
        turned_ref[rows, :] = out.T
        return 0

    lax.fori_loop(0, near, functools.partial(query_block, False), 0)
    lax.fori_loop(near, blocks, functools.partial(query_block, True), 0)
    turned_ref[span:, :] = turned_ref[: BQ + 8, :]

    def turn_back(i, _):
        rows = pl.ds(pl.multiple_of(i * BQ, BQ), BQ)
        mixed_ref[rows, :] = rows_from(turned_ref, lax.rem(i * BQ + span - shift, span), BQ).astype(BF16)
        return 0

    lax.fori_loop(0, blocks, turn_back, 0)


def column_block(shape):
    return pl.BlockSpec(shape, lambda i, lengths, me, slots: (0, me[0]))


def whole_block(shape):
    return pl.BlockSpec(shape, lambda i, lengths, me, slots: (0,) * len(shape))


def attend_forward(x_all, pieces, lengths, me, slots, wq, wk, wv, bq, bv):
    span = x_all.shape[0]
    rows_shape = jax.ShapeDtypeStruct((span, C), BF16)
    return pl.pallas_call(
        functools.partial(forward_kernel, pieces),
        grid_spec=pltpu.PrefetchScalarGridSpec(
            num_scalar_prefetch=3,
            grid=(1,),
            in_specs=[
                whole_block((span, D)),
                column_block((D, C)),
                column_block((D, C)),
                column_block((D, C)),
                column_block((1, C)),
                column_block((1, C)),
            ],
            out_specs=[whole_block((span, D))] + [whole_block((span, C))] * 4
            + [whole_block((C, span)), whole_block((8, span)), whole_block((span // 2, D))],
            scratch_shapes=[
                VMEM((C, span), BF16),
                VMEM((C, BQ), F32),
                VMEM((HL, span // 2, BQ), F32),
                VMEM((span + BQ + 8, D), F32),
                VMEM((span + BQ + 8, C), F32),
            ],
        ),
        out_shape=[jax.ShapeDtypeStruct((span, D), BF16)] + [rows_shape] * 4
        + [jax.ShapeDtypeStruct((C, span), F32), jax.ShapeDtypeStruct((8, span), F32)]
        + [jax.ShapeDtypeStruct((span // 2, D), BF16)],
        name="attend_forward",
    )(lengths, me, slots, x_all, wq, wk, wv, bq.reshape(1, D), bv.reshape(1, D))


def backward_kernel(pieces, sums, *refs):
    len_ref, slot_ref, x_ref, q_ref, k_ref, v_ref, g_ref, out_ref, lse_ref = refs[:9]
    weights, res_ref = refs[9:12], refs[12]
    refs = refs[13:]
    if sums:
        raw, refs = refs[:3], refs[3:]
    gw_ref, sums_ref, ga_ref, gb_ref = refs[:4]
    refs = refs[4:]
    if sums:
        full, refs = refs[:3], refs[3:]
    kt_ref, gq_ref, gk_ref, gv_ref, gqt_ref, qs_ref, gs_ref, w_ref, ds_ref = refs[:9]
    term_ref, turned_ref, gx_ref = refs[9:12]
    me = lax.axis_index("seq")
    span = x_ref.shape[0]
    half, blocks = span // 2, span // BQ
    near = blocks // 2
    scale = HEAD**-0.5
    ticks = []
    if sums:
        acc_ref, landing_ref, send, recv = refs[12:]
        env = chip_links(send, recv)
        meet([env["partner"]] + [peer for peer, _ in env["axes"]] + env["stack"])
        lines = [
            Chunk(env, c, source, target, acc_ref.at[c], landing_ref.at[c], True).steps()
            for c, (source, target) in enumerate(square_blocks(raw, full))
        ]
        for c, line in enumerate(lines):
            for j, step in enumerate(line):
                at = c + 2 * j
                ticks += [[] for _ in range(at + 1 - len(ticks))]
                ticks[at].append(step)

    def tick(now, candidates):
        for t in candidates:
            if t < len(ticks):

                @pl.when(now == t)
                def _(t=t):
                    for step in ticks[t]:
                        step()

    def straight(candidates):
        for t in candidates:
            if t < len(ticks):
                for step in ticks[t]:
                    step()

    straight([0])
    shift, ends = rotation(len_ref, span)

    def prepare(i, _):
        rows = pl.ds(pl.multiple_of(i * BQ, BQ), BQ)
        kt_ref[:, rows] = k_ref[rows, :].T
        gk_ref[rows, :] = jnp.zeros((BQ, C), F32)
        gv_ref[rows, :] = jnp.zeros((BQ, C), F32)
        turned_ref[rows, :] = g_ref[rows, :].astype(F32)
        return 0

    lax.fori_loop(0, blocks, prepare, 0)
    turned_ref[span:, :] = turned_ref[: BQ + 8, :]
    straight([1])
    lane = lax.broadcasted_iota(jnp.int32, (1, C), 1) // HEAD
    masks = [(lane == h).astype(F32).astype(BF16) for h in range(HL)]

    def query_block(masked, i, _):
        rows = pl.ds(pl.multiple_of(i * BQ, BQ), BQ)
        base = near if masked else 0
        if masked:
            start, end = tile_mask(ends, i)
        q = q_ref[rows, :]
        exact = rows_from(turned_ref, lax.rem(i * BQ + shift, span), BQ)
        g = exact.astype(BF16)
        for h in range(HL):
            part = slice(h * BQ, (h + 1) * BQ)
            qs_ref[part, :] = q * masks[h]
            gs_ref[part, :] = g * masks[h]
        weighted = exact.T * out_ref[:, rows]
        inner = [
            jnp.sum(weighted[h * HEAD : (h + 1) * HEAD], axis=0, keepdims=True) for h in range(HL)
        ]
        logsum = [lse_ref[h : h + 1, rows] for h in range(HL)]
        gqt_ref[...] = jnp.zeros_like(gqt_ref)

        def key_block(j, _):
            keys = pl.ds(pl.multiple_of((base + j) * BK, BK), BK)
            here = pl.ds(pl.multiple_of(j * BK, BK), BK)
            if masked:
                kpos = (base + j) * BK + lax.broadcasted_iota(jnp.int32, (BK, BQ), 0)
                mask = (kpos >= start) & (kpos < end)
            for h in range(HL):
                part = slice(h * BQ, (h + 1) * BQ)
                pair = slice((h // 2) * PAIR, (h // 2 + 1) * PAIR)
                s = product_right(k_ref[keys, pair], qs_ref[part, pair])
                w = jnp.exp2(s * LOG2E - logsum[h])
                if masked:
                    w = jnp.where(mask, w, 0.0)
                gw = product_right(v_ref[keys, pair], gs_ref[part, pair])
                gs = (w * (gw - inner[h])).astype(BF16)
                w_ref[here, part] = w.astype(BF16)
                ds_ref[here, part] = gs
            return 0

        def product_block(j, _):
            keys = pl.ds(pl.multiple_of((base + j) * BK, BK), BK)
            here = pl.ds(pl.multiple_of(j * BK, BK), BK)
            for h in range(HL):
                part = slice(h * BQ, (h + 1) * BQ)
                lanes = slice(h * HEAD, (h + 1) * HEAD)
                gqt_ref[lanes, :] += product(kt_ref[lanes, keys], ds_ref[here, part])
            gv_ref[keys, :] += product(w_ref[here, :], gs_ref[...])
            gk_ref[keys, :] += product(ds_ref[here, :], qs_ref[...])
            return 0

        first = 2 + 2 * base
        lax.fori_loop(0, near, key_block, 0)
        tick(2 + 2 * i, range(first, first + 2 * near, 2))
        lax.fori_loop(0, near, product_block, 0)
        gq_ref[rows, :] = (gqt_ref[...].T * scale).astype(BF16)
        tick(3 + 2 * i, range(first + 1, first + 2 * near, 2))
        return 0

    lax.fori_loop(0, near, functools.partial(query_block, False), 0)
    lax.fori_loop(near, blocks, functools.partial(query_block, True), 0)

    columns = pl.ds(pl.multiple_of(me * C, C), C)
    after = 2 + 2 * blocks
    term_ref[...] = jnp.zeros_like(term_ref)
    sums_ref[...] = jnp.zeros_like(sums_ref)

    def gradients(i, _):
        rows = pl.ds(pl.multiple_of(i * BQ, BQ), BQ)
        parts = [gq_ref[rows, :], gk_ref[rows, :].astype(BF16), gv_ref[rows, :].astype(BF16)]
        x = x_ref[rows, :]
        for n, part in enumerate(parts):
            term_ref[n] += product_left(x, part)
        sums_ref[...] += jnp.concatenate(
            [jnp.sum(a.astype(F32), axis=0, keepdims=True) for a in (parts[0], parts[2])], axis=1
        )
        gx_ref[rows, :] = (
            product_right(parts[0], weights[0][:, columns])
            + product_right(parts[1], weights[1][:, columns])
            + product_right(parts[2], weights[2][:, columns])
        )
        tick(after + i, range(after, after + blocks))
        return 0

    lax.fori_loop(0, blocks, gradients, 0)
    gw_ref[...] = term_ref[...].astype(BF16)
    count = pieces if pieces else 32
    each = count // 2
    piece = span // count
    gx_ref[span:, :] = gx_ref[: piece + 8, :]

    def piece_rows(part, k):
        row = (slot_ref[part * each + k] if pieces else k) * piece
        return rows_from(gx_ref, lax.rem(part * half + row + span - shift, span), piece), row

    def own_piece(k, _):
        gx, row = piece_rows(me, k)
        ga_ref[pl.ds(pl.multiple_of(k * piece, piece), piece), :] = (
            gx + res_ref[pl.ds(row, piece), :]
        )
        return 0

    def other_piece(k, _):
        gx, _ = piece_rows(1 - me, k)
        gb_ref[pl.ds(pl.multiple_of(k * piece, piece), piece), :] = gx.astype(BF16)
        return 0

    lax.fori_loop(0, each, own_piece, 0)
    lax.fori_loop(0, each, other_piece, 0)
    straight(range(after + blocks, len(ticks)))


def attend_backward(lengths, slots, pieces, x, q, k, v, g, out, lse, wq, wk, wv, res, raw, collective_id):
    span = x.shape[0]
    vmem, smem = pl.BlockSpec(memory_space=VMEM), pl.BlockSpec(memory_space=SMEM)
    shape = jax.ShapeDtypeStruct
    sums = len(raw) > 0
    chunks = sum(a.size for a in raw) // (D * D)
    dma = pltpu.SemaphoreType.DMA
    comm = [VMEM((chunks, D, D), BF16)] * 2 + [dma((chunks, 12))] * 2 if sums else []
    params = dict(collective_id=collective_id, has_side_effects=True) if sums else {}
    return pl.pallas_call(
        functools.partial(backward_kernel, pieces, sums),
        out_shape=[
            shape((3, D, C), BF16),
            shape((1, 2 * C), F32),
            shape((span // 2, D), F32),
            shape((span // 2, D), BF16),
        ]
        + [shape(a.shape, BF16) for a in raw],
        in_specs=[smem] * 2 + [vmem] * (11 + len(raw)),
        out_specs=[vmem] * (4 + len(raw)),
        scratch_shapes=[
            VMEM((C, span), BF16),
            VMEM((span, C), BF16),
            VMEM((span, C), F32),
            VMEM((span, C), F32),
            VMEM((C, BQ), F32),
            VMEM((HL * BQ, C), BF16),
            VMEM((HL * BQ, C), BF16),
            VMEM((span // 2, HL * BQ), BF16),
            VMEM((span // 2, HL * BQ), BF16),
            VMEM((3, D, C), F32),
            VMEM((span + BQ + 8, C), F32),
            VMEM((span + span // (pieces if pieces else 32) + 8, D), F32),
        ]
        + comm,
        compiler_params=pltpu.CompilerParams(vmem_limit_bytes=63 << 20, **params),
        name="attend_backward",
    )(lengths, slots, x, q, k, v, g, out, lse, wq, wk, wv, res, *raw)


def arrange_kernel(groups, route_ref, x_ref, o_ref, slot_ref):
    for k in range(groups):
        packed = route_ref[k]
        group = packed // (2 * groups)
        o_ref[group] = x_ref[k]
        slot_ref[group] = jnp.full(slot_ref.shape[1:], packed % groups, jnp.int32)


def arrange(pieces, route):
    groups, piece, _ = pieces.shape
    return pl.pallas_call(
        functools.partial(arrange_kernel, groups),
        grid_spec=pltpu.PrefetchScalarGridSpec(
            num_scalar_prefetch=1,
            grid=(1,),
            in_specs=[pl.BlockSpec(pieces.shape, lambda i, r: (0, 0, 0))],
            out_specs=[
                pl.BlockSpec(pieces.shape, lambda i, r: (0, 0, 0)),
                pl.BlockSpec((groups, 8, 128), lambda i, r: (0, 0, 0)),
            ],
        ),
        out_shape=[
            jax.ShapeDtypeStruct(pieces.shape, BF16),
            jax.ShapeDtypeStruct((groups, 8, 128), jnp.int32),
        ],
        name="arrange",
    )(route, pieces)


def restore_kernel(groups, route_ref, x_ref, o_ref):
    for k in range(groups):
        o_ref[k] = x_ref[route_ref[k] // (2 * groups)]


def restore(pieces, route):
    spec = pl.BlockSpec(pieces.shape, lambda i, r: (0, 0, 0))
    return pl.pallas_call(
        functools.partial(restore_kernel, pieces.shape[0]),
        grid_spec=pltpu.PrefetchScalarGridSpec(
            num_scalar_prefetch=1, grid=(1,), in_specs=[spec], out_specs=spec
        ),
        out_shape=jax.ShapeDtypeStruct(pieces.shape, BF16),
        name="restore",
    )(route, pieces)


def far_first(n):
    return sorted(range(1, n), key=lambda k: abs(k - n // 2))


def dispatch_kernel(n, x_ref, slot_ref, o_ref, slots_ref, send, recv, ssend, srecv, fsend, frecv):
    dp, me = lax.axis_index("dp"), lax.axis_index("seq")
    partner = (dp, 1 - me)
    barrier = pltpu.get_barrier_semaphore()
    for k in range(1, n):
        pl.semaphore_signal(barrier, inc=1, device_id=((dp + k) % n, me), device_id_type=MESH)
    pl.semaphore_signal(barrier, inc=1, device_id=partner, device_id_type=MESH)
    pl.semaphore_wait(barrier, n)

    order = far_first(n)
    copies, small = {}, {}
    for k in order:
        p = (dp + k) % n
        copies[k] = push(x_ref.at[p], o_ref.at[me, dp], send.at[k], recv.at[k], (p, me))
        copies[k].start()
        small[k] = push(slot_ref.at[p], slots_ref.at[me, dp], ssend.at[k], srecv.at[k], (p, me))
        small[k].start()
    forwards = [push(x_ref.at[dp], o_ref.at[me, dp], fsend.at[0], frecv.at[0], partner)]
    forwards[0].start()
    o_ref[me, dp] = x_ref[dp]
    slots_ref[me, dp] = slot_ref[dp]
    for k in order:
        s = (dp + n - k) % n
        copies[k].wait_recv()
        forward = push(o_ref.at[me, s], o_ref.at[me, s], fsend.at[k], frecv.at[k], partner)
        forward.start()
        forwards.append(forward)
    for k in order:
        small[k].wait_recv()
    last = push(slots_ref.at[me], slots_ref.at[me], fsend.at[n], frecv.at[n], partner)
    last.start()
    forwards.append(last)
    for k in order:
        copies[k].wait_send()
        small[k].wait_send()
    for forward in forwards:
        forward.wait()


def dispatch(outgoing, slots, collective_id):
    n = outgoing.shape[0]
    vmem = pl.BlockSpec(memory_space=VMEM)
    return pl.pallas_call(
        functools.partial(dispatch_kernel, n),
        out_shape=[
            jax.ShapeDtypeStruct((2,) + outgoing.shape, BF16),
            jax.ShapeDtypeStruct((2,) + slots.shape, jnp.int32),
        ],
        in_specs=[vmem] * 2,
        out_specs=[vmem] * 2,
        scratch_shapes=[pltpu.SemaphoreType.DMA((n,))] * 4 + [pltpu.SemaphoreType.DMA((n + 1,))] * 2,
        compiler_params=pltpu.CompilerParams(collective_id=collective_id, has_side_effects=True),
        name="dispatch",
    )(outgoing, slots)


def push(src, dst, send, recv, device):
    return pltpu.make_async_remote_copy(
        src_ref=src, dst_ref=dst, send_sem=send, recv_sem=recv,
        device_id=device, device_id_type=MESH,
    )


def meet(peers):
    barrier = pltpu.get_barrier_semaphore()
    for peer in peers:
        pl.semaphore_signal(barrier, inc=1, device_id=peer, device_id_type=MESH)
    pl.semaphore_wait(barrier, len(peers))


def chip_links(send, recv):
    dp, me = lax.axis_index("dp"), lax.axis_index("seq")
    axes = []
    for w in (1 + me, 2 - me):
        bit = (dp // w) % 2
        axes.append(((dp + (1 - 2 * bit) * w, me), bit))
    return {
        "dp": dp,
        "me": me,
        "z": dp // 4,
        "partner": (dp, 1 - me),
        "axes": axes,
        "stack": [((dp + 4 * k) % 16, me) for k in range(1, 4)],
        "send": send,
        "recv": recv,
    }


def square_blocks(sources, targets):
    for source, target in zip(sources, targets):
        tall, wide = source.shape
        for r in range(tall // D):
            for c in range(wide // D):
                at = (pl.ds(r * D, D), pl.ds(c * D, D))
                yield source.at[at], target.at[at]


class Chunk:
    def __init__(self, env, number, source, full, acc, landing, shared):
        self.env, self.number, self.shared = env, number, shared
        self.source, self.full, self.acc, self.landing = source, full, acc, landing
        base, size, offset = 0, source.shape[0], 0
        self.levels = []
        for device, bit in ([(env["partner"], env["me"])] if shared else []) + env["axes"]:
            half = size // 2
            keep, give = base + bit * half, base + (1 - bit) * half
            self.levels.append((device, keep, give, half, offset))
            base, size, offset = keep, half, offset + half
        self.base, self.size, self.offset = base, size // 4, offset

    def copy(self, stage, src, dst, device):
        e = self.env
        return push(src, dst, e["send"].at[self.number, stage], e["recv"].at[self.number, stage], device)

    def at(self, ref, start, size):
        return ref.at[pl.ds(start if isinstance(start, int) else pl.multiple_of(start, 16), size), :]

    def halves(self, level):
        device, _, give, half, offset = self.levels[level]
        src = self.acc if level else self.source
        return [self.copy(level, self.at(src, give, half), self.at(self.landing, offset, half), device)]

    def add(self, level):
        _, keep, _, half, offset = self.levels[level]
        src = self.acc if level else self.source
        step = min(half, 64)

        def run(i, _):
            here = pl.ds(pl.multiple_of(keep + i * step, 16), step)
            there = pl.ds(pl.multiple_of(offset + i * step, 16), step)
            total = src[here, :].astype(F32) + self.landing[there, :].astype(F32)
            self.acc[here, :] = total.astype(BF16)
            return 0

        lax.fori_loop(0, half // step, run, 0)

    def quarters(self):
        copies = []
        for k in range(1, 4):
            z = (self.env["z"] + k) % 4
            copies.append(
                self.copy(
                    len(self.levels) + k - 1,
                    self.at(self.acc, self.base + z * self.size, self.size),
                    self.at(self.landing, self.offset + (k - 1) * self.size, self.size),
                    self.env["stack"][k - 1],
                )
            )
        return copies

    def total(self):
        here = pl.ds(pl.multiple_of(self.base + self.env["z"] * self.size, 16), self.size)
        total = self.acc[here, :].astype(F32)
        for k in range(3):
            there = slice(self.offset + k * self.size, self.offset + (k + 1) * self.size)
            total += self.landing[there, :].astype(F32)
        self.full[here, :] = total.astype(BF16)

    def gathers(self):
        region = self.at(self.full, self.base + self.env["z"] * self.size, self.size)
        first = len(self.levels) + 3
        return [self.copy(first + k, region, region, self.env["stack"][k]) for k in range(3)]

    def spread(self, level):
        device, keep, _, half, _ = self.levels[level]
        region = self.at(self.full, keep, half)
        return [self.copy(len(self.levels) + 6 + level, region, region, device)]

    def hand_over(self):
        return [self.copy(2 * len(self.levels) + 6, self.full, self.full, self.env["partner"])]

    def steps(self):
        count = len(self.levels)
        stages = [functools.partial(self.halves, n) for n in range(count)] + [self.quarters, self.gathers]
        stages += [functools.partial(self.spread, n) for n in range(count - 1, -1, -1)]
        between = [functools.partial(self.add, n) for n in range(count)] + [self.total]
        if not self.shared:
            stages.append(self.hand_over)

        def step(n):
            if n > 0:
                for copy in stages[n - 1]():
                    copy.wait()
                if n - 1 < len(between):
                    between[n - 1]()
            if n < len(stages):
                for copy in stages[n]():
                    copy.start()

        return [functools.partial(step, n) for n in range(len(stages) + 1)]


def final_kernel(
    ga_ref, gb_ref, qkv_ref, vec_ref,
    back_ref, qkv_full, vec_full,
    ret_ref, gbr_ref, acc_ref, landing_ref, vec_recv,
    send, recv, asend, arecv, gsend, grecv, vsend, vrecv,
):
    n = 16
    rows = ga_ref.shape[0]
    piece = rows // n
    env = chip_links(send, recv)
    dp, me, partner = env["dp"], env["me"], env["partner"]
    meet([((dp + k) % n, me) for k in range(1, n)] + [partner])

    quarter = rows // 4
    halves = []
    for j in range(4):
        part = pl.ds(j * quarter, quarter)
        copy = push(gb_ref.at[part, :], gbr_ref.at[part, :], gsend.at[j], grecv.at[j], partner)
        copy.start()
        halves.append(copy)

    lines = []
    for c in range(3):
        lines.append(
            Chunk(
                env, c, qkv_ref.at[c], qkv_full.at[me, c], acc_ref.at[c], landing_ref.at[c], False
            ).steps()
        )
    peers = [partner]
    for w in (1, 2, 4, 8):
        bit = (dp // w) % 2
        peers.append((dp + (1 - 2 * bit) * w, me))
    vec_copies = []

    def vec_step(s):
        if s == 0:
            vec_full[...] = vec_ref[...]
        else:
            vec_copies[-1].wait()
            vec_full[...] += vec_recv[s - 1]
        if s < len(peers):
            sent = vec_recv.at[len(peers) + s]
            sent[...] = vec_full[...]
            copy = push(sent, vec_recv.at[s], vsend.at[s], vrecv.at[s], peers[s])
            copy.start()
            vec_copies.append(copy)

    lines.append([functools.partial(vec_step, s) for s in range(len(peers) + 1)])

    returns = []

    def give_back():
        for j in range(4):
            halves[j].wait()

            def add(i, _, j=j):
                here = pl.ds(pl.multiple_of(j * quarter + i * 64, 64), 64)
                ret_ref[here, :] = (ga_ref[here, :] + gbr_ref[here, :].astype(F32)).astype(BF16)
                return 0

            lax.fori_loop(0, quarter // 64, add, 0)
        mine = pl.ds(pl.multiple_of(dp * piece, piece), piece)
        for k in far_first(n):
            p = (dp + k) % n
            theirs = pl.ds(pl.multiple_of(p * piece, piece), piece)
            copy = push(
                ret_ref.at[theirs, :], back_ref.at[mine, :], asend.at[k], arecv.at[k], (p, me)
            )
            copy.start()
            returns.append(copy)
        back_ref[mine, :] = ret_ref[mine, :]

    ticks = max(len(line) for line in lines)
    for t in range(ticks):
        for line in lines:
            if t < len(line):
                line[t]()
        if t == 0:
            give_back()
    for copy in returns:
        copy.wait()


def give_back_and_sum(ga, gb, qkv, vec, collective_id):
    vmem = pl.BlockSpec(memory_space=VMEM)
    shape = jax.ShapeDtypeStruct
    dma = pltpu.SemaphoreType.DMA
    return pl.pallas_call(
        final_kernel,
        out_shape=[shape(gb.shape, BF16), shape((2,) + qkv.shape, BF16), shape(vec.shape, F32)],
        in_specs=[vmem] * 4,
        out_specs=[vmem] * 3,
        scratch_shapes=[
            VMEM(gb.shape, BF16),
            VMEM(gb.shape, BF16),
            VMEM((3, D, C), BF16),
            VMEM((3, D, C), BF16),
            VMEM((10,) + vec.shape, F32),
            dma((3, 12)), dma((3, 12)),
            dma((16,)), dma((16,)),
            dma((4,)), dma((4,)),
            dma((5,)), dma((5,)),
        ],
        compiler_params=pltpu.CompilerParams(collective_id=collective_id, has_side_effects=True),
        name="give_back_and_sum",
    )(ga, gb, qkv, vec)


def body(
    tokens,
    route,
    lengths,
    query_weight,
    query_bias,
    key_weight,
    value_weight,
    value_bias,
    output_weight,
    output_bias,
    first_gain,
    first_shift,
    up_weight,
    up_bias,
    down_weight,
    down_bias,
    second_gain,
    second_shift,
    cotangent,
):
    groups = lax.axis_size("dp")
    rows = tokens.shape[0]
    piece = rows // groups
    span = rows * lax.axis_size("seq")
    seq = lax.axis_index("seq")
    tables = lengths[0]
    me = seq.reshape(1).astype(jnp.int32)
    kernels = groups == 16 and piece % 16 == 0
    if kernels:
        pieces = 2 * groups
        outgoing, slots_out = arrange(tokens.reshape(groups, piece, D), route)
        x_all, slots_all = dispatch(outgoing, slots_out, 0)
        x_all = x_all.reshape(span, D)
        slots = slots_all[:, :, 0, 0].reshape(pieces)
    else:
        pieces = 0
        target = route // groups // lax.axis_size("seq")
        place = route % groups
        outgoing = jnp.zeros((groups, piece, D), BF16).at[target].set(tokens.reshape(groups, piece, D))
        slots_out = jnp.zeros((groups,), jnp.int32).at[target].set(place)
        incoming, slots = (
            lax.all_to_all(outgoing, "dp", split_axis=0, concat_axis=0, tiled=True),
            lax.all_to_all(slots_out, "dp", split_axis=0, concat_axis=0, tiled=True),
        )
        inputs = jnp.zeros_like(incoming).at[slots].set(incoming).reshape(rows, D)
        x_all = swap(inputs, 0).reshape(span, D)
    x_turned, q, k, v, mixed_all, attend_out, lse, inputs = attend_forward(
        x_all, pieces, tables, me, slots,
        query_weight, key_weight, value_weight, query_bias, value_bias,
    )
    mixed_halves = swap(mixed_all.reshape(2, rows, C), 1)
    mixed = jnp.concatenate([mixed_halves[0], mixed_halves[1]], axis=1)
    branch = product(mixed, output_weight) + output_bias
    residual = inputs.astype(F32) + branch
    first, first_back = jax.vjp(
        norm_rows, residual, first_gain.astype(F32), first_shift.astype(F32)
    )
    first_low = first.astype(BF16)
    hidden = product(first_low, up_weight) + up_bias
    active = gelu_exact(hidden).astype(BF16)
    update = product(active, down_weight) + down_bias
    layer_out, second_back = jax.vjp(
        norm_rows, first + update, second_gain.astype(F32), second_shift.astype(F32)
    )
    grad_second, grad_second_gain, grad_second_shift = second_back(cotangent.astype(F32))
    grad_update = grad_second.astype(BF16)
    again = product(first_low, up_weight) + up_bias
    active_again, gelu_back = jax.vjp(gelu_exact, again)
    active_low = active_again.astype(BF16)
    grad_down = product_left(active_low, grad_update)
    grad_down_bias = column_sums(grad_update)
    (grad_active,) = gelu_back(product_right(grad_update, down_weight))
    grad_hidden = grad_active.astype(BF16)
    grad_up = product_left(first_low, grad_hidden)
    grad_up_bias = column_sums(grad_hidden)
    grad_first = grad_second + product_right(grad_hidden, up_weight)
    grad_residual, grad_first_gain, grad_first_shift = first_back(grad_first)
    grad_branch = grad_residual.astype(BF16)
    grad_output = product_left(mixed, grad_branch)
    grad_output_bias = column_sums(grad_branch)
    grad_mixed = product_right(grad_branch, output_weight).astype(BF16)
    grad_halves = jnp.stack([grad_mixed[:, :C], grad_mixed[:, C:]])
    grad_mixed_all = swap(grad_halves, 2).reshape(span, C)
    raw = [a.astype(BF16) for a in (grad_up, grad_down, grad_output)] if kernels else []
    grad_columns, column_parts, grad_own, grad_other, *summed = attend_backward(
        tables, slots, pieces, x_turned, q, k, v, grad_mixed_all, attend_out, lse,
        query_weight, key_weight, value_weight, grad_residual, raw, 3,
    )

    def own_columns(part):
        return lax.dynamic_update_slice(jnp.zeros((1, D), F32), part, (0, seq * C))

    vec = jnp.concatenate(
        [
            own_columns(column_parts[:, :C]),
            own_columns(column_parts[:, C:]),
            jnp.stack(
                [
                    grad_output_bias,
                    grad_first_gain,
                    grad_first_shift,
                    grad_down_bias,
                    grad_second_gain,
                    grad_second_shift,
                ]
            ),
            grad_up_bias.reshape(-1, D),
            jnp.zeros((4, D), F32),
        ]
    )
    if kernels:
        back, columns, vec = give_back_and_sum(grad_own, grad_other, grad_columns, vec, 4)
        token_grad = restore(back.reshape(groups, piece, D), route).reshape(rows, D)
        up_sum, down_sum, out_sum = (a.astype(F32) for a in summed)
        columns = jnp.concatenate([columns[0], columns[1]], axis=2).astype(F32)
    else:
        grad_inputs = grad_own + swap(jnp.stack([grad_other, grad_other]), 5)[1 - seq].astype(F32)
        back_rows = grad_inputs.astype(BF16).reshape(groups, piece, D)[slots]
        returned = lax.all_to_all(back_rows, "dp", split_axis=0, concat_axis=0, tiled=True)
        token_grad = returned[target].reshape(rows, D)
        up_sum, down_sum, out_sum, vec = lax.psum((grad_up, grad_down, grad_output, vec), ("dp", "seq"))
        columns = lax.psum(grad_columns.astype(F32), "dp")
        columns = lax.all_gather(columns, "seq", axis=2, tiled=True)
    query_sum, key_sum, value_sum = columns[0], columns[1], columns[2]
    return (
        layer_out.astype(BF16),
        token_grad,
        query_sum,
        vec[0],
        key_sum,
        value_sum,
        vec[1],
        out_sum,
        vec[2],
        vec[3],
        vec[4],
        up_sum,
        vec[8:12].reshape(-1),
        down_sum,
        vec[5],
        vec[6],
        vec[7],
    )


def solution(mesh):
    both, one = P(("dp", "seq"), None), P()
    return jax.shard_map(
        body,
        mesh=mesh,
        in_specs=(both, P(("dp", "seq")), P("dp", None)) + (one,) * 15 + (both,),
        out_specs=(both, both) + (one,) * 15,
        check_vma=False,
    )
```

```python
import functools

import jax
import jax.numpy as jnp
from jax import lax
from jax.experimental import pallas as pl
from jax.experimental.pallas import tpu as pltpu
from jax.sharding import PartitionSpec as P

D = 512
HEADS = 8
HEAD = 64
HL = HEADS // 2
C = HL * HEAD
PAIR = 128
NEG = -1e30
LOG2E = 1.4426950408889634
BQ = 256
BK = 256
PACE = 1.2
F32 = jnp.float32
BF16 = jnp.bfloat16
MESH = pl.DeviceIdType.MESH
VMEM = pltpu.VMEM
SMEM = pltpu.SMEM


def norm_rows(value, gain, shift):
    center = value - jnp.mean(value, axis=-1, keepdims=True)
    spread = jnp.mean(center * center, axis=-1, keepdims=True)
    return center * lax.rsqrt(spread + 1e-05) * gain + shift


def gelu_exact(value):
    return jax.nn.gelu(value, approximate=False)


def product(left, right):
    return jnp.dot(left, right, preferred_element_type=F32)


def product_left(left, right):
    return lax.dot_general(left, right, (((0,), (0,)), ((), ())), preferred_element_type=F32)


def product_right(left, right):
    return lax.dot_general(left, right, (((1,), (1,)), ((), ())), preferred_element_type=F32)


def column_sums(value):
    return jnp.sum(value.astype(F32), axis=0)


def swap_kernel(x_ref, o_ref, send, recv, local):
    dp, me = lax.axis_index("dp"), lax.axis_index("seq")
    other = 1 - me
    barrier = pltpu.get_barrier_semaphore()
    pl.semaphore_signal(barrier, inc=1, device_id=(dp, other), device_id_type=MESH)
    pl.semaphore_wait(barrier, 1)
    rows, width = o_ref.shape
    if x_ref.shape == (2 * rows, width // 2):
        target = o_ref.at[:, pl.ds(pl.multiple_of(me * (width // 2), width // 2), width // 2)]
        sources = [x_ref.at[pl.ds(pl.multiple_of(d * rows, rows), rows), :] for d in (other, me)]
    elif x_ref.shape == (rows // 2, 2 * width):
        target = o_ref.at[pl.ds(pl.multiple_of(me * (rows // 2), rows // 2), rows // 2), :]
        sources = [x_ref.at[:, pl.ds(pl.multiple_of(d * width, width), width)] for d in (other, me)]
    else:
        target = o_ref.at[pl.ds(pl.multiple_of(me * (rows // 2), rows // 2), rows // 2), :]
        sources = [x_ref, x_ref]
    copy = push(sources[0], target, send, recv, (dp, other))
    copy.start()
    own = pltpu.make_async_copy(sources[1], target, local)
    own.start()
    own.wait()
    copy.wait()


def swap(x, shape, collective_id):
    return pl.pallas_call(
        swap_kernel,
        out_shape=jax.ShapeDtypeStruct(shape, x.dtype),
        in_specs=[pl.BlockSpec(memory_space=VMEM)],
        out_specs=pl.BlockSpec(memory_space=VMEM),
        scratch_shapes=[pltpu.SemaphoreType.DMA] * 3,
        compiler_params=pltpu.CompilerParams(collective_id=collective_id, has_side_effects=True),
    )(x)


def rotation(len_ref, span):
    lengths = [len_ref[j] for j in range(len_ref.shape[0])]
    longest = functools.reduce(jnp.maximum, lengths)
    shift, total, ends = jnp.int32(0), jnp.int32(0), []
    for length in lengths:
        shift = jnp.where(length == longest, total, shift)
        total = total + length
        ends.append(total)
    turned = [e - shift for e in ends]
    return shift, [jnp.where(e <= 0, e + span, e) for e in turned]


def rows_from(ref, start, count):
    base = lax.div(start, 8) * 8
    r = start - base
    x = ref[pl.ds(base, count + 8), :]
    width = x.shape[1]
    row = lax.broadcasted_iota(jnp.int32, (1, 8, 1), 1)
    for bit in (1, 2, 4):
        by_eights = x.reshape(x.shape[0] // 8, 8, width)
        turned = pltpu.roll(by_eights, 8 - bit, axis=1)
        following = jnp.concatenate([turned[1:], turned[:1]], axis=0)
        moved = jnp.where(row < 8 - bit, turned, following).reshape(x.shape)
        x = jnp.where(jnp.full(x.shape, r & bit) != 0, moved, x)
    return x[:count]


def table_of(ends, position):
    start, end = jnp.zeros_like(position), jnp.full_like(position, 1 << 30)
    for e in ends:
        start = jnp.where(e <= position, jnp.maximum(start, e), start)
        end = jnp.where(e > position, jnp.minimum(end, e), end)
    return start, end


def tile_mask(ends, i):
    return table_of(ends, i * BQ + lax.broadcasted_iota(jnp.int32, (1, BQ), 1))


def head_masks():
    lane = lax.broadcasted_iota(jnp.int32, (1, PAIR), 1)
    low = (lane < HEAD).astype(F32).astype(BF16)
    return low, (lane >= HEAD).astype(F32).astype(BF16)


def by_eight(value, op):
    return op(value.reshape(value.shape[0] // 8, 8, value.shape[1]), axis=0)


def forward_kernel(
    pieces, len_ref, me_ref, slot_ref, loaded_ref, wq_ref, wk_ref, wv_ref, bq_ref, bv_ref,
    x_ref, q_ref, k_ref, v_ref, mixed_ref, out_ref, lse_ref, own_ref,
    vt_ref, acc_ref, s_ref, packed_ref, turned_ref,
):
    span = loaded_ref.shape[0]
    half, blocks = span // 2, span // BQ
    near = blocks // 2
    shift, ends = rotation(len_ref, span)
    count = pieces if pieces else 32
    piece = span // count

    def place(k, _):
        slot = slot_ref[k] if pieces else k % (count // 2)
        row = (k // (count // 2)) * half + slot * piece
        packed_ref[pl.ds(pl.multiple_of(row, piece), piece), :] = loaded_ref[
            pl.ds(pl.multiple_of(k * piece, piece), piece), :
        ].astype(F32)
        return 0

    lax.fori_loop(0, count, place, 0)
    packed_ref[span:, :] = packed_ref[: BQ + 8, :]
    own_ref[...] = packed_ref[pl.ds(pl.multiple_of(me_ref[0] * half, half), half), :].astype(BF16)

    def project(i, _):
        rows = pl.ds(pl.multiple_of(i * BQ, BQ), BQ)
        x = rows_from(packed_ref, lax.rem(i * BQ + shift, span), BQ).astype(BF16)
        x_ref[rows, :] = x
        q = (product(x, wq_ref[...]) + bq_ref[...].astype(F32)).astype(BF16)
        q_ref[rows, :] = (q.astype(F32) * (HEAD**-0.5)).astype(BF16)
        k_ref[rows, :] = product(x, wk_ref[...]).astype(BF16)
        v = (product(x, wv_ref[...]) + bv_ref[...].astype(F32)).astype(BF16)
        v_ref[rows, :] = v
        vt_ref[:, rows] = v.T
        return 0

    lax.fori_loop(0, blocks, project, 0)
    masks = head_masks()

    def query_block(masked, i, _):
        rows = pl.ds(pl.multiple_of(i * BQ, BQ), BQ)
        base = near if masked else 0
        if masked:
            start, end = tile_mask(ends, i)
        q = q_ref[rows, :]
        heads = [q[:, (h // 2) * PAIR : (h // 2 + 1) * PAIR] * masks[h % 2] for h in range(HL)]
        acc_ref[...] = jnp.zeros_like(acc_ref)

        def score_block(j, tops):
            keys = pl.ds(pl.multiple_of((base + j) * BK, BK), BK)
            if masked:
                kpos = (base + j) * BK + lax.broadcasted_iota(jnp.int32, (BK, BQ), 0)
                mask = (kpos >= start) & (kpos < end)
            new = []
            for h in range(HL):
                kp = k_ref[keys, (h // 2) * PAIR : (h // 2 + 1) * PAIR]
                s = product_right(kp, heads[h]) * LOG2E
                if masked:
                    s = jnp.where(mask, s, NEG)
                s_ref[h, pl.ds(pl.multiple_of(j * BK, BK), BK), :] = s
                new.append(jnp.maximum(tops[h], by_eight(s, jnp.max)))
            return tuple(new)

        tops = lax.fori_loop(
            0, near, score_block, tuple(jnp.full((8, BQ), NEG, F32) for _ in range(HL))
        )
        tops = [jnp.max(t, axis=0, keepdims=True) for t in tops]

        def mix_block(j, totals):
            keys = pl.ds(pl.multiple_of((base + j) * BK, BK), BK)
            new = []
            for h in range(HL):
                p = jnp.exp2(s_ref[h, pl.ds(pl.multiple_of(j * BK, BK), BK), :] - tops[h])
                new.append(totals[h] + by_eight(p, jnp.sum))
                lanes = slice(h * HEAD, (h + 1) * HEAD)
                acc_ref[lanes, :] += product(vt_ref[lanes, keys], p.astype(BF16))
            return tuple(new)

        totals = lax.fori_loop(
            0, near, mix_block, tuple(jnp.zeros((8, BQ), F32) for _ in range(HL))
        )
        for h in range(HL):
            total = jnp.sum(totals[h], axis=0, keepdims=True)
            lanes = slice(h * HEAD, (h + 1) * HEAD)
            acc_ref[lanes, :] = acc_ref[lanes, :] / total
            lse_ref[h : h + 1, rows] = tops[h] + jnp.log2(total)
        out = acc_ref[...]
        out_ref[:, rows] = out
        turned_ref[rows, :] = out.T
        return 0

    lax.fori_loop(0, near, functools.partial(query_block, False), 0)
    lax.fori_loop(near, blocks, functools.partial(query_block, True), 0)
    turned_ref[span:, :] = turned_ref[: BQ + 8, :]

    def turn_back(i, _):
        rows = pl.ds(pl.multiple_of(i * BQ, BQ), BQ)
        mixed_ref[rows, :] = rows_from(turned_ref, lax.rem(i * BQ + span - shift, span), BQ).astype(BF16)
        return 0

    lax.fori_loop(0, blocks, turn_back, 0)


def column_block(shape):
    return pl.BlockSpec(shape, lambda i, lengths, me, slots: (0, me[0]))


def whole_block(shape):
    return pl.BlockSpec(shape, lambda i, lengths, me, slots: (0,) * len(shape))


def attend_forward(x_all, pieces, lengths, me, slots, wq, wk, wv, bq, bv):
    span = x_all.shape[0]
    rows_shape = jax.ShapeDtypeStruct((span, C), BF16)
    return pl.pallas_call(
        functools.partial(forward_kernel, pieces),
        grid_spec=pltpu.PrefetchScalarGridSpec(
            num_scalar_prefetch=3,
            grid=(1,),
            in_specs=[
                whole_block((span, D)),
                column_block((D, C)),
                column_block((D, C)),
                column_block((D, C)),
                column_block((1, C)),
                column_block((1, C)),
            ],
            out_specs=[whole_block((span, D))] + [whole_block((span, C))] * 4
            + [whole_block((C, span)), whole_block((8, span)), whole_block((span // 2, D))],
            scratch_shapes=[
                VMEM((C, span), BF16),
                VMEM((C, BQ), F32),
                VMEM((HL, span // 2, BQ), F32),
                VMEM((span + BQ + 8, D), F32),
                VMEM((span + BQ + 8, C), F32),
            ],
        ),
        out_shape=[jax.ShapeDtypeStruct((span, D), BF16)] + [rows_shape] * 4
        + [jax.ShapeDtypeStruct((C, span), F32), jax.ShapeDtypeStruct((8, span), F32)]
        + [jax.ShapeDtypeStruct((span // 2, D), BF16)],
        name="attend_forward",
    )(lengths, me, slots, x_all, wq, wk, wv, bq.reshape(1, D), bv.reshape(1, D))


def backward_kernel(pieces, sums, *refs):
    len_ref, slot_ref, x_ref, q_ref, k_ref, v_ref, g_ref, out_ref, lse_ref = refs[:9]
    weights, res_ref = refs[9:12], refs[12]
    refs = refs[13:]
    if sums:
        raw, vec_ref = refs[:3], refs[3]
        full, back_ref, qkv_full, vec_full = refs[4:7], refs[7], refs[8], refs[9]
        refs = refs[10:]
    gw_ref, sums_ref, ga_ref, gb_ref = refs[:4]
    refs = refs[4:]
    kt_ref, gq_ref, gk_ref, gv_ref, gqt_ref, qs_ref, gs_ref, w_ref, ds_ref = refs[:9]
    term_ref, turned_ref, gx_ref = refs[9:12]
    me = lax.axis_index("seq")
    span = x_ref.shape[0]
    half, blocks = span // 2, span // BQ
    near = blocks // 2
    scale = HEAD**-0.5
    columns = pl.ds(pl.multiple_of(me * C, C), C)
    ticks = []
    if sums:
        acc_ref, landing_ref, acc_own, landing_own, gbr_ref, arrived_ref, vec_recv = refs[12:19]
        send, recv, asend, arecv, gsend, grecv, vsend, vrecv = refs[19:]
        env = chip_links(send, recv)
        dp, partner = env["dp"], env["partner"]
        meet([(lax.rem(dp + k, 16), me) for k in range(1, 16)] + [partner])
        cross = push(
            g_ref.at[:, pl.ds(pl.multiple_of((1 - me) * C, C), C)], arrived_ref,
            gsend.at[4], grecv.at[4], partner,
        )
        cross.start()
        lines = [
            Chunk(env, c, source, target, acc_ref.at[c], landing_ref.at[c], True).steps()
            for c, (source, target) in enumerate(square_blocks(raw, full))
        ]
        for c, line in enumerate(lines):
            for j, step in enumerate(line):
                at = int((c + 2 * j) * PACE)
                ticks += [[] for _ in range(at + 1 - len(ticks))]
                ticks[at].append(step)

    def tick(now, candidates):
        for t in candidates:
            if t < len(ticks) and ticks[t]:

                @pl.when(now == t)
                def _(t=t):
                    for step in ticks[t]:
                        step()

    def straight(t):
        for step in ticks[t] if t < len(ticks) else []:
            step()

    straight(0)
    shift, ends = rotation(len_ref, span)

    def prepare(i, _):
        rows = pl.ds(pl.multiple_of(i * BQ, BQ), BQ)
        kt_ref[:, rows] = k_ref[rows, :].T
        gk_ref[rows, :] = jnp.zeros((BQ, C), F32)
        gv_ref[rows, :] = jnp.zeros((BQ, C), F32)
        if not sums:
            turned_ref[rows, :] = g_ref[rows, :].astype(F32)
        return 0

    lax.fori_loop(0, blocks, prepare, 0)
    if sums:
        turned_ref[pl.ds(pl.multiple_of(me * half, half), half), :] = g_ref[:, columns].astype(F32)
        cross.wait()
        turned_ref[pl.ds(pl.multiple_of((1 - me) * half, half), half), :] = arrived_ref[...].astype(F32)
    turned_ref[span:, :] = turned_ref[: BQ + 8, :]
    straight(1)
    lane = lax.broadcasted_iota(jnp.int32, (1, C), 1) // HEAD
    masks = [(lane == h).astype(F32).astype(BF16) for h in range(HL)]

    def query_block(masked, i, _):
        rows = pl.ds(pl.multiple_of(i * BQ, BQ), BQ)
        base = near if masked else 0
        if masked:
            start, end = tile_mask(ends, i)
        q = q_ref[rows, :]
        exact = rows_from(turned_ref, lax.rem(i * BQ + shift, span), BQ)
        g = exact.astype(BF16)
        for h in range(HL):
            part = slice(h * BQ, (h + 1) * BQ)
            qs_ref[part, :] = q * masks[h]
            gs_ref[part, :] = g * masks[h]
        weighted = exact.T * out_ref[:, rows]
        inner = [
            jnp.sum(weighted[h * HEAD : (h + 1) * HEAD], axis=0, keepdims=True) for h in range(HL)
        ]
        logsum = [lse_ref[h : h + 1, rows] for h in range(HL)]
        gqt_ref[...] = jnp.zeros_like(gqt_ref)

        def key_block(j, _):
            keys = pl.ds(pl.multiple_of((base + j) * BK, BK), BK)
            here = pl.ds(pl.multiple_of(j * BK, BK), BK)
            if masked:
                kpos = (base + j) * BK + lax.broadcasted_iota(jnp.int32, (BK, BQ), 0)
                mask = (kpos >= start) & (kpos < end)
            for h in range(HL):
                part = slice(h * BQ, (h + 1) * BQ)
                pair = slice((h // 2) * PAIR, (h // 2 + 1) * PAIR)
                s = product_right(k_ref[keys, pair], qs_ref[part, pair])
                w = jnp.exp2(s * LOG2E - logsum[h])
                if masked:
                    w = jnp.where(mask, w, 0.0)
                gw = product_right(v_ref[keys, pair], gs_ref[part, pair])
                gs = (w * (gw - inner[h])).astype(BF16)
                w_ref[here, part] = w.astype(BF16)
                ds_ref[here, part] = gs
            return 0

        def product_block(j, _):
            keys = pl.ds(pl.multiple_of((base + j) * BK, BK), BK)
            here = pl.ds(pl.multiple_of(j * BK, BK), BK)
            for h in range(HL):
                part = slice(h * BQ, (h + 1) * BQ)
                lanes = slice(h * HEAD, (h + 1) * HEAD)
                gqt_ref[lanes, :] += product(kt_ref[lanes, keys], ds_ref[here, part])
            gv_ref[keys, :] += product(w_ref[here, :], gs_ref[...])
            gk_ref[keys, :] += product(ds_ref[here, :], qs_ref[...])
            return 0

        first = 2 + 2 * base
        lax.fori_loop(0, near, key_block, 0)
        tick(2 + 2 * i, range(first, first + 2 * near, 2))
        lax.fori_loop(0, near, product_block, 0)
        gq_ref[rows, :] = (gqt_ref[...].T * scale).astype(BF16)
        tick(3 + 2 * i, range(first + 1, first + 2 * near, 2))
        return 0

    lax.fori_loop(0, near, functools.partial(query_block, False), 0)
    lax.fori_loop(near, blocks, functools.partial(query_block, True), 0)

    after = 2 + 2 * blocks
    term_ref[...] = jnp.zeros_like(term_ref)
    sums_ref[...] = jnp.zeros_like(sums_ref)

    def gradients(i, _):
        rows = pl.ds(pl.multiple_of(i * BQ, BQ), BQ)
        parts = [gq_ref[rows, :], gk_ref[rows, :].astype(BF16), gv_ref[rows, :].astype(BF16)]
        x = x_ref[rows, :]
        for n, part in enumerate(parts):
            term_ref[n] += product_left(x, part)
        sums_ref[...] += jnp.concatenate(
            [jnp.sum(a.astype(F32), axis=0, keepdims=True) for a in (parts[0], parts[2])], axis=1
        )
        gx_ref[rows, :] = (
            product_right(parts[0], weights[0][:, columns])
            + product_right(parts[1], weights[1][:, columns])
            + product_right(parts[2], weights[2][:, columns])
        )
        tick(after + i, range(after, after + blocks))
        return 0

    lax.fori_loop(0, blocks, gradients, 0)
    gw_ref[...] = term_ref[...].astype(BF16)
    count = pieces if pieces else 32
    each = count // 2
    piece = span // count
    gx_ref[span:, :] = gx_ref[: piece + 8, :]

    def piece_rows(part, k):
        row = (slot_ref[part * each + k] if pieces else k) * piece
        return rows_from(gx_ref, lax.rem(part * half + row + span - shift, span), piece), row

    def own_piece(k, _):
        gx, row = piece_rows(me, k)
        here = pl.ds(pl.multiple_of(k * piece, piece), piece)
        gx = gx + res_ref[pl.ds(row, piece), :]
        if sums:
            ga_ref[here, :] = (gx + gbr_ref[here, :].astype(F32)).astype(BF16)
        else:
            ga_ref[here, :] = gx
        return 0

    def other_piece(k, _):
        gx, _ = piece_rows(1 - me, k)
        gb_ref[pl.ds(pl.multiple_of(k * piece, piece), piece), :] = gx.astype(BF16)
        return 0

    if not sums:
        lax.fori_loop(0, each, own_piece, 0)
        lax.fori_loop(0, each, other_piece, 0)
        return

    lines = [
        Chunk(
            env, 9 + c, gw_ref.at[c], qkv_full.at[me, c], acc_own.at[c], landing_own.at[c], False
        ).steps()
        for c in range(3)
    ]
    peers = [partner]
    for w in (1, 2, 4, 8):
        bit = (dp // w) % 2
        peers.append((dp + (1 - 2 * bit) * w, me))

    def vec_copy(s):
        return push(vec_recv.at[len(peers) + s], vec_recv.at[s], vsend.at[s], vrecv.at[s], peers[s])

    def vec_step(s):
        if s == 0:
            vec_full[...] = vec_ref[...]
            vec_full[0:1, columns] = sums_ref[:, :C]
            vec_full[1:2, columns] = sums_ref[:, C:]
        else:
            vec_copy(s - 1).wait()
            vec_full[...] += vec_recv[s - 1]
        if s < len(peers):
            vec_recv[len(peers) + s] = vec_full[...]
            vec_copy(s).start()

    lines.append([functools.partial(vec_step, s) for s in range(len(peers) + 1)])
    left = [ticks[t] for t in range(after + blocks, len(ticks))]
    queue = [
        (left[n] if n < len(left) else []) + [line[n] for line in lines if n < len(line)]
        for n in range(max([len(left)] + [len(line) for line in lines]))
    ]

    def advance():
        for step in queue.pop(0) if queue else []:
            step()

    floor, place = env["z"], lax.rem(dp, 4)
    order = (2, 1, 3, 0)
    plane = 4 * piece

    def across(k):
        here = pl.ds(pl.multiple_of(lax.rem(floor + k, 4) * plane, plane), plane)
        return push(gb_ref.at[here, :], gbr_ref.at[here, :], gsend.at[k], grecv.at[k], partner)

    advance()
    for k in order:
        first = lax.rem(floor + k, 4) * 4
        lax.fori_loop(first, first + 4, other_piece, 0)
        across(k).start()
    advance()
    mine = pl.ds(pl.multiple_of(dp * piece, piece), piece)
    returns = []
    for k in order:
        first = lax.rem(floor + k, 4) * 4
        across(k).wait()
        lax.fori_loop(first, first + 4, own_piece, 0)
        for i in range(4):
            if k == 0 and i == 0:
                back_ref[mine, :] = ga_ref[mine, :]
                continue
            p = first + lax.rem(place + i, 4)
            theirs = pl.ds(pl.multiple_of(p * piece, piece), piece)
            n = 4 * k + i
            copy = push(ga_ref.at[theirs, :], back_ref.at[mine, :], asend.at[n], arecv.at[n], (p, me))
            copy.start()
            returns.append(copy)
        advance()
    while queue:
        advance()
    for copy in returns:
        copy.wait()


def attend_backward(lengths, slots, pieces, x, q, k, v, g, out, lse, wq, wk, wv, res, raw, vec, collective_id):
    span = x.shape[0]
    half = span // 2
    vmem, smem = pl.BlockSpec(memory_space=VMEM), pl.BlockSpec(memory_space=SMEM)
    shape = jax.ShapeDtypeStruct
    sums = len(raw) > 0
    dma = pltpu.SemaphoreType.DMA
    results = [
        ((3, D, C), BF16),
        ((1, 2 * C), F32),
        ((half, D), BF16 if sums else F32),
        ((half, D), BF16),
    ]
    outs = [shape(*r) for r in results]
    operands = (lengths, slots, x, q, k, v, g, out, lse, wq, wk, wv, res)
    before, comm, params = [], [], {}
    if sums:
        chunks = sum(a.size for a in raw) // (D * D)
        outs = [shape(a.shape, BF16) for a in raw]
        outs += [shape((half, D), BF16), shape((2, 3, D, C), BF16), shape(vec.shape, F32)]
        before = [VMEM(*r) for r in results]
        comm = [VMEM((chunks, D, D), BF16)] * 2 + [VMEM((3, D, C), BF16)] * 2
        comm += [VMEM((half, D), BF16), VMEM((half, C), BF16), VMEM((10,) + vec.shape, F32)]
        comm += [dma((chunks + 3, 13))] * 2 + [dma((16,))] * 2 + [dma((5,))] * 4
        params = dict(collective_id=collective_id, has_side_effects=True)
        operands += (*raw, vec)
    return pl.pallas_call(
        functools.partial(backward_kernel, pieces, sums),
        out_shape=outs,
        in_specs=[smem] * 2 + [vmem] * (len(operands) - 2),
        out_specs=[vmem] * len(outs),
        scratch_shapes=before
        + [
            VMEM((C, span), BF16),
            VMEM((span, C), BF16),
            VMEM((span, C), F32),
            VMEM((span, C), F32),
            VMEM((C, BQ), F32),
            VMEM((HL * BQ, C), BF16),
            VMEM((HL * BQ, C), BF16),
            VMEM((half, HL * BQ), BF16),
            VMEM((half, HL * BQ), BF16),
            VMEM((3, D, C), F32),
            VMEM((span + BQ + 8, C), F32),
            VMEM((span + span // (pieces if pieces else 32) + 8, D), F32),
        ]
        + comm,
        compiler_params=pltpu.CompilerParams(vmem_limit_bytes=63 << 20, **params),
        name="attend_backward",
    )(*operands)


def arrange_kernel(groups, route_ref, x_ref, o_ref, slot_ref):
    for k in range(groups):
        packed = route_ref[k]
        group = packed // (2 * groups)
        o_ref[group] = x_ref[k]
        slot_ref[group] = jnp.full(slot_ref.shape[1:], packed % groups, jnp.int32)


def arrange(pieces, route):
    groups, piece, _ = pieces.shape
    return pl.pallas_call(
        functools.partial(arrange_kernel, groups),
        grid_spec=pltpu.PrefetchScalarGridSpec(
            num_scalar_prefetch=1,
            grid=(1,),
            in_specs=[pl.BlockSpec(pieces.shape, lambda i, r: (0, 0, 0))],
            out_specs=[
                pl.BlockSpec(pieces.shape, lambda i, r: (0, 0, 0)),
                pl.BlockSpec((groups, 8, 128), lambda i, r: (0, 0, 0)),
            ],
        ),
        out_shape=[
            jax.ShapeDtypeStruct(pieces.shape, BF16),
            jax.ShapeDtypeStruct((groups, 8, 128), jnp.int32),
        ],
        name="arrange",
    )(route, pieces)


def restore_kernel(groups, route_ref, x_ref, o_ref):
    for k in range(groups):
        o_ref[k] = x_ref[route_ref[k] // (2 * groups)]


def restore(pieces, route):
    spec = pl.BlockSpec(pieces.shape, lambda i, r: (0, 0, 0))
    return pl.pallas_call(
        functools.partial(restore_kernel, pieces.shape[0]),
        grid_spec=pltpu.PrefetchScalarGridSpec(
            num_scalar_prefetch=1, grid=(1,), in_specs=[spec], out_specs=spec
        ),
        out_shape=jax.ShapeDtypeStruct(pieces.shape, BF16),
        name="restore",
    )(route, pieces)


def far_first(n):
    return sorted(range(1, n), key=lambda k: abs(k - n // 2))


def dispatch_kernel(n, x_ref, slot_ref, o_ref, slots_ref, send, recv, ssend, srecv, fsend, frecv):
    dp, me = lax.axis_index("dp"), lax.axis_index("seq")
    partner = (dp, 1 - me)
    barrier = pltpu.get_barrier_semaphore()
    for k in range(1, n):
        pl.semaphore_signal(barrier, inc=1, device_id=((dp + k) % n, me), device_id_type=MESH)
    pl.semaphore_signal(barrier, inc=1, device_id=partner, device_id_type=MESH)
    pl.semaphore_wait(barrier, n)

    order = far_first(n)
    copies, small = {}, {}
    for k in order:
        p = (dp + k) % n
        copies[k] = push(x_ref.at[p], o_ref.at[me, dp], send.at[k], recv.at[k], (p, me))
        copies[k].start()
        small[k] = push(slot_ref.at[p], slots_ref.at[me, dp], ssend.at[k], srecv.at[k], (p, me))
        small[k].start()
    forwards = [push(x_ref.at[dp], o_ref.at[me, dp], fsend.at[0], frecv.at[0], partner)]
    forwards[0].start()
    o_ref[me, dp] = x_ref[dp]
    slots_ref[me, dp] = slot_ref[dp]
    for k in order:
        s = (dp + n - k) % n
        copies[k].wait_recv()
        forward = push(o_ref.at[me, s], o_ref.at[me, s], fsend.at[k], frecv.at[k], partner)
        forward.start()
        forwards.append(forward)
    for k in order:
        small[k].wait_recv()
    last = push(slots_ref.at[me], slots_ref.at[me], fsend.at[n], frecv.at[n], partner)
    last.start()
    forwards.append(last)
    for k in order:
        copies[k].wait_send()
        small[k].wait_send()
    for forward in forwards:
        forward.wait()


def dispatch(outgoing, slots, collective_id):
    n = outgoing.shape[0]
    vmem = pl.BlockSpec(memory_space=VMEM)
    return pl.pallas_call(
        functools.partial(dispatch_kernel, n),
        out_shape=[
            jax.ShapeDtypeStruct((2,) + outgoing.shape, BF16),
            jax.ShapeDtypeStruct((2,) + slots.shape, jnp.int32),
        ],
        in_specs=[vmem] * 2,
        out_specs=[vmem] * 2,
        scratch_shapes=[pltpu.SemaphoreType.DMA((n,))] * 4 + [pltpu.SemaphoreType.DMA((n + 1,))] * 2,
        compiler_params=pltpu.CompilerParams(collective_id=collective_id, has_side_effects=True),
        name="dispatch",
    )(outgoing, slots)


def push(src, dst, send, recv, device):
    return pltpu.make_async_remote_copy(
        src_ref=src, dst_ref=dst, send_sem=send, recv_sem=recv,
        device_id=device, device_id_type=MESH,
    )


def meet(peers):
    barrier = pltpu.get_barrier_semaphore()
    for peer in peers:
        pl.semaphore_signal(barrier, inc=1, device_id=peer, device_id_type=MESH)
    pl.semaphore_wait(barrier, len(peers))


def chip_links(send, recv):
    dp, me = lax.axis_index("dp"), lax.axis_index("seq")
    axes = []
    for w in (1 + me, 2 - me):
        bit = (dp // w) % 2
        axes.append(((dp + (1 - 2 * bit) * w, me), bit))
    return {
        "dp": dp,
        "me": me,
        "z": dp // 4,
        "partner": (dp, 1 - me),
        "axes": axes,
        "stack": [((dp + 4 * k) % 16, me) for k in range(1, 4)],
        "send": send,
        "recv": recv,
    }


def square_blocks(sources, targets):
    for source, target in zip(sources, targets):
        tall, wide = source.shape
        for r in range(tall // D):
            for c in range(wide // D):
                at = (pl.ds(r * D, D), pl.ds(c * D, D))
                yield source.at[at], target.at[at]


class Chunk:
    def __init__(self, env, number, source, full, acc, landing, shared):
        self.env, self.number, self.shared = env, number, shared
        self.source, self.full, self.acc, self.landing = source, full, acc, landing
        base, size, offset = 0, source.shape[0], 0
        self.levels = []
        for device, bit in ([(env["partner"], env["me"])] if shared else []) + env["axes"]:
            half = size // 2
            keep, give = base + bit * half, base + (1 - bit) * half
            self.levels.append((device, keep, give, half, offset))
            base, size, offset = keep, half, offset + half
        self.base, self.size, self.offset = base, size // 4, offset

    def copy(self, stage, src, dst, device):
        e = self.env
        return push(src, dst, e["send"].at[self.number, stage], e["recv"].at[self.number, stage], device)

    def at(self, ref, start, size):
        return ref.at[pl.ds(start if isinstance(start, int) else pl.multiple_of(start, 16), size), :]

    def halves(self, level):
        device, _, give, half, offset = self.levels[level]
        src = self.acc if level else self.source
        return [self.copy(level, self.at(src, give, half), self.at(self.landing, offset, half), device)]

    def add(self, level):
        _, keep, _, half, offset = self.levels[level]
        src = self.acc if level else self.source
        step = min(half, 64)

        def run(i, _):
            here = pl.ds(pl.multiple_of(keep + i * step, 16), step)
            there = pl.ds(pl.multiple_of(offset + i * step, 16), step)
            total = src[here, :].astype(F32) + self.landing[there, :].astype(F32)
            self.acc[here, :] = total.astype(BF16)
            return 0

        lax.fori_loop(0, half // step, run, 0)

    def quarters(self):
        copies = []
        for k in range(1, 4):
            z = (self.env["z"] + k) % 4
            copies.append(
                self.copy(
                    len(self.levels) + k - 1,
                    self.at(self.acc, self.base + z * self.size, self.size),
                    self.at(self.landing, self.offset + (k - 1) * self.size, self.size),
                    self.env["stack"][k - 1],
                )
            )
        return copies

    def total(self):
        here = pl.ds(pl.multiple_of(self.base + self.env["z"] * self.size, 16), self.size)
        total = self.acc[here, :].astype(F32)
        for k in range(3):
            there = slice(self.offset + k * self.size, self.offset + (k + 1) * self.size)
            total += self.landing[there, :].astype(F32)
        self.full[here, :] = total.astype(BF16)

    def gathers(self):
        region = self.at(self.full, self.base + self.env["z"] * self.size, self.size)
        first = len(self.levels) + 3
        return [self.copy(first + k, region, region, self.env["stack"][k]) for k in range(3)]

    def spread(self, level):
        device, keep, _, half, _ = self.levels[level]
        region = self.at(self.full, keep, half)
        return [self.copy(len(self.levels) + 6 + level, region, region, device)]

    def hand_over(self):
        return [self.copy(2 * len(self.levels) + 6, self.full, self.full, self.env["partner"])]

    def steps(self):
        count = len(self.levels)
        stages = [functools.partial(self.halves, n) for n in range(count)] + [self.quarters, self.gathers]
        stages += [functools.partial(self.spread, n) for n in range(count - 1, -1, -1)]
        between = [functools.partial(self.add, n) for n in range(count)] + [self.total]
        if not self.shared:
            stages.append(self.hand_over)

        def step(n):
            if n > 0:
                for copy in stages[n - 1]():
                    copy.wait()
                if n - 1 < len(between):
                    between[n - 1]()
            if n < len(stages):
                for copy in stages[n]():
                    copy.start()

        return [functools.partial(step, n) for n in range(len(stages) + 1)]


def body(
    tokens,
    route,
    lengths,
    query_weight,
    query_bias,
    key_weight,
    value_weight,
    value_bias,
    output_weight,
    output_bias,
    first_gain,
    first_shift,
    up_weight,
    up_bias,
    down_weight,
    down_bias,
    second_gain,
    second_shift,
    cotangent,
):
    groups = lax.axis_size("dp")
    rows = tokens.shape[0]
    piece = rows // groups
    span = rows * lax.axis_size("seq")
    seq = lax.axis_index("seq")
    tables = lengths[0]
    me = seq.reshape(1).astype(jnp.int32)
    kernels = groups == 16 and piece % 16 == 0
    if kernels:
        pieces = 2 * groups
        outgoing, slots_out = arrange(tokens.reshape(groups, piece, D), route)
        x_all, slots_all = dispatch(outgoing, slots_out, 0)
        x_all = x_all.reshape(span, D)
        slots = slots_all[:, :, 0, 0].reshape(pieces)
    else:
        pieces = 0
        target = route // groups // lax.axis_size("seq")
        place = route % groups
        outgoing = jnp.zeros((groups, piece, D), BF16).at[target].set(tokens.reshape(groups, piece, D))
        slots_out = jnp.zeros((groups,), jnp.int32).at[target].set(place)
        incoming, slots = (
            lax.all_to_all(outgoing, "dp", split_axis=0, concat_axis=0, tiled=True),
            lax.all_to_all(slots_out, "dp", split_axis=0, concat_axis=0, tiled=True),
        )
        inputs = jnp.zeros_like(incoming).at[slots].set(incoming).reshape(rows, D)
        x_all = swap(inputs, (span, D), 0)
    x_turned, q, k, v, mixed_all, attend_out, lse, inputs = attend_forward(
        x_all, pieces, tables, me, slots,
        query_weight, key_weight, value_weight, query_bias, value_bias,
    )
    mixed = swap(mixed_all, (rows, D), 1)
    branch = product(mixed, output_weight) + output_bias
    residual = inputs.astype(F32) + branch
    first, first_back = jax.vjp(
        norm_rows, residual, first_gain.astype(F32), first_shift.astype(F32)
    )
    first_low = first.astype(BF16)
    hidden = product(first_low, up_weight) + up_bias
    active = gelu_exact(hidden).astype(BF16)
    update = product(active, down_weight) + down_bias
    layer_out, second_back = jax.vjp(
        norm_rows, first + update, second_gain.astype(F32), second_shift.astype(F32)
    )
    grad_second, grad_second_gain, grad_second_shift = second_back(cotangent.astype(F32))
    grad_update = grad_second.astype(BF16)
    again = product(first_low, up_weight) + up_bias
    active_again, gelu_back = jax.vjp(gelu_exact, again)
    active_low = active_again.astype(BF16)
    grad_down = product_left(active_low, grad_update)
    grad_down_bias = column_sums(grad_update)
    (grad_active,) = gelu_back(product_right(grad_update, down_weight))
    grad_hidden = grad_active.astype(BF16)
    grad_up = product_left(first_low, grad_hidden)
    grad_up_bias = column_sums(grad_hidden)
    grad_first = grad_second + product_right(grad_hidden, up_weight)
    grad_residual, grad_first_gain, grad_first_shift = first_back(grad_first)
    grad_branch = grad_residual.astype(BF16)
    grad_output = product_left(mixed, grad_branch)
    grad_output_bias = column_sums(grad_branch)
    grad_mixed = product_right(grad_branch, output_weight).astype(BF16)
    vec = jnp.concatenate(
        [
            jnp.zeros((2, D), F32),
            jnp.stack(
                [
                    grad_output_bias,
                    grad_first_gain,
                    grad_first_shift,
                    grad_down_bias,
                    grad_second_gain,
                    grad_second_shift,
                ]
            ),
            grad_up_bias.reshape(-1, D),
            jnp.zeros((4, D), F32),
        ]
    )
    shared = (tables, slots, pieces, x_turned, q, k, v)
    rest = (attend_out, lse, query_weight, key_weight, value_weight, grad_residual)
    if kernels:
        raw = [a.astype(BF16) for a in (grad_up, grad_down, grad_output)]
        up_sum, down_sum, out_sum, back, columns, vec = attend_backward(
            *shared, grad_mixed, *rest, raw, vec, 3
        )
        token_grad = restore(back.reshape(groups, piece, D), route).reshape(rows, D)
        up_sum, down_sum, out_sum = (a.astype(F32) for a in (up_sum, down_sum, out_sum))
        columns = jnp.concatenate([columns[0], columns[1]], axis=2).astype(F32)
    else:
        grad_mixed_all = swap(grad_mixed, (span, C), 2)
        grad_columns, parts, grad_own, grad_other = attend_backward(
            *shared, grad_mixed_all, *rest, [], vec, 3
        )
        parts = parts.reshape(2, C)
        vec = vec + lax.dynamic_update_slice(jnp.zeros_like(vec), parts, (0, seq * C))
        both = swap(grad_other, (span, D), 5).reshape(2, rows, D)
        grad_inputs = grad_own + both[1 - seq].astype(F32)
        back_rows = grad_inputs.astype(BF16).reshape(groups, piece, D)[slots]
        returned = lax.all_to_all(back_rows, "dp", split_axis=0, concat_axis=0, tiled=True)
        token_grad = returned[target].reshape(rows, D)
        up_sum, down_sum, out_sum, vec = lax.psum((grad_up, grad_down, grad_output, vec), ("dp", "seq"))
        columns = lax.psum(grad_columns.astype(F32), "dp")
        columns = lax.all_gather(columns, "seq", axis=2, tiled=True)
    query_sum, key_sum, value_sum = columns[0], columns[1], columns[2]
    return (
        layer_out.astype(BF16),
        token_grad,
        query_sum,
        vec[0],
        key_sum,
        value_sum,
        vec[1],
        out_sum,
        vec[2],
        vec[3],
        vec[4],
        up_sum,
        vec[8:12].reshape(-1),
        down_sum,
        vec[5],
        vec[6],
        vec[7],
    )


def solution(mesh):
    both, one = P(("dp", "seq"), None), P()
    return jax.shard_map(
        body,
        mesh=mesh,
        in_specs=(both, P(("dp", "seq")), P("dp", None)) + (one,) * 15 + (both,),
        out_specs=(both, both) + (one,) * 15,
        check_vma=False,
    )
```

```python
import functools

import jax
import jax.numpy as jnp
from jax import lax
from jax.experimental import pallas as pl
from jax.experimental.pallas import tpu as pltpu
from jax.sharding import PartitionSpec as P

D = 512
HEADS = 8
HEAD = 64
HL = HEADS // 2
C = HL * HEAD
PAIR = 128
NEG = -1e30
LOG2E = 1.4426950408889634
BQ = 256
BK = 256
BR = 128
PACE = 1.2
F32 = jnp.float32
BF16 = jnp.bfloat16
MESH = pl.DeviceIdType.MESH
VMEM = pltpu.VMEM
SMEM = pltpu.SMEM


ERFC_RATE = 0.38
ERFC = (
    0.214409851453,
    0.213944088337,
    0.203688192149,
    0.139667636356,
    0.227252140359,
    -0.1568920127,
    0.359389202242,
    -0.259886715084,
    0.0584276049124,
)


def gelu_and_slope(value):
    bell = jnp.exp(-0.5 * value * value)
    t = 1.0 / (1.0 + (ERFC_RATE * 0.5**0.5) * jnp.abs(value))
    tail = ERFC[-1]
    for c in ERFC[-2::-1]:
        tail = tail * t + c
    tail = (0.5 * bell) * (tail * t)
    share = jnp.where(value < 0, tail, 1.0 - tail)
    return value * share, share + value * bell * 0.3989422804014327


def product(left, right):
    return jnp.dot(left, right, preferred_element_type=F32)


def product_left(left, right):
    return lax.dot_general(left, right, (((0,), (0,)), ((), ())), preferred_element_type=F32)


def product_right(left, right):
    return lax.dot_general(left, right, (((1,), (1,)), ((), ())), preferred_element_type=F32)


def swap_kernel(x_ref, o_ref, send, recv, local):
    dp, me = lax.axis_index("dp"), lax.axis_index("seq")
    other = 1 - me
    barrier = pltpu.get_barrier_semaphore()
    pl.semaphore_signal(barrier, inc=1, device_id=(dp, other), device_id_type=MESH)
    pl.semaphore_wait(barrier, 1)
    rows, width = o_ref.shape
    if x_ref.shape == (2 * rows, width // 2):
        target = o_ref.at[:, pl.ds(pl.multiple_of(me * (width // 2), width // 2), width // 2)]
        sources = [x_ref.at[pl.ds(pl.multiple_of(d * rows, rows), rows), :] for d in (other, me)]
    elif x_ref.shape == (rows // 2, 2 * width):
        target = o_ref.at[pl.ds(pl.multiple_of(me * (rows // 2), rows // 2), rows // 2), :]
        sources = [x_ref.at[:, pl.ds(pl.multiple_of(d * width, width), width)] for d in (other, me)]
    else:
        target = o_ref.at[pl.ds(pl.multiple_of(me * (rows // 2), rows // 2), rows // 2), :]
        sources = [x_ref, x_ref]
    copy = push(sources[0], target, send, recv, (dp, other))
    copy.start()
    own = pltpu.make_async_copy(sources[1], target, local)
    own.start()
    own.wait()
    copy.wait()


def swap(x, shape, collective_id):
    return pl.pallas_call(
        swap_kernel,
        out_shape=jax.ShapeDtypeStruct(shape, x.dtype),
        in_specs=[pl.BlockSpec(memory_space=VMEM)],
        out_specs=pl.BlockSpec(memory_space=VMEM),
        scratch_shapes=[pltpu.SemaphoreType.DMA] * 3,
        compiler_params=pltpu.CompilerParams(collective_id=collective_id, has_side_effects=True),
    )(x)


def rotation(len_ref, span):
    lengths = [len_ref[j] for j in range(len_ref.shape[0])]
    longest = functools.reduce(jnp.maximum, lengths)
    shift, total, ends = jnp.int32(0), jnp.int32(0), []
    for length in lengths:
        shift = jnp.where(length == longest, total, shift)
        total = total + length
        ends.append(total)
    turned = [e - shift for e in ends]
    return shift, [jnp.where(e <= 0, e + span, e) for e in turned]


def rows_from(ref, start, count):
    base = lax.div(start, 8) * 8
    r = start - base
    x = ref[pl.ds(base, count + 8), :]
    width = x.shape[1]
    row = lax.broadcasted_iota(jnp.int32, (1, 8, 1), 1)
    for bit in (1, 2, 4):
        by_eights = x.reshape(x.shape[0] // 8, 8, width)
        turned = pltpu.roll(by_eights, 8 - bit, axis=1)
        following = jnp.concatenate([turned[1:], turned[:1]], axis=0)
        moved = jnp.where(row < 8 - bit, turned, following).reshape(x.shape)
        x = jnp.where(jnp.full(x.shape, r & bit) != 0, moved, x)
    return x[:count]


def table_of(ends, position):
    start, end = jnp.zeros_like(position), jnp.full_like(position, 1 << 30)
    for e in ends:
        start = jnp.where(e <= position, jnp.maximum(start, e), start)
        end = jnp.where(e > position, jnp.minimum(end, e), end)
    return start, end


def tile_mask(ends, i):
    return table_of(ends, i * BQ + lax.broadcasted_iota(jnp.int32, (1, BQ), 1))


def head_masks():
    lane = lax.broadcasted_iota(jnp.int32, (1, PAIR), 1)
    low = (lane < HEAD).astype(F32).astype(BF16)
    return low, (lane >= HEAD).astype(F32).astype(BF16)


def by_eight(value, op):
    return op(value.reshape(value.shape[0] // 8, 8, value.shape[1]), axis=0)


def forward_kernel(
    pieces, len_ref, me_ref, slot_ref, loaded_ref, wq_ref, wk_ref, wv_ref, bq_ref, bv_ref,
    x_ref, q_ref, k_ref, v_ref, mixed_ref, out_ref, lse_ref, own_ref,
    vt_ref, acc_ref, s_ref, packed_ref, turned_ref,
):
    span = loaded_ref.shape[0]
    half, blocks = span // 2, span // BQ
    near = blocks // 2
    shift, ends = rotation(len_ref, span)
    count = pieces if pieces else 32
    piece = span // count

    def place(k, _):
        slot = slot_ref[k] if pieces else k % (count // 2)
        row = (k // (count // 2)) * half + slot * piece
        packed_ref[pl.ds(pl.multiple_of(row, piece), piece), :] = loaded_ref[
            pl.ds(pl.multiple_of(k * piece, piece), piece), :
        ].astype(F32)
        return 0

    lax.fori_loop(0, count, place, 0)
    packed_ref[span:, :] = packed_ref[: BQ + 8, :]
    own_ref[...] = packed_ref[pl.ds(pl.multiple_of(me_ref[0] * half, half), half), :].astype(BF16)

    def project(i, _):
        rows = pl.ds(pl.multiple_of(i * BQ, BQ), BQ)
        x = rows_from(packed_ref, lax.rem(i * BQ + shift, span), BQ).astype(BF16)
        x_ref[rows, :] = x
        q = (product(x, wq_ref[...]) + bq_ref[...].astype(F32)).astype(BF16)
        q_ref[rows, :] = (q.astype(F32) * (HEAD**-0.5)).astype(BF16)
        k_ref[rows, :] = product(x, wk_ref[...]).astype(BF16)
        v = (product(x, wv_ref[...]) + bv_ref[...].astype(F32)).astype(BF16)
        v_ref[rows, :] = v
        vt_ref[:, rows] = v.T
        return 0

    lax.fori_loop(0, blocks, project, 0)
    masks = head_masks()

    def query_block(masked, i, _):
        rows = pl.ds(pl.multiple_of(i * BQ, BQ), BQ)
        base = near if masked else 0
        if masked:
            start, end = tile_mask(ends, i)
        q = q_ref[rows, :]
        heads = [q[:, (h // 2) * PAIR : (h // 2 + 1) * PAIR] * masks[h % 2] for h in range(HL)]
        acc_ref[...] = jnp.zeros_like(acc_ref)

        def score_block(j, tops):
            keys = pl.ds(pl.multiple_of((base + j) * BK, BK), BK)
            if masked:
                kpos = (base + j) * BK + lax.broadcasted_iota(jnp.int32, (BK, BQ), 0)
                mask = (kpos >= start) & (kpos < end)
            new = []
            for h in range(HL):
                kp = k_ref[keys, (h // 2) * PAIR : (h // 2 + 1) * PAIR]
                s = product_right(kp, heads[h]) * LOG2E
                if masked:
                    s = jnp.where(mask, s, NEG)
                s_ref[h, pl.ds(pl.multiple_of(j * BK, BK), BK), :] = s
                new.append(jnp.maximum(tops[h], by_eight(s, jnp.max)))
            return tuple(new)

        tops = lax.fori_loop(
            0, near, score_block, tuple(jnp.full((8, BQ), NEG, F32) for _ in range(HL))
        )
        tops = [jnp.max(t, axis=0, keepdims=True) for t in tops]

        def mix_block(j, totals):
            keys = pl.ds(pl.multiple_of((base + j) * BK, BK), BK)
            new = []
            for h in range(HL):
                p = jnp.exp2(s_ref[h, pl.ds(pl.multiple_of(j * BK, BK), BK), :] - tops[h])
                new.append(totals[h] + by_eight(p, jnp.sum))
                lanes = slice(h * HEAD, (h + 1) * HEAD)
                acc_ref[lanes, :] += product(vt_ref[lanes, keys], p.astype(BF16))
            return tuple(new)

        totals = lax.fori_loop(
            0, near, mix_block, tuple(jnp.zeros((8, BQ), F32) for _ in range(HL))
        )
        for h in range(HL):
            total = jnp.sum(totals[h], axis=0, keepdims=True)
            lanes = slice(h * HEAD, (h + 1) * HEAD)
            acc_ref[lanes, :] = acc_ref[lanes, :] / total
            lse_ref[h : h + 1, rows] = tops[h] + jnp.log2(total)
        out = acc_ref[...]
        out_ref[:, rows] = out
        turned_ref[rows, :] = out.T
        return 0

    lax.fori_loop(0, near, functools.partial(query_block, False), 0)
    lax.fori_loop(near, blocks, functools.partial(query_block, True), 0)
    turned_ref[span:, :] = turned_ref[: BQ + 8, :]

    def turn_back(i, _):
        rows = pl.ds(pl.multiple_of(i * BQ, BQ), BQ)
        mixed_ref[rows, :] = rows_from(turned_ref, lax.rem(i * BQ + span - shift, span), BQ).astype(BF16)
        return 0

    lax.fori_loop(0, blocks, turn_back, 0)


def column_block(shape):
    return pl.BlockSpec(shape, lambda i, lengths, me, slots: (0, me[0]))


def whole_block(shape):
    return pl.BlockSpec(shape, lambda i, lengths, me, slots: (0,) * len(shape))


def attend_forward(x_all, pieces, lengths, me, slots, wq, wk, wv, bq, bv):
    span = x_all.shape[0]
    rows_shape = jax.ShapeDtypeStruct((span, C), BF16)
    return pl.pallas_call(
        functools.partial(forward_kernel, pieces),
        grid_spec=pltpu.PrefetchScalarGridSpec(
            num_scalar_prefetch=3,
            grid=(1,),
            in_specs=[
                whole_block((span, D)),
                column_block((D, C)),
                column_block((D, C)),
                column_block((D, C)),
                column_block((1, C)),
                column_block((1, C)),
            ],
            out_specs=[whole_block((span, D))] + [whole_block((span, C))] * 4
            + [whole_block((C, span)), whole_block((8, span)), whole_block((span // 2, D))],
            scratch_shapes=[
                VMEM((C, span), BF16),
                VMEM((C, BQ), F32),
                VMEM((HL, span // 2, BQ), F32),
                VMEM((span + BQ + 8, D), F32),
                VMEM((span + BQ + 8, C), F32),
            ],
        ),
        out_shape=[jax.ShapeDtypeStruct((span, D), BF16)] + [rows_shape] * 4
        + [jax.ShapeDtypeStruct((C, span), F32), jax.ShapeDtypeStruct((8, span), F32)]
        + [jax.ShapeDtypeStruct((span // 2, D), BF16)],
        name="attend_forward",
    )(lengths, me, slots, x_all, wq, wk, wv, bq.reshape(1, D), bv.reshape(1, D))


def backward_kernel(pieces, sums, *refs):
    len_ref, slot_ref, x_ref, q_ref, k_ref, v_ref, g_ref, out_ref, lse_ref = refs[:9]
    weights, res_ref = refs[9:12], refs[12]
    refs = refs[13:]
    if sums:
        raw, vec_ref = refs[:3], refs[3]
        full, back_ref, qkv_full, vec_full = refs[4:7], refs[7], refs[8], refs[9]
        refs = refs[10:]
    gw_ref, sums_ref, ga_ref, gb_ref = refs[:4]
    refs = refs[4:]
    kt_ref, gq_ref, gk_ref, gv_ref, gqt_ref, qs_ref, gs_ref, w_ref, ds_ref = refs[:9]
    term_ref, turned_ref, gx_ref = refs[9:12]
    me = lax.axis_index("seq")
    span = x_ref.shape[0]
    half, blocks = span // 2, span // BQ
    near = blocks // 2
    scale = HEAD**-0.5
    columns = pl.ds(pl.multiple_of(me * C, C), C)
    ticks = []
    if sums:
        acc_ref, landing_ref, acc_own, landing_own, gbr_ref, arrived_ref, vec_recv = refs[12:19]
        send, recv, asend, arecv, gsend, grecv, vsend, vrecv = refs[19:]
        env = chip_links(send, recv)
        dp, partner = env["dp"], env["partner"]
        meet([(lax.rem(dp + k, 16), me) for k in range(1, 16)] + [partner])
        cross = push(
            g_ref.at[:, pl.ds(pl.multiple_of((1 - me) * C, C), C)], arrived_ref,
            gsend.at[4], grecv.at[4], partner,
        )
        cross.start()
        lines = [
            Chunk(env, c, source, target, acc_ref.at[c], landing_ref.at[c], True).steps()
            for c, (source, target) in enumerate(square_blocks(raw, full))
        ]
        for c, line in enumerate(lines):
            for j, step in enumerate(line):
                at = int((c + 2 * j) * PACE)
                ticks += [[] for _ in range(at + 1 - len(ticks))]
                ticks[at].append(step)

    def tick(now, candidates):
        for t in candidates:
            if t < len(ticks) and ticks[t]:

                @pl.when(now == t)
                def _(t=t):
                    for step in ticks[t]:
                        step()

    def straight(t):
        for step in ticks[t] if t < len(ticks) else []:
            step()

    straight(0)
    shift, ends = rotation(len_ref, span)

    def prepare(i, _):
        rows = pl.ds(pl.multiple_of(i * BQ, BQ), BQ)
        kt_ref[:, rows] = k_ref[rows, :].T
        gk_ref[rows, :] = jnp.zeros((BQ, C), F32)
        gv_ref[rows, :] = jnp.zeros((BQ, C), F32)
        if not sums:
            turned_ref[rows, :] = g_ref[rows, :].astype(F32)
        return 0

    lax.fori_loop(0, blocks, prepare, 0)
    if sums:
        turned_ref[pl.ds(pl.multiple_of(me * half, half), half), :] = g_ref[:, columns].astype(F32)
        cross.wait()
        turned_ref[pl.ds(pl.multiple_of((1 - me) * half, half), half), :] = arrived_ref[...].astype(F32)
    turned_ref[span:, :] = turned_ref[: BQ + 8, :]
    straight(1)
    lane = lax.broadcasted_iota(jnp.int32, (1, C), 1) // HEAD
    masks = [(lane == h).astype(F32).astype(BF16) for h in range(HL)]

    def query_block(masked, i, _):
        rows = pl.ds(pl.multiple_of(i * BQ, BQ), BQ)
        base = near if masked else 0
        if masked:
            start, end = tile_mask(ends, i)
        q = q_ref[rows, :]
        exact = rows_from(turned_ref, lax.rem(i * BQ + shift, span), BQ)
        g = exact.astype(BF16)
        for h in range(HL):
            part = slice(h * BQ, (h + 1) * BQ)
            qs_ref[part, :] = q * masks[h]
            gs_ref[part, :] = g * masks[h]
        weighted = exact.T * out_ref[:, rows]
        inner = [
            jnp.sum(weighted[h * HEAD : (h + 1) * HEAD], axis=0, keepdims=True) for h in range(HL)
        ]
        logsum = [lse_ref[h : h + 1, rows] for h in range(HL)]
        gqt_ref[...] = jnp.zeros_like(gqt_ref)

        def key_block(j, _):
            keys = pl.ds(pl.multiple_of((base + j) * BK, BK), BK)
            here = pl.ds(pl.multiple_of(j * BK, BK), BK)
            if masked:
                kpos = (base + j) * BK + lax.broadcasted_iota(jnp.int32, (BK, BQ), 0)
                mask = (kpos >= start) & (kpos < end)
            for h in range(HL):
                part = slice(h * BQ, (h + 1) * BQ)
                pair = slice((h // 2) * PAIR, (h // 2 + 1) * PAIR)
                s = product_right(k_ref[keys, pair], qs_ref[part, pair])
                w = jnp.exp2(s * LOG2E - logsum[h])
                if masked:
                    w = jnp.where(mask, w, 0.0)
                gw = product_right(v_ref[keys, pair], gs_ref[part, pair])
                gs = (w * (gw - inner[h])).astype(BF16)
                w_ref[here, part] = w.astype(BF16)
                ds_ref[here, part] = gs
            return 0

        def product_block(j, _):
            keys = pl.ds(pl.multiple_of((base + j) * BK, BK), BK)
            here = pl.ds(pl.multiple_of(j * BK, BK), BK)
            for h in range(HL):
                part = slice(h * BQ, (h + 1) * BQ)
                lanes = slice(h * HEAD, (h + 1) * HEAD)
                gqt_ref[lanes, :] += product(kt_ref[lanes, keys], ds_ref[here, part])
            gv_ref[keys, :] += product(w_ref[here, :], gs_ref[...])
            gk_ref[keys, :] += product(ds_ref[here, :], qs_ref[...])
            return 0

        first = 2 + 2 * base
        lax.fori_loop(0, near, key_block, 0)
        tick(2 + 2 * i, range(first, first + 2 * near, 2))
        lax.fori_loop(0, near, product_block, 0)
        gq_ref[rows, :] = (gqt_ref[...].T * scale).astype(BF16)
        tick(3 + 2 * i, range(first + 1, first + 2 * near, 2))
        return 0

    lax.fori_loop(0, near, functools.partial(query_block, False), 0)
    lax.fori_loop(near, blocks, functools.partial(query_block, True), 0)

    after = 2 + 2 * blocks
    term_ref[...] = jnp.zeros_like(term_ref)
    sums_ref[...] = jnp.zeros_like(sums_ref)

    def gradients(i, _):
        rows = pl.ds(pl.multiple_of(i * BQ, BQ), BQ)
        parts = [gq_ref[rows, :], gk_ref[rows, :].astype(BF16), gv_ref[rows, :].astype(BF16)]
        x = x_ref[rows, :]
        for n, part in enumerate(parts):
            term_ref[n] += product_left(x, part)
        sums_ref[...] += jnp.concatenate(
            [jnp.sum(a.astype(F32), axis=0, keepdims=True) for a in (parts[0], parts[2])], axis=1
        )
        gx_ref[rows, :] = (
            product_right(parts[0], weights[0][:, columns])
            + product_right(parts[1], weights[1][:, columns])
            + product_right(parts[2], weights[2][:, columns])
        )
        tick(after + i, range(after, after + blocks))
        return 0

    lax.fori_loop(0, blocks, gradients, 0)
    gw_ref[...] = term_ref[...].astype(BF16)
    count = pieces if pieces else 32
    each = count // 2
    piece = span // count
    gx_ref[span:, :] = gx_ref[: piece + 8, :]

    def piece_rows(part, k):
        row = (slot_ref[part * each + k] if pieces else k) * piece
        return rows_from(gx_ref, lax.rem(part * half + row + span - shift, span), piece), row

    def own_piece(k, _):
        gx, row = piece_rows(me, k)
        here = pl.ds(pl.multiple_of(k * piece, piece), piece)
        gx = gx + res_ref[pl.ds(row, piece), :]
        if sums:
            ga_ref[here, :] = (gx + gbr_ref[here, :].astype(F32)).astype(BF16)
        else:
            ga_ref[here, :] = gx
        return 0

    def other_piece(k, _):
        gx, _ = piece_rows(1 - me, k)
        gb_ref[pl.ds(pl.multiple_of(k * piece, piece), piece), :] = gx.astype(BF16)
        return 0

    if not sums:
        lax.fori_loop(0, each, own_piece, 0)
        lax.fori_loop(0, each, other_piece, 0)
        return

    lines = [
        Chunk(
            env, 9 + c, gw_ref.at[c], qkv_full.at[me, c], acc_own.at[c], landing_own.at[c], False
        ).steps()
        for c in range(3)
    ]
    peers = [partner]
    for w in (1, 2, 4, 8):
        bit = (dp // w) % 2
        peers.append((dp + (1 - 2 * bit) * w, me))

    def vec_copy(s):
        return push(vec_recv.at[len(peers) + s], vec_recv.at[s], vsend.at[s], vrecv.at[s], peers[s])

    def vec_step(s):
        if s == 0:
            vec_full[...] = vec_ref[...]
            vec_full[0:1, columns] = sums_ref[:, :C]
            vec_full[1:2, columns] = sums_ref[:, C:]
        else:
            vec_copy(s - 1).wait()
            vec_full[...] += vec_recv[s - 1]
        if s < len(peers):
            vec_recv[len(peers) + s] = vec_full[...]
            vec_copy(s).start()

    lines.append([functools.partial(vec_step, s) for s in range(len(peers) + 1)])
    left = [ticks[t] for t in range(after + blocks, len(ticks))]
    queue = [
        (left[n] if n < len(left) else []) + [line[n] for line in lines if n < len(line)]
        for n in range(max([len(left)] + [len(line) for line in lines]))
    ]

    def advance():
        for step in queue.pop(0) if queue else []:
            step()

    floor, place = env["z"], lax.rem(dp, 4)
    order = (2, 1, 3, 0)
    plane = 4 * piece

    def across(k):
        here = pl.ds(pl.multiple_of(lax.rem(floor + k, 4) * plane, plane), plane)
        return push(gb_ref.at[here, :], gbr_ref.at[here, :], gsend.at[k], grecv.at[k], partner)

    advance()
    for k in order:
        first = lax.rem(floor + k, 4) * 4
        lax.fori_loop(first, first + 4, other_piece, 0)
        across(k).start()
    advance()
    mine = pl.ds(pl.multiple_of(dp * piece, piece), piece)
    returns = []
    for k in order:
        first = lax.rem(floor + k, 4) * 4
        across(k).wait()
        lax.fori_loop(first, first + 4, own_piece, 0)
        for i in range(4):
            if k == 0 and i == 0:
                back_ref[mine, :] = ga_ref[mine, :]
                continue
            p = first + lax.rem(place + i, 4)
            theirs = pl.ds(pl.multiple_of(p * piece, piece), piece)
            n = 4 * k + i
            copy = push(ga_ref.at[theirs, :], back_ref.at[mine, :], asend.at[n], arecv.at[n], (p, me))
            copy.start()
            returns.append(copy)
        advance()
    while queue:
        advance()
    for copy in returns:
        copy.wait()


def attend_backward(lengths, slots, pieces, x, q, k, v, g, out, lse, wq, wk, wv, res, raw, vec, collective_id):
    span = x.shape[0]
    half = span // 2
    vmem, smem = pl.BlockSpec(memory_space=VMEM), pl.BlockSpec(memory_space=SMEM)
    shape = jax.ShapeDtypeStruct
    sums = len(raw) > 0
    dma = pltpu.SemaphoreType.DMA
    results = [
        ((3, D, C), BF16),
        ((1, 2 * C), F32),
        ((half, D), BF16 if sums else F32),
        ((half, D), BF16),
    ]
    outs = [shape(*r) for r in results]
    operands = (lengths, slots, x, q, k, v, g, out, lse, wq, wk, wv, res)
    before, comm, params = [], [], {}
    if sums:
        chunks = sum(a.size for a in raw) // (D * D)
        outs = [shape(a.shape, BF16) for a in raw]
        outs += [shape((half, D), BF16), shape((2, 3, D, C), BF16), shape(vec.shape, F32)]
        before = [VMEM(*r) for r in results]
        comm = [VMEM((chunks, D, D), BF16)] * 2 + [VMEM((3, D, C), BF16)] * 2
        comm += [VMEM((half, D), BF16), VMEM((half, C), BF16), VMEM((10,) + vec.shape, F32)]
        comm += [dma((chunks + 3, 13))] * 2 + [dma((16,))] * 2 + [dma((5,))] * 4
        params = dict(collective_id=collective_id, has_side_effects=True)
        operands += (*raw, vec)
    return pl.pallas_call(
        functools.partial(backward_kernel, pieces, sums),
        out_shape=outs,
        in_specs=[smem] * 2 + [vmem] * (len(operands) - 2),
        out_specs=[vmem] * len(outs),
        scratch_shapes=before
        + [
            VMEM((C, span), BF16),
            VMEM((span, C), BF16),
            VMEM((span, C), F32),
            VMEM((span, C), F32),
            VMEM((C, BQ), F32),
            VMEM((HL * BQ, C), BF16),
            VMEM((HL * BQ, C), BF16),
            VMEM((half, HL * BQ), BF16),
            VMEM((half, HL * BQ), BF16),
            VMEM((3, D, C), F32),
            VMEM((span + BQ + 8, C), F32),
            VMEM((span + span // (pieces if pieces else 32) + 8, D), F32),
        ]
        + comm,
        compiler_params=pltpu.CompilerParams(vmem_limit_bytes=63 << 20, **params),
        name="attend_backward",
    )(*operands)


def norm_forward(value):
    center = value - jnp.mean(value, axis=-1, keepdims=True)
    spread = jnp.mean(center * center, axis=-1, keepdims=True)
    rate = lax.rsqrt(spread + 1e-05)
    return center * rate, rate


def norm_backward(grad, unit, rate, gain):
    grad = grad * gain
    mean = jnp.mean(grad, axis=-1, keepdims=True)
    along = jnp.mean(grad * unit, axis=-1, keepdims=True)
    return rate * (grad - mean - unit * along)


def feed_kernel(
    mixed_ref, own_ref, cotangent_ref, wo_ref, wu_ref, wd_ref, bu_ref, bo_ref, g1_ref, s1_ref, bd_ref, g2_ref, s2_ref,
    out_ref, res_ref, gm_ref, up_ref, down_ref, outw_ref, vec_ref,
    first_ref, unit1_ref, rate1_ref, low_ref, act_ref, slope_ref, gu_ref, gs_ref, gh_ref, gb_ref,
    up_acc, down_acc, outw_acc,
):
    step, last = pl.program_id(0), pl.num_programs(0) - 1
    rows = mixed_ref.shape[0]
    wide = bu_ref.shape[1] // D
    bo, g1, s1, bd, g2, s2 = (
        r[...].astype(F32) for r in (bo_ref, g1_ref, s1_ref, bd_ref, g2_ref, s2_ref)
    )

    @pl.when(step == 0)
    def _():
        up_acc[...] = jnp.zeros_like(up_acc)
        down_acc[...] = jnp.zeros_like(down_acc)
        outw_acc[...] = jnp.zeros_like(outw_acc)
        vec_ref[...] = jnp.zeros_like(vec_ref)

    def total(value):
        return jnp.sum(value, axis=0, keepdims=True)

    def part(r):
        return pl.ds(pl.multiple_of(r * BR, BR), BR)

    def block(c):
        return pl.ds(pl.multiple_of(c * D, D), D)

    def project(r, _):
        here = part(r)
        branch = product(mixed_ref[here, :], wo_ref[...]) + bo
        unit, rate = norm_forward(own_ref[here, :].astype(F32) + branch)
        unit1_ref[here, :] = unit
        rate1_ref[here, :] = rate
        first = unit * g1 + s1
        first_ref[here, :] = first
        low_ref[here, :] = first.astype(BF16)
        return 0

    lax.fori_loop(0, rows // BR, project, 0)

    def widen(n, _):
        here, c = part(n // wide), block(n % wide)
        hidden = product(low_ref[here, :], wu_ref[:, c]) + bu_ref[:, c].astype(F32)
        active, slope = gelu_and_slope(hidden)
        act_ref[here, c] = active.astype(BF16)
        slope_ref[here, c] = slope
        return 0

    lax.fori_loop(0, rows // BR * wide, widen, 0)

    def narrow(r, sums):
        here = part(r)
        update = product(act_ref[here, :], wd_ref[...]) + bd
        unit, rate = norm_forward(first_ref[here, :] + update)
        out_ref[here, :] = (unit * g2 + s2).astype(BF16)
        cotangent = cotangent_ref[here, :].astype(F32)
        grad = norm_backward(cotangent, unit, rate, g2)
        gs_ref[here, :] = grad
        low = grad.astype(BF16)
        gu_ref[here, :] = low
        new = (total(low.astype(F32)), total(cotangent * unit), total(cotangent))
        return tuple(a + b for a, b in zip(sums, new))

    zero = jnp.zeros((1, D), F32)
    sums = lax.fori_loop(0, rows // BR, narrow, (zero,) * 3)
    for n, value in enumerate(sums):
        vec_ref[5 + n : 6 + n, :] += value

    def widen_back(n, _):
        here, c = part(n // wide), block(n % wide)
        grad = product_right(gu_ref[here, :], wd_ref[c, :]) * slope_ref[here, c]
        gh_ref[here, c] = grad.astype(BF16)
        return 0

    lax.fori_loop(0, rows // BR * wide, widen_back, 0)

    for c in range(wide):
        lanes = slice(c * D, (c + 1) * D)
        vec_ref[8 + c : 9 + c, :] += total(gh_ref[:, lanes].astype(F32))

    def weights(c, _):
        lanes = block(c)
        up_acc[:, lanes] += product_left(low_ref[...], gh_ref[:, lanes])
        down_acc[lanes, :] += product_left(act_ref[:, lanes], gu_ref[...])
        return 0

    lax.fori_loop(0, wide, weights, 0)

    def narrow_back(r, sums):
        here = part(r)
        grad = gs_ref[here, :] + product_right(gh_ref[here, :], wu_ref[...])
        unit = unit1_ref[here, :]
        residual = norm_backward(grad, unit, rate1_ref[here, :], g1)
        res_ref[here, :] = residual
        low = residual.astype(BF16)
        gb_ref[here, :] = low
        gm_ref[here, :] = product_right(low, wo_ref[...]).astype(BF16)
        new = (total(low.astype(F32)), total(grad * unit), total(grad))
        return tuple(a + b for a, b in zip(sums, new))

    sums = lax.fori_loop(0, rows // BR, narrow_back, (zero,) * 3)
    for n, value in enumerate(sums):
        vec_ref[2 + n : 3 + n, :] += value
    outw_acc[...] += product_left(mixed_ref[...], gb_ref[...])

    @pl.when(step == last)
    def _():
        up_ref[...] = up_acc[...].astype(BF16)
        down_ref[...] = down_acc[...].astype(BF16)
        outw_ref[...] = outw_acc[...].astype(BF16)


def feed(mixed, own, cotangent, wo, wu, wd, bu, *vectors):
    count = 2
    rows = mixed.shape[0] // count
    ff = wu.shape[1]
    shape = jax.ShapeDtypeStruct
    block = pl.BlockSpec((rows, D), lambda i: (i, 0))

    def whole(a):
        return pl.BlockSpec(a, lambda i: (0, 0))

    return pl.pallas_call(
        feed_kernel,
        grid=(count,),
        in_specs=[block] * 3 + [whole(a.shape) for a in (wo, wu, wd)] + [whole((1, ff))] + [whole((1, D))] * 6,
        out_specs=[block] * 3 + [whole(wu.shape), whole(wd.shape), whole(wo.shape), whole((16, D))],
        out_shape=[shape(mixed.shape, BF16), shape(mixed.shape, F32), shape(mixed.shape, BF16)]
        + [shape(a.shape, BF16) for a in (wu, wd, wo)]
        + [shape((16, D), F32)],
        scratch_shapes=[
            VMEM((rows, D), F32),
            VMEM((rows, D), F32),
            VMEM((rows, 1), F32),
            VMEM((rows, D), BF16),
            VMEM((rows, ff), BF16),
            VMEM((rows, ff), F32),
            VMEM((rows, D), BF16),
            VMEM((rows, D), F32),
            VMEM((rows, ff), BF16),
            VMEM((rows, D), BF16),
            VMEM(wu.shape, F32),
            VMEM(wd.shape, F32),
            VMEM(wo.shape, F32),
        ],
        name="feed",
    )(mixed, own, cotangent, wo, wu, wd, bu.reshape(1, ff), *(v.reshape(1, D) for v in vectors))


def arrange_kernel(groups, route_ref, x_ref, o_ref, slot_ref):
    for k in range(groups):
        packed = route_ref[k]
        group = packed // (2 * groups)
        o_ref[group] = x_ref[k]
        slot_ref[group] = jnp.full(slot_ref.shape[1:], packed % groups, jnp.int32)


def arrange(pieces, route):
    groups, piece, _ = pieces.shape
    return pl.pallas_call(
        functools.partial(arrange_kernel, groups),
        grid_spec=pltpu.PrefetchScalarGridSpec(
            num_scalar_prefetch=1,
            grid=(1,),
            in_specs=[pl.BlockSpec(pieces.shape, lambda i, r: (0, 0, 0))],
            out_specs=[
                pl.BlockSpec(pieces.shape, lambda i, r: (0, 0, 0)),
                pl.BlockSpec((groups, 8, 128), lambda i, r: (0, 0, 0)),
            ],
        ),
        out_shape=[
            jax.ShapeDtypeStruct(pieces.shape, BF16),
            jax.ShapeDtypeStruct((groups, 8, 128), jnp.int32),
        ],
        name="arrange",
    )(route, pieces)


def finish_kernel(route_ref, up, down, out, columns, back, up_o, down_o, out_o, q_o, k_o, v_o, back_o):
    up_o[...] = up[...].astype(F32)
    down_o[...] = down[...].astype(F32)
    out_o[...] = out[...].astype(F32)
    for n, ref in enumerate((q_o, k_o, v_o)):
        ref[:, :C] = columns[0, n].astype(F32)
        ref[:, C:] = columns[1, n].astype(F32)
    back_o[...] = back[...]


def finish(up, down, out, columns, back, route):
    groups, piece, _ = back.shape

    def rows(shape):
        return pl.BlockSpec((shape[0] // groups, shape[1]), lambda i, r: (i, 0))

    square = jax.ShapeDtypeStruct((D, D), F32)
    return pl.pallas_call(
        finish_kernel,
        grid_spec=pltpu.PrefetchScalarGridSpec(
            num_scalar_prefetch=1,
            grid=(groups,),
            in_specs=[
                rows(up.shape),
                rows(down.shape),
                rows(out.shape),
                pl.BlockSpec((2, 3, D // groups, C), lambda i, r: (0, 0, i, 0)),
                pl.BlockSpec((1, piece, D), lambda i, r: (r[i] // (2 * groups), 0, 0)),
            ],
            out_specs=[rows(up.shape), rows(down.shape)]
            + [rows(square.shape)] * 4
            + [pl.BlockSpec((1, piece, D), lambda i, r: (i, 0, 0))],
        ),
        out_shape=[jax.ShapeDtypeStruct(up.shape, F32), jax.ShapeDtypeStruct(down.shape, F32)]
        + [square] * 4
        + [jax.ShapeDtypeStruct(back.shape, BF16)],
        name="finish",
    )(route, up, down, out, columns, back)


def far_first(n):
    return sorted(range(1, n), key=lambda k: abs(k - n // 2))


def dispatch_kernel(n, x_ref, slot_ref, o_ref, slots_ref, send, recv, ssend, srecv, fsend, frecv):
    dp, me = lax.axis_index("dp"), lax.axis_index("seq")
    partner = (dp, 1 - me)
    barrier = pltpu.get_barrier_semaphore()
    for k in range(1, n):
        pl.semaphore_signal(barrier, inc=1, device_id=((dp + k) % n, me), device_id_type=MESH)
    pl.semaphore_signal(barrier, inc=1, device_id=partner, device_id_type=MESH)
    pl.semaphore_wait(barrier, n)

    order = far_first(n)
    copies, small = {}, {}
    for k in order:
        p = (dp + k) % n
        copies[k] = push(x_ref.at[p], o_ref.at[me, dp], send.at[k], recv.at[k], (p, me))
        copies[k].start()
        small[k] = push(slot_ref.at[p], slots_ref.at[me, dp], ssend.at[k], srecv.at[k], (p, me))
        small[k].start()
    forwards = [push(x_ref.at[dp], o_ref.at[me, dp], fsend.at[0], frecv.at[0], partner)]
    forwards[0].start()
    o_ref[me, dp] = x_ref[dp]
    slots_ref[me, dp] = slot_ref[dp]
    for k in order:
        s = (dp + n - k) % n
        copies[k].wait_recv()
        forward = push(o_ref.at[me, s], o_ref.at[me, s], fsend.at[k], frecv.at[k], partner)
        forward.start()
        forwards.append(forward)
    for k in order:
        small[k].wait_recv()
    last = push(slots_ref.at[me], slots_ref.at[me], fsend.at[n], frecv.at[n], partner)
    last.start()
    forwards.append(last)
    for k in order:
        copies[k].wait_send()
        small[k].wait_send()
    for forward in forwards:
        forward.wait()


def dispatch(outgoing, slots, collective_id):
    n = outgoing.shape[0]
    vmem = pl.BlockSpec(memory_space=VMEM)
    return pl.pallas_call(
        functools.partial(dispatch_kernel, n),
        out_shape=[
            jax.ShapeDtypeStruct((2,) + outgoing.shape, BF16),
            jax.ShapeDtypeStruct((2,) + slots.shape, jnp.int32),
        ],
        in_specs=[vmem] * 2,
        out_specs=[vmem] * 2,
        scratch_shapes=[pltpu.SemaphoreType.DMA((n,))] * 4 + [pltpu.SemaphoreType.DMA((n + 1,))] * 2,
        compiler_params=pltpu.CompilerParams(collective_id=collective_id, has_side_effects=True),
        name="dispatch",
    )(outgoing, slots)


def push(src, dst, send, recv, device):
    return pltpu.make_async_remote_copy(
        src_ref=src, dst_ref=dst, send_sem=send, recv_sem=recv,
        device_id=device, device_id_type=MESH,
    )


def meet(peers):
    barrier = pltpu.get_barrier_semaphore()
    for peer in peers:
        pl.semaphore_signal(barrier, inc=1, device_id=peer, device_id_type=MESH)
    pl.semaphore_wait(barrier, len(peers))


def chip_links(send, recv):
    dp, me = lax.axis_index("dp"), lax.axis_index("seq")
    axes = []
    for w in (1 + me, 2 - me):
        bit = (dp // w) % 2
        axes.append(((dp + (1 - 2 * bit) * w, me), bit))
    return {
        "dp": dp,
        "me": me,
        "z": dp // 4,
        "partner": (dp, 1 - me),
        "axes": axes,
        "stack": [((dp + 4 * k) % 16, me) for k in range(1, 4)],
        "send": send,
        "recv": recv,
    }


def square_blocks(sources, targets):
    for source, target in zip(sources, targets):
        tall, wide = source.shape
        for r in range(tall // D):
            for c in range(wide // D):
                at = (pl.ds(r * D, D), pl.ds(c * D, D))
                yield source.at[at], target.at[at]


class Chunk:
    def __init__(self, env, number, source, full, acc, landing, shared):
        self.env, self.number, self.shared = env, number, shared
        self.source, self.full, self.acc, self.landing = source, full, acc, landing
        base, size, offset = 0, source.shape[0], 0
        self.levels = []
        for device, bit in ([(env["partner"], env["me"])] if shared else []) + env["axes"]:
            half = size // 2
            keep, give = base + bit * half, base + (1 - bit) * half
            self.levels.append((device, keep, give, half, offset))
            base, size, offset = keep, half, offset + half
        self.base, self.size, self.offset = base, size // 4, offset

    def copy(self, stage, src, dst, device):
        e = self.env
        return push(src, dst, e["send"].at[self.number, stage], e["recv"].at[self.number, stage], device)

    def at(self, ref, start, size):
        return ref.at[pl.ds(start if isinstance(start, int) else pl.multiple_of(start, 16), size), :]

    def halves(self, level):
        device, _, give, half, offset = self.levels[level]
        src = self.acc if level else self.source
        return [self.copy(level, self.at(src, give, half), self.at(self.landing, offset, half), device)]

    def add(self, level):
        _, keep, _, half, offset = self.levels[level]
        src = self.acc if level else self.source
        step = min(half, 64)

        def run(i, _):
            here = pl.ds(pl.multiple_of(keep + i * step, 16), step)
            there = pl.ds(pl.multiple_of(offset + i * step, 16), step)
            total = src[here, :].astype(F32) + self.landing[there, :].astype(F32)
            self.acc[here, :] = total.astype(BF16)
            return 0

        lax.fori_loop(0, half // step, run, 0)

    def quarters(self):
        copies = []
        for k in range(1, 4):
            z = (self.env["z"] + k) % 4
            copies.append(
                self.copy(
                    len(self.levels) + k - 1,
                    self.at(self.acc, self.base + z * self.size, self.size),
                    self.at(self.landing, self.offset + (k - 1) * self.size, self.size),
                    self.env["stack"][k - 1],
                )
            )
        return copies

    def total(self):
        here = pl.ds(pl.multiple_of(self.base + self.env["z"] * self.size, 16), self.size)
        total = self.acc[here, :].astype(F32)
        for k in range(3):
            there = slice(self.offset + k * self.size, self.offset + (k + 1) * self.size)
            total += self.landing[there, :].astype(F32)
        self.full[here, :] = total.astype(BF16)

    def gathers(self):
        region = self.at(self.full, self.base + self.env["z"] * self.size, self.size)
        first = len(self.levels) + 3
        return [self.copy(first + k, region, region, self.env["stack"][k]) for k in range(3)]

    def spread(self, level):
        device, keep, _, half, _ = self.levels[level]
        region = self.at(self.full, keep, half)
        return [self.copy(len(self.levels) + 6 + level, region, region, device)]

    def hand_over(self):
        return [self.copy(2 * len(self.levels) + 6, self.full, self.full, self.env["partner"])]

    def steps(self):
        count = len(self.levels)
        stages = [functools.partial(self.halves, n) for n in range(count)] + [self.quarters, self.gathers]
        stages += [functools.partial(self.spread, n) for n in range(count - 1, -1, -1)]
        between = [functools.partial(self.add, n) for n in range(count)] + [self.total]
        if not self.shared:
            stages.append(self.hand_over)

        def step(n):
            if n > 0:
                for copy in stages[n - 1]():
                    copy.wait()
                if n - 1 < len(between):
                    between[n - 1]()
            if n < len(stages):
                for copy in stages[n]():
                    copy.start()

        return [functools.partial(step, n) for n in range(len(stages) + 1)]


def body(
    tokens,
    route,
    lengths,
    query_weight,
    query_bias,
    key_weight,
    value_weight,
    value_bias,
    output_weight,
    output_bias,
    first_gain,
    first_shift,
    up_weight,
    up_bias,
    down_weight,
    down_bias,
    second_gain,
    second_shift,
    cotangent,
):
    groups = lax.axis_size("dp")
    rows = tokens.shape[0]
    piece = rows // groups
    span = rows * lax.axis_size("seq")
    seq = lax.axis_index("seq")
    tables = lengths[0]
    me = seq.reshape(1).astype(jnp.int32)
    kernels = groups == 16 and piece % 16 == 0
    if kernels:
        pieces = 2 * groups
        outgoing, slots_out = arrange(tokens.reshape(groups, piece, D), route)
        x_all, slots_all = dispatch(outgoing, slots_out, 0)
        x_all = x_all.reshape(span, D)
        slots = slots_all[:, :, 0, 0].reshape(pieces)
    else:
        pieces = 0
        target = route // groups // lax.axis_size("seq")
        place = route % groups
        outgoing = jnp.zeros((groups, piece, D), BF16).at[target].set(tokens.reshape(groups, piece, D))
        slots_out = jnp.zeros((groups,), jnp.int32).at[target].set(place)
        incoming, slots = (
            lax.all_to_all(outgoing, "dp", split_axis=0, concat_axis=0, tiled=True),
            lax.all_to_all(slots_out, "dp", split_axis=0, concat_axis=0, tiled=True),
        )
        inputs = jnp.zeros_like(incoming).at[slots].set(incoming).reshape(rows, D)
        x_all = swap(inputs, (span, D), 0)
    x_turned, q, k, v, mixed_all, attend_out, lse, inputs = attend_forward(
        x_all, pieces, tables, me, slots,
        query_weight, key_weight, value_weight, query_bias, value_bias,
    )
    mixed = swap(mixed_all, (rows, D), 1)
    layer_out, grad_residual, grad_mixed, grad_up, grad_down, grad_output, vec = feed(
        mixed, inputs, cotangent, output_weight, up_weight, down_weight, up_bias,
        output_bias, first_gain, first_shift, down_bias, second_gain, second_shift,
    )
    shared = (tables, slots, pieces, x_turned, q, k, v)
    rest = (attend_out, lse, query_weight, key_weight, value_weight, grad_residual)
    if kernels:
        raw = [grad_up, grad_down, grad_output]
        up_sum, down_sum, out_sum, back, columns, vec = attend_backward(
            *shared, grad_mixed, *rest, raw, vec, 3
        )
        up_sum, down_sum, out_sum, query_sum, key_sum, value_sum, token_grad = finish(
            up_sum, down_sum, out_sum, columns, back.reshape(groups, piece, D), route
        )
        token_grad = token_grad.reshape(rows, D)
    else:
        grad_mixed_all = swap(grad_mixed, (span, C), 2)
        grad_columns, parts, grad_own, grad_other = attend_backward(
            *shared, grad_mixed_all, *rest, [], vec, 3
        )
        parts = parts.reshape(2, C)
        vec = vec + lax.dynamic_update_slice(jnp.zeros_like(vec), parts, (0, seq * C))
        both = swap(grad_other, (span, D), 5).reshape(2, rows, D)
        grad_inputs = grad_own + both[1 - seq].astype(F32)
        back_rows = grad_inputs.astype(BF16).reshape(groups, piece, D)[slots]
        returned = lax.all_to_all(back_rows, "dp", split_axis=0, concat_axis=0, tiled=True)
        token_grad = returned[target].reshape(rows, D)
        up_sum, down_sum, out_sum, vec = lax.psum(
            tuple(a.astype(F32) for a in (grad_up, grad_down, grad_output, vec)), ("dp", "seq")
        )
        columns = lax.psum(grad_columns.astype(F32), "dp")
        columns = lax.all_gather(columns, "seq", axis=2, tiled=True)
        query_sum, key_sum, value_sum = columns[0], columns[1], columns[2]
    return (
        layer_out,
        token_grad,
        query_sum,
        vec[0],
        key_sum,
        value_sum,
        vec[1],
        out_sum,
        vec[2],
        vec[3],
        vec[4],
        up_sum,
        vec[8:12].reshape(-1),
        down_sum,
        vec[5],
        vec[6],
        vec[7],
    )


def solution(mesh):
    both, one = P(("dp", "seq"), None), P()
    return jax.shard_map(
        body,
        mesh=mesh,
        in_specs=(both, P(("dp", "seq")), P("dp", None)) + (one,) * 15 + (both,),
        out_specs=(both, both) + (one,) * 15,
        check_vma=False,
    )
```
